32 devices in a mesh: task: 4 (over y, x), batch: 8 (over z, core).
Axes of the slice: x: 2, y: 2, z: 4, core: 2. Of those that a mesh axis runs over, the one named last changes fastest.
Arguments:
- hidden_in: bfloat16 [128, 512, 768], P(('task', 'batch')), may hold values from -6 to 6
- out_grad: bfloat16 [128, 512, 768], P(('task', 'batch')), may hold values from -6 to 6
- segment_ids: int32 [128, 512], P(('task', 'batch')), may hold values from 0 to 3, never falling along the last dimension, each value on 1 to 256 neighbouring positions
- pad_mask: int32 [128, 512], P(('task', 'batch')), may hold values 0 or 1
- task_weight: float32 [4], P('task'), may hold values from 0.002 to 0.008
- w_qkv: bfloat16 [768, 2304], P(('task', 'batch')), may hold values from -0.3125 to 0.3125
- b_query: bfloat16 [768], P(('task', 'batch')), may hold values from -3 to 3
- b_value: bfloat16 [768], P(('task', 'batch')), may hold values from -3 to 3
- w_out: bfloat16 [768, 768], P(('task', 'batch')), may hold values from -0.625 to 0.625
- b_out: bfloat16 [768], P(('task', 'batch')), may hold values from -3 to 3
- gain_one: bfloat16 [768], P(('task', 'batch')), may hold values from 0.5 to 1.5
- shift_one: bfloat16 [768], P(('task', 'batch')), may hold values from -2 to 2
- w_in: bfloat16 [768, 3072], P(('task', 'batch')), may hold values from -0.21875 to 0.21875
- b_in: bfloat16 [3072], P(('task', 'batch')), may hold values from -3 to 3
- w_down: bfloat16 [3072, 768], P(('task', 'batch')), may hold values from -0.15625 to 0.15625
- b_down: bfloat16 [768], P(('task', 'batch')), may hold values from -3 to 3
- gain_two: bfloat16 [768], P(('task', 'batch')), may hold values from 0.5 to 1.5
- shift_two: bfloat16 [768], P(('task', 'batch')), may hold values from -2 to 2
Outputs:
- hidden_out: bfloat16 [128, 512, 768], P(('task', 'batch'))
- input_grad: float32 [128, 512, 768], P(('task', 'batch'))
- grad_w_qkv: float32 [768, 2304], P(('task', 'batch'))
- grad_b_query: float32 [768], P(('task', 'batch'))
- grad_b_value: float32 [768], P(('task', 'batch'))
- grad_w_out: float32 [768, 768], P(('task', 'batch'))
- grad_b_out: float32 [768], P(('task', 'batch'))
- grad_gain_one: float32 [768], P(('task', 'batch'))
- grad_shift_one: float32 [768], P(('task', 'batch'))
- grad_w_in: float32 [768, 3072], P(('task', 'batch'))
- grad_b_in: float32 [3072], P(('task', 'batch'))
- grad_w_down: float32 [3072, 768], P(('task', 'batch'))
- grad_b_down: float32 [768], P(('task', 'batch'))
- grad_gain_two: float32 [768], P(('task', 'batch'))
- grad_shift_two: float32 [768], P(('task', 'batch'))
The draws below stay inside these ranges and needn't reach their ends.
All inputs are finite; a program needn't handle non-finite values. No bound on the sum of `pad_mask` on one device may be relied on, other than what follows from the above.
Results may differ from the reference program's by a relative error of at most 0.014.
The reference program's roundings to bfloat16 on the way count: a program that leaves them out, or rounds other values in their place, can miss the bound.
Values may be sent and summed in bfloat16 or wider, within the bound.
A program may use at most 256 MiB of HBM per device.

```python
import math
import jax
import jax.numpy as jnp
import numpy as np
from jax import lax

HEADS = 12
HEAD = 64
D = 768
FF = 3072
LEN = 512
SEQ_DEV = 4
SEQS = 128
N_TASK = 4
N_BATCH = 8


def plant(result, key, smallest, high):
    longest = result.shape.index(max(result.shape))
    spots = []
    for shift in (0, 1):
        where = [jax.random.randint(jax.random.fold_in(key, axis), (), 0, length) for axis, length in enumerate(result.shape)]
        where[longest] = (where[longest] + shift) % result.shape[longest]
        spots.append(tuple(where))
    return result.at[spots[0]].set(smallest).at[spots[1]].set(high)


def levels(stream_key, shape, shards, smallest, top_value):
    loudness, own = 1.0, jax.random.fold_in(stream_key, 6)
    for position, blocks in shards:
        steps = jnp.exp(jax.random.uniform(jax.random.fold_in(own, position), (blocks,), jnp.float32, smallest / len(shards), top_value / len(shards)))
        loudness = loudness * jnp.repeat(steps, shape[position] // blocks).reshape([-1 if axis == position else 1 for axis in range(len(shape))])
    return loudness


def profile(amount, total, limit, skew):
    portions = [(1 << 20) // math.isqrt(rank ** skew) + 1 for rank in range(2, amount + 1)]
    rest, given = total - limit - (amount - 1), [1] * (amount - 1)
    while rest > 0:
        candidates = [i for i in range(amount - 1) if given[i] < limit]
        whole, budget = sum([portions[i] for i in candidates]), rest
        for i in candidates:
            addition = min(limit - given[i], max(1, budget * portions[i] // whole), rest)
            given[i] = given[i] + addition
            rest = rest - addition
    return np.array([limit] + given)


def ragged_sizes(key, number_of, total, bound, lean):
    if number_of == 2:
        one = jax.random.randint(key, (), max(1, total - bound), min(bound, total - 1) + 1)
        return jnp.stack([one, total - one])
    tallies = jnp.asarray(profile(number_of, total, bound, lean), jnp.int32)
    couples = (number_of - 1) // 2
    source_of, receiver = tallies[1:1 + 2 * couples:2], tallies[2:2 + 2 * couples:2]
    slack = jnp.minimum(source_of - 1, bound - receiver)
    shifted = jax.random.randint(jax.random.fold_in(key, 1), (couples,), 0, 1 << 20) % (slack + 1)
    tallies = tallies.at[1:1 + 2 * couples:2].set(source_of - shifted).at[2:2 + 2 * couples:2].set(receiver + shifted)
    return tallies[jax.random.permutation(jax.random.fold_in(key, 2), number_of)]


def centred(own_key, shape, scale, limit, pieces=(), held_as=jnp.bfloat16):
    array = jax.random.normal(own_key, shape, jnp.float32) * scale
    if len(pieces) > 0:
        array = levels(own_key, shape, pieces, -0.22, 0.18) * array
    return jnp.clip(array, min=-limit, max=limit).astype(held_as)


def setup_inputs(seed: int = 0) -> dict:
    seeds = jax.random.split(jax.random.key(seed), 19)
    return {
        "hidden_in": centred(seeds[0], (SEQS, LEN, D), 1.0, 6.0, ((0, 32),)),
        "out_grad": centred(seeds[1], (SEQS, LEN, D), 1.0, 6.0, ((0, 32),)),
        "segment_ids": jax.vmap(lambda own: jnp.searchsorted(jnp.cumsum(ragged_sizes(own, 4, LEN, LEN // 2, 0)), jnp.arange(LEN), side="right"))(jax.random.split(seeds[2], SEQS)).reshape((SEQS, LEN)).astype(jnp.int32),
        "pad_mask": plant((jax.random.randint(seeds[3], (SEQS, LEN), 0, 8) < 7).astype(jnp.int32), jax.random.fold_in(seeds[3], 1), 0, 1),
        "task_weight": jnp.clip(jnp.exp(math.log(0.008) - 1.3862944 * jax.random.uniform(seeds[4], (N_TASK,), jnp.float32) ** levels(seeds[4], (N_TASK,), ((0, 4),), -0.2, 0.2)), 0.002, 0.008),
        "w_qkv": centred(seeds[5], (D, 3 * D), (D // 2) ** -0.5, 0.3125, ((0, 32),)),
        "b_query": centred(seeds[6], (D,), 0.5, 3.0, ((0, 32),)),
        "b_value": centred(seeds[7], (D,), 0.5, 3.0, ((0, 32),)),
        "w_out": centred(seeds[8], (D, D), (D // 8) ** -0.5, 0.625, ((0, 32),)),
        "b_out": centred(seeds[9], (D,), 0.5, 3.0, ((0, 32),)),
        "gain_one": jnp.clip(1.0 + 0.1 * jax.random.normal(seeds[10], (D,), jnp.float32), 0.5, 1.5).astype(jnp.bfloat16),
        "shift_one": centred(seeds[11], (D,), 0.3, 2.0, ((0, 32),)),
        "w_in": centred(seeds[12], (D, FF), D ** -0.5, 0.21875, ((0, 32),)),
        "b_in": centred(seeds[13], (FF,), 0.5, 3.0, ((0, 32),)),
        "w_down": centred(seeds[14], (FF, D), (FF // 2) ** -0.5, 0.15625, ((0, 32),)),
        "b_down": centred(seeds[15], (D,), 0.5, 3.0, ((0, 32),)),
        "gain_two": jnp.clip(1.0 + 0.1 * jax.random.normal(seeds[16], (D,), jnp.float32), 0.5, 1.5).astype(jnp.bfloat16),
        "shift_two": centred(seeds[17], (D,), 0.3, 2.0, ((0, 32),)),
    }


@jax.custom_vjp
def low(v):
    return lax.optimization_barrier(v.astype(jnp.bfloat16)).astype(jnp.float32)

@jax.custom_vjp
def low_back(v):
    return v

def low_keep(v):
    return (low(v), None)

def low_pass(kept, grad):
    return (grad,)

def back_keep(v):
    return (v, None)

def back_low(kept, grad):
    return (low(grad),)
low.defvjp(low_keep, low_pass)
low_back.defvjp(back_keep, back_low)

def normalize(arr_in, gain_in, shift_in):
    centre = arr_in - lax.optimization_barrier(jnp.mean(arr_in, -1, keepdims=True))
    spread = lax.optimization_barrier(jnp.mean(centre * centre, -1, keepdims=True))
    return centre * lax.rsqrt(spread + 1e-12) * gain_in + shift_in

def highest(left, right):
    return jnp.dot(left, right, precision=lax.Precision.HIGHEST)

def attend(inputs):
    queries, keys_in, values_in, segment_row, pad_row = inputs
    length = queries.shape[0]
    scores = jnp.einsum('qhd,khd->hqk', queries, keys_in, precision=lax.Precision.HIGHEST) * 0.125
    scores = low_back(scores)
    places = jnp.arange(length)
    allowed = (segment_row[:, None] == segment_row[None, :]) & ((pad_row[None, :] == 1) | (places[:, None] == places[None, :]))
    masked = jnp.where(allowed[None], scores, -1e+30)
    top_row = lax.optimization_barrier(jnp.max(masked, -1, keepdims=True))
    expo = jnp.exp(masked - top_row)
    probs_row = expo / lax.optimization_barrier(jnp.sum(expo, -1, keepdims=True))
    return jnp.einsum('hqk,khd->qhd', low(probs_row), values_in, precision=lax.Precision.HIGHEST)

def layer(block_in, params, segment_block, pad_block):
    w_qkv, b_query, b_value, w_out, b_out, gain_one, shift_one, w_in, b_in, w_down, b_down, gain_two, shift_two = params
    seqs_here = block_in.shape[0]
    rows = block_in.reshape(-1, D)
    qkv = highest(rows, w_qkv)
    queries = low_back(low(qkv[:, :D] + b_query)).reshape(seqs_here, LEN, HEADS, HEAD)
    keys_all = low_back(low(qkv[:, D:2 * D])).reshape(seqs_here, LEN, HEADS, HEAD)
    values_all = low_back(low(qkv[:, 2 * D:] + b_value)).reshape(seqs_here, LEN, HEADS, HEAD)
    attended = lax.map(jax.checkpoint(attend), (queries, keys_all, values_all, segment_block, pad_block))
    attended = low_back(low(attended.reshape(-1, D)))
    branch_one = low_back(highest(attended, w_out) + b_out)
    first = normalize(rows + branch_one, gain_one, shift_one)
    pre_act = low_back(highest(low(first), w_in) + b_in)
    act_low = low(jax.nn.gelu(pre_act, approximate=False))
    branch_two = low_back(highest(act_low, w_down) + b_down)
    return normalize(first + branch_two, gain_two, shift_two).reshape(block_in.shape)

def reference(hidden_in, out_grad, segment_ids, pad_mask, task_weight, w_qkv, b_query, b_value, w_out, b_out, gain_one, shift_one, w_in, b_in, w_down, b_down, gain_two, shift_two):
    params = tuple((p.astype(jnp.float32) for p in (w_qkv, b_query, b_value, w_out, b_out, gain_one, shift_one, w_in, b_in, w_down, b_down, gain_two, shift_two)))
    blocks = N_TASK * N_BATCH
    inputs_b = hidden_in.astype(jnp.float32).reshape(blocks, SEQ_DEV, LEN, D)
    cotan_b = out_grad.astype(jnp.float32).reshape(blocks, SEQ_DEV, LEN, D)
    segment_b = segment_ids.reshape(blocks, SEQ_DEV, LEN)
    pad_b = pad_mask.reshape(blocks, SEQ_DEV, LEN)
    weight_b = jnp.repeat(task_weight.astype(jnp.float32), N_BATCH)

    def advance(totals, item):
        block_in, block_cot, block_seg, block_pad, block_weight = item

        def forward(inner_x, inner_p):
            return layer(inner_x, inner_p, block_seg, block_pad)
        block_out, pullback = jax.vjp(forward, block_in, params)
        grad_x, grad_p = pullback(block_cot)
        totals = jax.tree.map(lambda summed, term: summed + block_weight * term, totals, grad_p)
        return (totals, (block_out.astype(jnp.bfloat16), grad_x))
    zeros = jax.tree.map(jnp.zeros_like, params)
    totals, (outs_b, grads_b) = lax.scan(advance, zeros, (inputs_b, cotan_b, segment_b, pad_b, weight_b))
    return (outs_b.reshape(SEQS, LEN, D), grads_b.reshape(SEQS, LEN, D), totals[0], totals[1], totals[2], totals[3], totals[4], totals[5], totals[6], totals[7], totals[8], totals[9], totals[10], totals[11], totals[12])
```

```python
from functools import partial

import jax
import jax.numpy as jnp
from jax import lax
from jax.experimental import pallas as pl
from jax.experimental.pallas import tpu as pltpu
from jax.sharding import PartitionSpec as P

HEADS = 12
AXES = ("task", "batch")
F32 = jnp.float32
BF16 = jnp.bfloat16
VMEM_BYTES = 66_000_000
BQ, BV, BO, G1, S1, BD, G2, S2, BIN = range(9)
VECTORS = 12


def dot(left, right):
    return lax.dot_general(left, right, (((1,), (0,)), ((), ())), preferred_element_type=F32)


def dot_right(left, right):
    return lax.dot_general(left, right, (((1,), (1,)), ((), ())), preferred_element_type=F32)


def fill_mask(seg_ref, pad_ref, mask_ref):
    length = mask_ref.shape[0]
    seg_row = seg_ref[0].astype(F32)
    pad_row = pad_ref[0].astype(F32)
    seg_col = jnp.transpose(jnp.broadcast_to(seg_row, (128, length)))
    pad_col = jnp.transpose(jnp.broadcast_to(pad_row, (128, length)))
    key_at = lax.broadcasted_iota(jnp.int32, (length, 128), 0)
    lane = lax.broadcasted_iota(jnp.int32, (length, 128), 1)
    for block in range(length // 128):
        same = seg_col == seg_row[:, 128 * block : 128 * block + 128]
        seen = (pad_col == 1.0) | (key_at == lane + 128 * block)
        mask_ref[:, 128 * block : 128 * block + 128] = jnp.where(same & seen, 0.0, -1e30)


def forward_kernel(x_ref, w_ref, vec_ref, seg_ref, pad_ref, qkv_ref, att_ref, lse_ref, mask_ref):
    width = x_ref.shape[1]
    fill_mask(seg_ref, pad_ref, mask_ref)
    for part, row in enumerate((BQ, None, BV)):
        cols = slice(part * width, (part + 1) * width)
        product = dot(x_ref[...], w_ref[:, cols])
        if row is not None:
            product = product + vec_ref[row : row + 1, :]
        qkv_ref[:, cols] = product.astype(BF16)
    half = width // HEADS
    first_half = lax.broadcasted_iota(jnp.int32, (1, 2 * half), 1) < half

    def pair(index, carry):
        base = pl.multiple_of(index * 2 * half, 2 * half)
        queries = qkv_ref[:, pl.ds(base, 2 * half)]
        keys = qkv_ref[:, pl.ds(width + base, 2 * half)]
        values_t = jnp.transpose(qkv_ref[:, pl.ds(2 * width + base, 2 * half)])
        keys = keys * jnp.asarray(0.125, BF16)
        outs = []
        for head in range(2):
            mine = first_half if head == 0 else ~first_half
            scores = dot_right(jnp.where(mine, keys, jnp.zeros_like(keys)), queries)
            scores = scores + mask_ref[...]
            top = jnp.max(scores, 0, keepdims=True)
            expo = jnp.exp(scores - top)
            total = jnp.sum(expo, 0, keepdims=True)
            probs = (expo * (1.0 / total)).astype(BF16)
            outs.append(dot(values_t[head * half : (head + 1) * half], probs))
            lse_ref[0, pl.ds(2 * index + head, 1), :] = top + jnp.log(total)
        att_ref[:, pl.ds(base, 2 * half)] = jnp.transpose(jnp.concatenate(outs, 0)).astype(BF16)
        return carry

    lax.fori_loop(0, HEADS // 2, pair, 0)


def attention_forward(rows, w_qkv, vectors, segments, pads):
    seqs, _, length = segments.shape
    width = rows.shape[1]
    whole = lambda shape: pl.BlockSpec(shape, lambda i: (0,) * len(shape), pipeline_mode=pl.Buffered(1))
    row = lambda cols: pl.BlockSpec((length, cols), lambda i: (i, 0))
    tokens = pl.BlockSpec((1, 1, length), lambda i: (i, 0, 0))
    return pl.pallas_call(
        forward_kernel,
        name="attention_forward",
        grid=(seqs,),
        in_specs=[row(width), whole(w_qkv.shape), whole(vectors.shape), tokens, tokens],
        out_specs=[row(3 * width), row(width), pl.BlockSpec((1, 16, length), lambda i: (i, 0, 0))],
        out_shape=[
            jax.ShapeDtypeStruct((rows.shape[0], 3 * width), BF16),
            jax.ShapeDtypeStruct((rows.shape[0], width), BF16),
            jax.ShapeDtypeStruct((seqs, 16, length), F32),
        ],
        scratch_shapes=[pltpu.VMEM((length, length), F32)],
        compiler_params=pltpu.CompilerParams(vmem_limit_bytes=VMEM_BYTES),
        cost_estimate=pl.CostEstimate(flops=12_000_000_000, bytes_accessed=20_000_000, transcendentals=12_000_000),
    )(rows, w_qkv, vectors, segments, pads)


def norm_parts(arr):
    centre = arr - jnp.mean(arr, -1, keepdims=True)
    scale = lax.rsqrt(jnp.mean(centre * centre, -1, keepdims=True) + 1e-12)
    return centre * scale, scale


def norm_back(grad_normal, normal, scale):
    return scale * (
        grad_normal
        - jnp.mean(grad_normal, -1, keepdims=True)
        - normal * jnp.mean(grad_normal * normal, -1, keepdims=True)
    )


def column_sum(arr):
    return jnp.sum(arr.astype(F32), 0, keepdims=True)


def middle_kernel(
    scale_ref, x_ref, att_ref, cot_ref, wo_ref, win_ref, wd_ref, vec_ref, bin_ref,
    out_ref, sum_ref, datt_ref, gwo_ref, gwin_ref, gwd_ref, gvec_ref, gbin_ref,
    acc_wo, acc_win, acc_wd, act_ref, slope_ref,
):
    step = pl.program_id(0)
    width = x_ref.shape[1]
    hidden = win_ref.shape[1]
    chunks = hidden // width

    @pl.when(step == 0)
    def _():
        acc_wo[...] = jnp.zeros_like(acc_wo)
        acc_win[...] = jnp.zeros_like(acc_win)
        acc_wd[...] = jnp.zeros_like(acc_wd)
        gvec_ref[...] = jnp.zeros_like(gvec_ref)
        gbin_ref[...] = jnp.zeros_like(gbin_ref)

    vec = lambda row: vec_ref[row : row + 1, :]
    branch = dot(att_ref[...], wo_ref[...]) + vec(BO)
    normal_one, scale_one = norm_parts(x_ref[...].astype(F32) + branch)
    first = normal_one * vec(G1) + vec(S1)
    first_low = first.astype(BF16)
    second = first + vec(BD)
    for chunk in range(chunks):
        cols = slice(chunk * width, (chunk + 1) * width)
        pre = dot(first_low, win_ref[:, cols]) + bin_ref[:, cols]
        below = 0.5 + 0.5 * lax.erf(pre * 0.7071067811865476)
        act = (pre * below).astype(BF16)
        act_ref[:, cols] = act
        slope_ref[:, cols] = below + pre * (jnp.exp(pre * pre * -0.5) * 0.3989422804014327)
        second = second + dot(act, wd_ref[cols, :])
    normal_two, scale_two = norm_parts(second)
    out_ref[...] = (normal_two * vec(G2) + vec(S2)).astype(BF16)
    cot = cot_ref[...].astype(F32)
    gvec_ref[G2 : G2 + 1, :] += column_sum(cot * normal_two)
    gvec_ref[S2 : S2 + 1, :] += column_sum(cot)
    grad_second = norm_back(cot * vec(G2), normal_two, scale_two)
    grad_low = grad_second.astype(BF16)
    gvec_ref[BD : BD + 1, :] += column_sum(grad_low)
    first_t = jnp.transpose(first_low)
    grad_first = grad_second
    for chunk in range(chunks):
        cols = slice(chunk * width, (chunk + 1) * width)
        grad_pre = (slope_ref[:, cols] * dot_right(grad_low, wd_ref[cols, :])).astype(BF16)
        gbin_ref[:, cols] += column_sum(grad_pre)
        acc_wd[cols, :] += dot(jnp.transpose(act_ref[:, cols]), grad_low)
        acc_win[:, cols] += dot(first_t, grad_pre)
        grad_first = grad_first + dot_right(grad_pre, win_ref[:, cols])
    gvec_ref[G1 : G1 + 1, :] += column_sum(grad_first * normal_one)
    gvec_ref[S1 : S1 + 1, :] += column_sum(grad_first)
    grad_sum = norm_back(grad_first * vec(G1), normal_one, scale_one)
    sum_ref[...] = grad_sum
    grad_one = grad_sum.astype(BF16)
    gvec_ref[BO : BO + 1, :] += column_sum(grad_one)
    acc_wo[...] += dot(jnp.transpose(att_ref[...]), grad_one)
    datt_ref[...] = dot_right(grad_one, wo_ref[...]).astype(BF16)

    @pl.when(step == pl.num_programs(0) - 1)
    def _():
        weight = scale_ref[0]
        gwo_ref[...] = (acc_wo[...] * weight).astype(BF16)
        gwin_ref[...] = (acc_win[...] * weight).astype(BF16)
        gwd_ref[...] = (acc_wd[...] * weight).astype(BF16)
        gvec_ref[...] = gvec_ref[...] * weight
        gbin_ref[...] = gbin_ref[...] * weight


def middle(scale, rows, att, cot, w_out, w_in, w_down, vectors, b_in):
    count, width = rows.shape
    hidden = w_in.shape[1]
    tile = 256
    whole = lambda shape: pl.BlockSpec(shape, lambda i: (0,) * len(shape), pipeline_mode=pl.Buffered(1))
    row = pl.BlockSpec((tile, width), lambda i: (i, 0))
    shape = jax.ShapeDtypeStruct
    return pl.pallas_call(
        middle_kernel,
        name="middle",
        grid=(count // tile,),
        in_specs=[pl.BlockSpec(memory_space=pltpu.SMEM), row, row, row]
        + [whole(a.shape) for a in (w_out, w_in, w_down, vectors, b_in)],
        out_specs=[row, row, row]
        + [whole(s) for s in (w_out.shape, w_in.shape, w_down.shape, (16, width), (1, hidden))],
        out_shape=[
            shape((count, width), BF16),
            shape((count, width), F32),
            shape((count, width), BF16),
            shape(w_out.shape, BF16),
            shape(w_in.shape, BF16),
            shape(w_down.shape, BF16),
            shape((16, width), F32),
            shape((1, hidden), F32),
        ],
        scratch_shapes=[
            pltpu.VMEM(w_out.shape, F32),
            pltpu.VMEM(w_in.shape, F32),
            pltpu.VMEM(w_down.shape, F32),
            pltpu.VMEM((tile, hidden), BF16),
            pltpu.VMEM((tile, hidden), F32),
        ],
        compiler_params=pltpu.CompilerParams(vmem_limit_bytes=VMEM_BYTES),
        cost_estimate=pl.CostEstimate(flops=65_000_000_000, bytes_accessed=60_000_000, transcendentals=12_000_000),
    )(scale, rows, att, cot, w_out, w_in, w_down, vectors, b_in)


def backward_kernel(
    scale_ref, x_ref, qkv_ref, datt_ref, lse_ref, seg_ref, pad_ref, sum_ref, w_ref,
    gx_ref, gw_ref, gvec_ref, acc_ref, dqkv_ref, mask_ref,
):
    step = pl.program_id(0)
    width = x_ref.shape[1]
    half = width // HEADS
    fill_mask(seg_ref, pad_ref, mask_ref)
    first_half = lax.broadcasted_iota(jnp.int32, (1, 2 * half), 1) < half

    @pl.when(step == 0)
    def _():
        acc_ref[...] = jnp.zeros_like(acc_ref)
        gvec_ref[...] = jnp.zeros_like(gvec_ref)

    def pair(index, carry):
        base = pl.multiple_of(index * 2 * half, 2 * half)
        queries = qkv_ref[:, pl.ds(base, 2 * half)]
        keys = qkv_ref[:, pl.ds(width + base, 2 * half)]
        values = qkv_ref[:, pl.ds(2 * width + base, 2 * half)]
        grads = datt_ref[:, pl.ds(base, 2 * half)]
        keys_t = jnp.transpose(keys)
        keys = keys * jnp.asarray(0.125, BF16)
        grad_k = jnp.zeros(keys.shape, F32)
        grad_v = jnp.zeros(keys.shape, F32)
        grad_q = []
        for head in range(2):
            mine = first_half if head == 0 else ~first_half
            only = lambda arr: jnp.where(mine, arr, jnp.zeros_like(arr))
            scores = dot_right(only(keys), queries) + mask_ref[...]
            probs = jnp.exp(scores - lse_ref[0, pl.ds(2 * index + head, 1), :])
            grad_probs = dot_right(only(values), grads)
            inner = jnp.sum(probs * grad_probs, 0, keepdims=True)
            grad_scores = (probs * (grad_probs - inner)).astype(BF16)
            grad_v = grad_v + dot(probs.astype(BF16), only(grads))
            grad_k = grad_k + dot(grad_scores, only(queries))
            grad_q.append(dot(keys_t[head * half : (head + 1) * half], grad_scores))
        grad_q = jnp.transpose(jnp.concatenate(grad_q, 0))
        dqkv_ref[:, pl.ds(base, 2 * half)] = (grad_q * 0.125).astype(BF16)
        dqkv_ref[:, pl.ds(width + base, 2 * half)] = (grad_k * 0.125).astype(BF16)
        dqkv_ref[:, pl.ds(2 * width + base, 2 * half)] = grad_v.astype(BF16)
        return carry

    lax.fori_loop(0, HEADS // 2, pair, 0)
    x_t = jnp.transpose(x_ref[...])
    grad_x = sum_ref[...]
    for part in range(3):
        cols = slice(part * width, (part + 1) * width)
        grad = dqkv_ref[:, cols]
        acc_ref[:, cols] += dot(x_t, grad)
        grad_x = grad_x + dot_right(grad, w_ref[:, cols])
        if part != 1:
            row = BQ if part == 0 else BV
            gvec_ref[row : row + 1, :] += column_sum(grad)
    gx_ref[...] = grad_x

    @pl.when(step == pl.num_programs(0) - 1)
    def _():
        gw_ref[...] = (acc_ref[...] * scale_ref[0]).astype(BF16)
        gvec_ref[...] = gvec_ref[...] * scale_ref[0]


def attention_backward(scale, rows, qkv, datt, lse, segments, pads, grad_sum, w_qkv):
    seqs, _, length = segments.shape
    count, width = rows.shape
    whole = lambda shape: pl.BlockSpec(shape, lambda i: (0,) * len(shape), pipeline_mode=pl.Buffered(1))
    row = lambda cols: pl.BlockSpec((length, cols), lambda i: (i, 0))
    tokens = pl.BlockSpec((1, 1, length), lambda i: (i, 0, 0))
    shape = jax.ShapeDtypeStruct
    return pl.pallas_call(
        backward_kernel,
        name="attention_backward",
        grid=(seqs,),
        in_specs=[
            pl.BlockSpec(memory_space=pltpu.SMEM),
            row(width),
            row(3 * width),
            row(width),
            pl.BlockSpec((1, 16, length), lambda i: (i, 0, 0)),
            tokens,
            tokens,
            row(width),
            whole(w_qkv.shape),
        ],
        out_specs=[row(width), whole(w_qkv.shape), whole((8, width))],
        out_shape=[shape((count, width), F32), shape(w_qkv.shape, BF16), shape((8, width), F32)],
        scratch_shapes=[
            pltpu.VMEM(w_qkv.shape, F32),
            pltpu.VMEM((length, 3 * width), BF16),
            pltpu.VMEM((length, length), F32),
        ],
        compiler_params=pltpu.CompilerParams(vmem_limit_bytes=VMEM_BYTES),
        cost_estimate=pl.CostEstimate(flops=31_000_000_000, bytes_accessed=35_000_000, transcendentals=12_000_000),
    )(scale, rows, qkv, datt, lse, segments, pads, grad_sum, w_qkv)


def body(
    hidden_in, out_grad, segment_ids, pad_mask, task_weight, w_qkv, b_query, b_value, w_out, b_out,
    gain_one, shift_one, w_in, b_in, w_down, b_down, gain_two, shift_two,
):
    seqs, length, width = hidden_in.shape
    mine = w_qkv.shape[0]
    gather = partial(lax.all_gather, axis_name=AXES, axis=0, tiled=True)
    scatter = partial(lax.psum_scatter, axis_name=AXES, scatter_dimension=0, tiled=True)
    packed = jnp.stack([b_query, b_value, b_out, gain_one, shift_one, b_down, gain_two, shift_two], 1)
    packed = jnp.concatenate([packed, b_in.reshape(mine, -1)], 1)
    packed = jnp.pad(packed, ((0, 0), (0, 128 - packed.shape[1])))
    early = gather(jnp.concatenate([w_qkv, packed], 1))
    qkv_full = early[:, : 3 * width]
    vectors = jnp.transpose(early[:, 3 * width : 3 * width + 8].astype(F32))
    bin_full = early[:, 3 * width + BIN : 3 * width + VECTORS].astype(F32).reshape(1, -1)
    wo_full, win_full, wd_full = gather(w_out), gather(w_in), gather(w_down)
    rows = hidden_in.reshape(-1, width)
    segments = segment_ids.reshape(seqs, 1, length)
    pads = pad_mask.reshape(seqs, 1, length)
    qkv, att, lse = attention_forward(rows, qkv_full, vectors, segments, pads)
    hidden_out, grad_sum, datt, g_wo, g_win, g_wd, g_vec, g_bin = middle(
        task_weight, rows, att, out_grad.reshape(-1, width), wo_full, win_full, wd_full, vectors, bin_full
    )
    grad_x, g_qkv, g_vec_b = attention_backward(
        task_weight, rows, qkv, datt, lse, segments, pads, grad_sum, qkv_full
    )
    g_packed = jnp.concatenate([jnp.transpose(g_vec_b[:2]), jnp.transpose(g_vec[2:8]), g_bin.reshape(width, -1)], 1)
    g_packed = jnp.pad(g_packed, ((0, 0), (0, 128 - g_packed.shape[1]))).astype(BF16)
    late = scatter(jnp.concatenate([g_qkv, g_packed], 1)).astype(F32)
    vector = lambda row: late[:, 3 * width + row]
    return (
        hidden_out.reshape(hidden_in.shape),
        grad_x.reshape(hidden_in.shape),
        late[:, : 3 * width],
        vector(BQ),
        vector(BV),
        scatter(g_wo).astype(F32),
        vector(BO),
        vector(G1),
        vector(S1),
        scatter(g_win).astype(F32),
        late[:, 3 * width + BIN : 3 * width + VECTORS].reshape(-1),
        scatter(g_wd).astype(F32),
        vector(BD),
        vector(G2),
        vector(S2),
    )


def solution(mesh):
    seq, mat, vec = P(AXES, None, None), P(AXES, None), P(AXES)
    weights = (mat, vec, vec, mat, vec, vec, vec, mat, vec, mat, vec, vec, vec)
    return jax.shard_map(
        body,
        mesh=mesh,
        in_specs=(seq, seq, mat, mat, P("task")) + weights,
        out_specs=(seq, seq) + weights,
        check_vma=False,
    )
```

```python
from functools import partial

import jax
import jax.numpy as jnp
from jax import lax
from jax.experimental import pallas as pl
from jax.experimental.pallas import tpu as pltpu
from jax.sharding import PartitionSpec as P

HEADS = 12
AXES = ("task", "batch")
F32 = jnp.float32
BF16 = jnp.bfloat16
VMEM_BYTES = 66_000_000
BQ, BV, BO, G1, S1, BD, G2, S2, BIN = range(9)
VECTORS = 12


MESH = pl.DeviceIdType.MESH


class Place:
    def __init__(self):
        self.task = lax.axis_index("task")
        self.batch = lax.axis_index("batch")
        self.core = self.batch % 2
        self.z = self.batch // 2
        x, y = self.task % 2, self.task // 2
        flip_x, flip_y = self.task + 1 - 2 * x, self.task + 2 - 4 * y
        self.task_a = (1 - self.core) * flip_x + self.core * flip_y
        self.task_b = (1 - self.core) * flip_y + self.core * flip_x
        self.task_ab = 3 - self.task
        self.partner = (self.task, self.batch + 1 - 2 * self.core)
        self.peer_a = (self.task_a, self.batch)
        self.peer_b = (self.task_b, self.batch)
        self.above = (self.task, self.batch + 2)
        self.below = (self.task, self.batch - 2)

    def device(self, task, z):
        return task * 8 + z * 2

    def meet(self):
        barrier = pltpu.get_barrier_semaphore()
        for peer in (self.partner, self.peer_a, self.peer_b):
            pl.semaphore_signal(barrier, inc=1, device_id=peer, device_id_type=MESH)

        @pl.when(self.z < 3)
        def _():
            pl.semaphore_signal(barrier, inc=1, device_id=self.above, device_id_type=MESH)

        @pl.when(self.z > 0)
        def _():
            pl.semaphore_signal(barrier, inc=1, device_id=self.below, device_id_type=MESH)

        pl.semaphore_wait(barrier, 4 + self.z * (3 - self.z) // 2)


GATHER_SEMS = [
    pltpu.SemaphoreType.DMA((16,)),
    pltpu.SemaphoreType.DMA((16,)),
    pltpu.SemaphoreType.DMA((14,)),
    pltpu.SemaphoreType.DMA((4,)),
]


class Gather:
    def __init__(self, place, shard, full, sems):
        self.place, self.shard, self.full = place, shard, full
        self.send, self.recv, self.recv_b, self.misc = sems
        self.half = shard.shape[1] // 2

    def chunk(self, task, z):
        start = pl.multiple_of(self.place.core * self.half, 128)
        first = self.place.device(task, z)
        return self.full.at[pl.ds(first, 2), :, pl.ds(start, self.half)]

    def copy(self, ref, send, recv, peer):
        return pltpu.make_async_remote_copy(ref, ref, send, recv, device_id=peer, device_id_type=MESH)

    def own(self):
        place = self.place
        return self.full.at[place.task * 8 + place.batch]

    def begin(self):
        place = self.place
        pltpu.make_async_copy(self.shard, self.own(), self.misc.at[0]).start()
        pltpu.make_async_remote_copy(
            self.shard, self.own(), self.send.at[0], self.recv.at[0], device_id=place.partner, device_id_type=MESH
        ).start()

    def to_z(self, task, z, index, up, start):
        slot = 2 + index + (0 if up else 6)
        peer = self.place.above if up else self.place.below
        copy = self.copy(self.chunk(task, z), self.send.at[slot], self.recv.at[slot], peer)
        copy.start() if start else copy.wait_send()

    def to_b(self, task, z, index):
        self.copy(self.chunk(task, z), self.misc.at[1], self.recv_b.at[index], self.place.peer_b).start()

    def hand_over(self, task, z):
        self.copy(self.chunk(task, z), self.misc.at[2], self.misc.at[3], self.place.partner).start()

    def spread(self):
        place = self.place
        pltpu.make_async_copy(self.shard, self.own(), self.misc.at[0]).wait()
        other = self.full.at[place.task * 8 + place.partner[1]]
        self.copy(other, self.send.at[0], self.recv.at[0], place.partner).wait_recv()
        self.copy(self.chunk(place.task, place.z), self.send.at[1], self.recv.at[1], place.peer_a).start()
        self.both_ways(place.task, place.z, 0)
        self.to_b(place.task, place.z, 0)

    def both_ways(self, task, z, index, start=True):
        @pl.when(self.place.z < 3)
        def _():
            self.to_z(task, z, index, True, start)

        @pl.when(self.place.z > 0)
        def _():
            self.to_z(task, z, index, False, start)

    def from_a(self):
        place = self.place
        self.copy(self.chunk(place.task_a, place.z), self.send.at[1], self.recv.at[1], place.peer_a).wait_recv()
        self.both_ways(place.task_a, place.z, 1)
        self.to_b(place.task_a, place.z, 1)
        self.hand_over(place.task_a, place.z)

    def along_z(self, far, which):
        place = self.place
        task = place.task if which == 0 else place.task_a
        index = 2 * (far - 1) + which
        for up in (True, False):
            z = place.z - far if up else place.z + far
            here = (place.z >= far) if up else (place.z + far <= 3)
            more = (place.z < 3) if up else (place.z > 0)
            slot = 2 + index + (0 if up else 6)

            @pl.when(here)
            def _():
                self.copy(self.chunk(task, z), self.send.at[slot], self.recv.at[slot], place.partner).wait_recv()
                if far < 3:

                    @pl.when(more)
                    def _():
                        self.to_z(task, z, index + 2, up, True)

                self.to_b(task, z, 2 + index + (0 if up else 6))
                self.hand_over(task, z)

    def from_b(self, index):
        place = self.place
        if index < 2:
            task = place.task_b if index == 0 else place.task_ab
            self.arrived_b(task, place.z, index)
            return
        up, far, which = index < 8, (index - 2) % 6 // 2 + 1, index % 2
        task = place.task_b if which == 0 else place.task_ab
        z = place.z - far if up else place.z + far

        @pl.when((place.z >= far) if up else (place.z + far <= 3))
        def _():
            self.arrived_b(task, z, index)

    def arrived_b(self, task, z, index):
        self.copy(self.chunk(task, z), self.misc.at[1], self.recv_b.at[index], self.place.peer_b).wait_recv()
        self.hand_over(task, z)

    def finish(self):
        place = self.place
        start = pl.multiple_of(place.core * self.half, 128)
        other = pl.multiple_of((1 - place.core) * self.half, 128)
        rest = self.full.at[pl.ds(0, 30), :, pl.ds(other, self.half)]
        self.copy(rest, self.misc.at[2], self.misc.at[3], place.partner).wait_recv()
        mine = self.full.at[pl.ds(0, 30), :, pl.ds(start, self.half)]
        self.copy(mine, self.misc.at[2], self.misc.at[3], place.partner).wait_send()
        eight = self.full.at[pl.ds(0, 16), :, pl.ds(start, self.half)]
        self.copy(eight, self.misc.at[1], self.recv_b.at[0], place.peer_b).wait_send()
        self.copy(self.shard, self.send.at[0], self.recv.at[0], place.partner).wait_send()
        self.copy(self.chunk(place.task, place.z), self.send.at[1], self.recv.at[1], place.peer_a).wait_send()
        self.both_ways(place.task, place.z, 0, False)
        self.both_ways(place.task_a, place.z, 1, False)
        for far in (1, 2):
            for which in (0, 1):
                task = place.task if which == 0 else place.task_a
                index = 2 * (far - 1) + which

                @pl.when((place.z >= far) & (place.z < 3))
                def _():
                    self.to_z(task, place.z - far, index + 2, True, False)

                @pl.when((place.z + far <= 3) & (place.z > 0))
                def _():
                    self.to_z(task, place.z + far, index + 2, False, False)

    def events(self):
        out = [self.begin, self.spread, self.from_a]
        out += [partial(self.along_z, 1, 0), partial(self.along_z, 1, 1), partial(self.from_b, 0), partial(self.from_b, 1)]
        out += [partial(self.along_z, 2, 0), partial(self.along_z, 2, 1)]
        out += [partial(self.from_b, i) for i in (2, 8, 3, 9)]
        out += [partial(self.along_z, 3, 0), partial(self.along_z, 3, 1)]
        out += [partial(self.from_b, i) for i in (4, 10, 5, 11, 6, 12, 7, 13)]
        return out + [self.finish]


def gather_kernel(count, *refs):
    shards, fulls, sems = refs[:count], refs[count : 2 * count], refs[2 * count :]
    place = Place()
    place.meet()
    jobs = [Gather(place, shards[i], fulls[i], sems[4 * i : 4 * i + 4]).events() for i in range(count)]
    for step in range(len(jobs[0]) + count - 1):
        for i in range(count):
            if 0 <= step - i < len(jobs[i]):
                jobs[i][step - i]()


def gather_all(shards, identity):
    count = len(shards)
    place = pl.BlockSpec(memory_space=pl.ANY)
    return pl.pallas_call(
        partial(gather_kernel, count),
        name="gather",
        in_specs=[place] * count,
        out_specs=[place] * count,
        out_shape=[jax.ShapeDtypeStruct((32, *s.shape), s.dtype) for s in shards],
        scratch_shapes=GATHER_SEMS * count,
        compiler_params=pltpu.CompilerParams(collective_id=identity, has_side_effects=True),
    )(*shards)


SCATTER_SEMS = [
    pltpu.SemaphoreType.DMA((4,)),
    pltpu.SemaphoreType.DMA((4,)),
    pltpu.SemaphoreType.DMA((4,)),
    pltpu.SemaphoreType.DMA((8,)),
    pltpu.SemaphoreType.DMA((8,)),
    pltpu.SemaphoreType.DMA((8,)),
    pltpu.SemaphoreType.DMA((10,)),
    pltpu.SemaphoreType.DMA((4,)),
]


def scatter_buffers(rows, cols):
    half = cols // 2
    return [
        pltpu.VMEM((16, rows, half), BF16),
        pltpu.VMEM((16, rows, half), BF16),
        pltpu.VMEM((8, rows, half), BF16),
        pltpu.VMEM((10, rows, half), BF16),
        pltpu.VMEM((rows, half), BF16),
        pltpu.VMEM((rows, half), F32),
        pltpu.VMEM((rows // 2, half), F32),
    ] + SCATTER_SEMS


class Scatter:
    def __init__(self, place, terms, out, buffers):
        self.place, self.terms, self.out = place, terms, out
        (self.own, self.other, self.got_b, self.got_z, self.got_a, self.total, self.got_f) = buffers[:7]
        (self.s_load, self.s_pair, self.r_pair, self.s_b, self.r_b, self.s_z, self.r_z, self.misc) = buffers[7:]
        self.half = self.own.shape[2]
        place_ = place
        self.tasks = (place_.task_ab, place_.task_b, place_.task_a, place_.task)
        self.tasks_partner = (place_.task_ab, place_.task_a, place_.task_b, place_.task)
        self.low = 1 - place_.z // 2
        self.inner = self.low * place_.z + (1 - self.low) * (3 - place_.z)
        self.far = (place_.task, place_.batch + 4 * self.low - 2)
        self.near = (place_.task, place_.batch + 2 - 4 * self.low)

    def cols(self, core):
        return pl.ds(pl.multiple_of(core * self.half, 128), self.half)

    def remote(self, src, dst, send, recv, peer):
        return pltpu.make_async_remote_copy(src, dst, send, recv, device_id=peer, device_id_type=MESH)

    def load(self, index):
        first = self.tasks[index] * 4
        return pltpu.make_async_copy(
            self.terms.at[pl.ds(first, 4), :, self.cols(self.place.core)],
            self.own.at[pl.ds(first, 4)],
            self.s_load.at[index],
        )

    def pair(self, index, sent=True):
        first = (self.tasks_partner if sent else self.tasks)[index] * 4
        return self.remote(
            self.terms.at[pl.ds(first, 4), :, self.cols(1 - self.place.core)],
            self.other.at[pl.ds(first, 4)],
            self.s_pair.at[index],
            self.r_pair.at[index],
            self.place.partner,
        )

    def begin(self):
        for index in range(4):
            self.load(index).start()
            self.pair(index).start()

    def add(self, at, ref, where):
        self.own[at] = (self.own[at].astype(F32) + ref[where].astype(F32)).astype(BF16)

    def along_b(self, which, z):
        at = self.tasks[which] * 4 + z
        slot = which * 4 + z
        return self.remote(
            self.own.at[at], self.got_b.at[slot], self.s_b.at[slot], self.r_b.at[slot], self.place.peer_b
        )

    def add_pair(self, index):
        self.load(index).wait()
        self.pair(index, False).wait_recv()
        first = self.tasks[index] * 4
        for m in (3, 2, 1, 0):
            z = self.level(m)
            self.add(first + z, self.other, first + z)
            if index < 2:
                self.along_b(index, z).start()

    def add_b(self, which, z):
        self.along_b(which, z).wait_recv()
        self.add(self.tasks[2 + which] * 4 + z, self.got_b, which * 4 + z)

    def level(self, m):
        return self.low * m + (1 - self.low) * (3 - m)

    def along_z(self, which, m, far):
        at = self.tasks[2 + which] * 4 + self.level(m)
        into = 5 * which + ((1 - self.inner) * (m - 1) + self.inner * (6 - m) if far else 3 + m)
        peer = self.far if far else self.near
        return self.remote(
            self.own.at[at], self.got_z.at[into], self.s_z.at[which * 4 + m], self.r_z.at[into], peer
        )

    def add_z(self, which, m, slot):
        into = 5 * which + slot
        self.remote(
            self.got_z.at[into], self.got_z.at[into], self.s_z.at[0], self.r_z.at[into], self.place.partner
        ).wait_recv()
        self.add(self.tasks[2 + which] * 4 + self.level(m), self.got_z, into)

    def step_far(self, which, m):
        @pl.when(self.inner == 1)
        def _():
            self.add_z(which, m, m - 1)

        @pl.when(self.inner < m)
        def _():
            self.along_z(which, m, True).start()

    def step_near(self, which, m):
        @pl.when(self.inner >= m)
        def _():
            self.add_z(which, m, 3 + m)

        @pl.when(self.inner > m)
        def _():
            self.along_z(which, m, False).start()

    def along_a(self):
        at = self.tasks[2] * 4 + self.place.z
        return self.remote(self.own.at[at], self.got_a, self.misc.at[0], self.misc.at[1], self.place.peer_a)

    def to_a(self):
        self.along_a().start()

    def last(self):
        rows = self.got_f.shape[0]
        away = pl.multiple_of((1 - self.place.core) * rows, rows)
        return self.remote(
            self.total.at[pl.ds(away, rows)], self.got_f, self.misc.at[2], self.misc.at[3], self.place.partner
        )

    def add_a(self):
        self.along_a().wait_recv()
        self.total[...] = self.own[self.tasks[3] * 4 + self.place.z].astype(F32) + self.got_a[...].astype(F32)
        self.last().start()

    def finish(self):
        rows = self.got_f.shape[0]
        core = self.place.core
        self.last().wait_recv()
        self.out[:, self.cols(core)] = self.total[pl.ds(pl.multiple_of(core * rows, rows), rows), :]
        self.out[:, self.cols(1 - core)] = self.got_f[...]
        for index in range(4):
            self.pair(index).wait_send()
        for which in range(2):
            for z in range(4):
                self.along_b(which, z).wait_send()

                @pl.when(self.inner < z)
                def _():
                    self.along_z(which, z, True).wait_send()

                @pl.when(self.inner > z)
                def _():
                    self.along_z(which, z, False).wait_send()

        self.along_a().wait_send()
        self.last().wait_send()

    def add_b_far(self, which, m):
        self.add_b(which, self.level(m))

    def events(self):
        out = [self.begin] + [partial(self.add_pair, i) for i in range(4)]
        for which in range(2):
            for m in (3, 2, 1):
                out += [partial(self.add_b_far, which, m), partial(self.step_far, which, m)]
            out.append(partial(self.add_b_far, which, 0))
        for which in range(2):
            out += [partial(self.step_near, which, m) for m in range(2)]
            if which == 0:
                out.append(self.to_a)
        return out + [self.add_a, self.finish]


def scatter_kernel(count, *refs):
    terms, outs, scratch = refs[:count], refs[count : 2 * count], refs[2 * count :]
    place = Place()
    place.meet()
    size = len(scratch) // count
    jobs = [Scatter(place, terms[i], outs[i], scratch[size * i : size * i + size]).events() for i in range(count)]
    lag = 6
    for step in range(len(jobs[0]) + lag * (count - 1)):
        for i in range(count):
            if 0 <= step - lag * i < len(jobs[i]):
                jobs[i][step - lag * i]()


def scatter_all(terms, identity):
    count = len(terms)
    scratch = []
    for t in terms:
        scratch += scatter_buffers(*t.shape[1:])
    return pl.pallas_call(
        partial(scatter_kernel, count),
        name="scatter",
        in_specs=[pl.BlockSpec(memory_space=pl.ANY)] * count,
        out_specs=[pl.BlockSpec(memory_space=pltpu.VMEM)] * count,
        out_shape=[jax.ShapeDtypeStruct((t.shape[1] // 2, t.shape[2]), F32) for t in terms],
        scratch_shapes=scratch,
        compiler_params=pltpu.CompilerParams(
            collective_id=identity, has_side_effects=True, vmem_limit_bytes=66_000_000
        ),
    )(*terms)


def dot(left, right):
    return lax.dot_general(left, right, (((1,), (0,)), ((), ())), preferred_element_type=F32)


def dot_right(left, right):
    return lax.dot_general(left, right, (((1,), (1,)), ((), ())), preferred_element_type=F32)


def fill_mask(seg_ref, pad_ref, mask_ref):
    length = mask_ref.shape[0]
    seg_row = seg_ref[0].astype(F32)
    pad_row = pad_ref[0].astype(F32)
    seg_col = jnp.transpose(jnp.broadcast_to(seg_row, (128, length)))
    pad_col = jnp.transpose(jnp.broadcast_to(pad_row, (128, length)))
    key_at = lax.broadcasted_iota(jnp.int32, (length, 128), 0)
    lane = lax.broadcasted_iota(jnp.int32, (length, 128), 1)
    for block in range(length // 128):
        same = seg_col == seg_row[:, 128 * block : 128 * block + 128]
        seen = (pad_col == 1.0) | (key_at == lane + 128 * block)
        mask_ref[:, 128 * block : 128 * block + 128] = jnp.where(same & seen, 0.0, -1e30)


def forward_kernel(x_ref, w_ref, vec_ref, seg_ref, pad_ref, qkv_ref, att_ref, lse_ref, mask_ref):
    width = x_ref.shape[1]
    fill_mask(seg_ref, pad_ref, mask_ref)
    for part, row in enumerate((BQ, None, BV)):
        cols = slice(part * width, (part + 1) * width)
        product = dot(x_ref[...], w_ref[:, cols])
        if row is not None:
            product = product + vec_ref[row : row + 1, :]
        qkv_ref[:, cols] = product.astype(BF16)
    half = width // HEADS
    first_half = lax.broadcasted_iota(jnp.int32, (1, 2 * half), 1) < half

    def pair(index, carry):
        base = pl.multiple_of(index * 2 * half, 2 * half)
        queries = qkv_ref[:, pl.ds(base, 2 * half)]
        keys = qkv_ref[:, pl.ds(width + base, 2 * half)]
        values_t = jnp.transpose(qkv_ref[:, pl.ds(2 * width + base, 2 * half)])
        keys = keys * jnp.asarray(0.125, BF16)
        outs = []
        for head in range(2):
            mine = first_half if head == 0 else ~first_half
            scores = dot_right(jnp.where(mine, keys, jnp.zeros_like(keys)), queries)
            scores = scores + mask_ref[...]
            top = jnp.max(scores, 0, keepdims=True)
            expo = jnp.exp(scores - top)
            total = jnp.sum(expo, 0, keepdims=True)
            probs = (expo * (1.0 / total)).astype(BF16)
            outs.append(dot(values_t[head * half : (head + 1) * half], probs))
            lse_ref[0, pl.ds(2 * index + head, 1), :] = top + jnp.log(total)
        att_ref[:, pl.ds(base, 2 * half)] = jnp.transpose(jnp.concatenate(outs, 0)).astype(BF16)
        return carry

    lax.fori_loop(0, HEADS // 2, pair, 0)


def attention_forward(rows, w_qkv, vectors, segments, pads):
    seqs, _, length = segments.shape
    width = rows.shape[1]
    whole = lambda shape: pl.BlockSpec(shape, lambda i: (0,) * len(shape), pipeline_mode=pl.Buffered(1))
    row = lambda cols: pl.BlockSpec((length, cols), lambda i: (i, 0))
    tokens = pl.BlockSpec((1, 1, length), lambda i: (i, 0, 0))
    return pl.pallas_call(
        forward_kernel,
        name="attention_forward",
        grid=(seqs,),
        in_specs=[row(width), whole((width, 3 * width)), whole(vectors.shape), tokens, tokens],
        out_specs=[row(3 * width), row(width), pl.BlockSpec((1, 16, length), lambda i: (i, 0, 0))],
        out_shape=[
            jax.ShapeDtypeStruct((rows.shape[0], 3 * width), BF16),
            jax.ShapeDtypeStruct((rows.shape[0], width), BF16),
            jax.ShapeDtypeStruct((seqs, 16, length), F32),
        ],
        scratch_shapes=[pltpu.VMEM((length, length), F32)],
        compiler_params=pltpu.CompilerParams(vmem_limit_bytes=VMEM_BYTES),
        cost_estimate=pl.CostEstimate(flops=12_000_000_000, bytes_accessed=20_000_000, transcendentals=12_000_000),
    )(rows, w_qkv, vectors, segments, pads)


def norm_parts(arr):
    centre = arr - jnp.mean(arr, -1, keepdims=True)
    scale = lax.rsqrt(jnp.mean(centre * centre, -1, keepdims=True) + 1e-12)
    return centre * scale, scale


def norm_back(grad_normal, normal, scale):
    return scale * (
        grad_normal
        - jnp.mean(grad_normal, -1, keepdims=True)
        - normal * jnp.mean(grad_normal * normal, -1, keepdims=True)
    )


def column_sum(arr):
    return jnp.sum(arr.astype(F32), 0, keepdims=True)


def middle_kernel(
    scale_ref, x_ref, att_ref, cot_ref, wo_ref, win_ref, wd_ref, vec_ref, bin_ref,
    out_ref, sum_ref, datt_ref, gwo_ref, gwin_ref, gwd_ref, gvec_ref, gbin_ref,
    acc_wo, acc_win, acc_wd, act_ref, slope_ref,
):
    step = pl.program_id(0)
    width = x_ref.shape[1]
    hidden = win_ref.shape[1]
    chunks = hidden // width

    @pl.when(step == 0)
    def _():
        acc_wo[...] = jnp.zeros_like(acc_wo)
        acc_win[...] = jnp.zeros_like(acc_win)
        acc_wd[...] = jnp.zeros_like(acc_wd)
        gvec_ref[...] = jnp.zeros_like(gvec_ref)
        gbin_ref[...] = jnp.zeros_like(gbin_ref)

    vec = lambda row: vec_ref[row : row + 1, :]
    branch = dot(att_ref[...], wo_ref[...]) + vec(BO)
    normal_one, scale_one = norm_parts(x_ref[...].astype(F32) + branch)
    first = normal_one * vec(G1) + vec(S1)
    first_low = first.astype(BF16)
    second = first + vec(BD)
    for chunk in range(chunks):
        cols = slice(chunk * width, (chunk + 1) * width)
        pre = dot(first_low, win_ref[:, cols]) + bin_ref[:, cols]
        below = 0.5 + 0.5 * lax.erf(pre * 0.7071067811865476)
        act = (pre * below).astype(BF16)
        act_ref[:, cols] = act
        slope_ref[:, cols] = below + pre * (jnp.exp(pre * pre * -0.5) * 0.3989422804014327)
        second = second + dot(act, wd_ref[cols, :])
    normal_two, scale_two = norm_parts(second)
    out_ref[...] = (normal_two * vec(G2) + vec(S2)).astype(BF16)
    cot = cot_ref[...].astype(F32)
    gvec_ref[G2 : G2 + 1, :] += column_sum(cot * normal_two)
    gvec_ref[S2 : S2 + 1, :] += column_sum(cot)
    grad_second = norm_back(cot * vec(G2), normal_two, scale_two)
    grad_low = grad_second.astype(BF16)
    gvec_ref[BD : BD + 1, :] += column_sum(grad_low)
    first_t = jnp.transpose(first_low)
    grad_first = grad_second
    for chunk in range(chunks):
        cols = slice(chunk * width, (chunk + 1) * width)
        grad_pre = (slope_ref[:, cols] * dot_right(grad_low, wd_ref[cols, :])).astype(BF16)
        gbin_ref[:, cols] += column_sum(grad_pre)
        acc_wd[cols, :] += dot(jnp.transpose(act_ref[:, cols]), grad_low)
        acc_win[:, cols] += dot(first_t, grad_pre)
        grad_first = grad_first + dot_right(grad_pre, win_ref[:, cols])
    gvec_ref[G1 : G1 + 1, :] += column_sum(grad_first * normal_one)
    gvec_ref[S1 : S1 + 1, :] += column_sum(grad_first)
    grad_sum = norm_back(grad_first * vec(G1), normal_one, scale_one)
    sum_ref[...] = grad_sum
    grad_one = grad_sum.astype(BF16)
    gvec_ref[BO : BO + 1, :] += column_sum(grad_one)
    acc_wo[...] += dot(jnp.transpose(att_ref[...]), grad_one)
    datt_ref[...] = dot_right(grad_one, wo_ref[...]).astype(BF16)

    @pl.when(step == pl.num_programs(0) - 1)
    def _():
        weight = scale_ref[0]
        gwo_ref[...] = (acc_wo[...] * weight).astype(BF16)
        gwin_ref[...] = (acc_win[...] * weight).astype(BF16)
        gwd_ref[...] = (acc_wd[...] * weight).astype(BF16)
        gvec_ref[...] = gvec_ref[...] * weight
        gbin_ref[...] = gbin_ref[...] * weight


def middle(scale, rows, att, cot, w_out, w_in, w_down, vectors, b_in):
    count, width = rows.shape
    hidden = w_in.shape[1]
    tile = 256
    whole = lambda shape: pl.BlockSpec(shape, lambda i: (0,) * len(shape), pipeline_mode=pl.Buffered(1))
    row = pl.BlockSpec((tile, width), lambda i: (i, 0))
    shape = jax.ShapeDtypeStruct
    return pl.pallas_call(
        middle_kernel,
        name="middle",
        grid=(count // tile,),
        in_specs=[pl.BlockSpec(memory_space=pltpu.SMEM), row, row, row]
        + [whole(a.shape) for a in (w_out, w_in, w_down, vectors, b_in)],
        out_specs=[row, row, row]
        + [whole(s) for s in (w_out.shape, w_in.shape, w_down.shape, (16, width), (1, hidden))],
        out_shape=[
            shape((count, width), BF16),
            shape((count, width), F32),
            shape((count, width), BF16),
            shape(w_out.shape, BF16),
            shape(w_in.shape, BF16),
            shape(w_down.shape, BF16),
            shape((16, width), F32),
            shape((1, hidden), F32),
        ],
        scratch_shapes=[
            pltpu.VMEM(w_out.shape, F32),
            pltpu.VMEM(w_in.shape, F32),
            pltpu.VMEM(w_down.shape, F32),
            pltpu.VMEM((tile, hidden), BF16),
            pltpu.VMEM((tile, hidden), F32),
        ],
        compiler_params=pltpu.CompilerParams(vmem_limit_bytes=VMEM_BYTES),
        cost_estimate=pl.CostEstimate(flops=65_000_000_000, bytes_accessed=60_000_000, transcendentals=12_000_000),
    )(scale, rows, att, cot, w_out, w_in, w_down, vectors, b_in)


def backward_kernel(
    scale_ref, x_ref, qkv_ref, datt_ref, lse_ref, seg_ref, pad_ref, sum_ref, w_ref, rest_ref,
    gx_ref, gw_ref, acc_ref, gvec_ref, dqkv_ref, mask_ref,
):
    step = pl.program_id(0)
    width = x_ref.shape[1]
    half = width // HEADS
    fill_mask(seg_ref, pad_ref, mask_ref)
    first_half = lax.broadcasted_iota(jnp.int32, (1, 2 * half), 1) < half

    @pl.when(step == 0)
    def _():
        acc_ref[...] = jnp.zeros_like(acc_ref)
        gvec_ref[...] = jnp.zeros_like(gvec_ref)

    def pair(index, carry):
        base = pl.multiple_of(index * 2 * half, 2 * half)
        queries = qkv_ref[:, pl.ds(base, 2 * half)]
        keys = qkv_ref[:, pl.ds(width + base, 2 * half)]
        values = qkv_ref[:, pl.ds(2 * width + base, 2 * half)]
        grads = datt_ref[:, pl.ds(base, 2 * half)]
        keys_t = jnp.transpose(keys)
        keys = keys * jnp.asarray(0.125, BF16)
        grad_k = jnp.zeros(keys.shape, F32)
        grad_v = jnp.zeros(keys.shape, F32)
        grad_q = []
        for head in range(2):
            mine = first_half if head == 0 else ~first_half
            only = lambda arr: jnp.where(mine, arr, jnp.zeros_like(arr))
            scores = dot_right(only(keys), queries) + mask_ref[...]
            probs = jnp.exp(scores - lse_ref[0, pl.ds(2 * index + head, 1), :])
            grad_probs = dot_right(only(values), grads)
            inner = jnp.sum(probs * grad_probs, 0, keepdims=True)
            grad_scores = (probs * (grad_probs - inner)).astype(BF16)
            grad_v = grad_v + dot(probs.astype(BF16), only(grads))
            grad_k = grad_k + dot(grad_scores, only(queries))
            grad_q.append(dot(keys_t[head * half : (head + 1) * half], grad_scores))
        grad_q = jnp.transpose(jnp.concatenate(grad_q, 0))
        dqkv_ref[:, pl.ds(base, 2 * half)] = (grad_q * 0.125).astype(BF16)
        dqkv_ref[:, pl.ds(width + base, 2 * half)] = (grad_k * 0.125).astype(BF16)
        dqkv_ref[:, pl.ds(2 * width + base, 2 * half)] = grad_v.astype(BF16)
        return carry

    lax.fori_loop(0, HEADS // 2, pair, 0)
    x_t = jnp.transpose(x_ref[...])
    grad_x = sum_ref[...]
    for part in range(3):
        cols = slice(part * width, (part + 1) * width)
        grad = dqkv_ref[:, cols]
        acc_ref[:, cols] += dot(x_t, grad)
        grad_x = grad_x + dot_right(grad, w_ref[:, cols])
        if part != 1:
            row = BQ if part == 0 else BV
            gvec_ref[row : row + 1, :] += column_sum(grad)
    gx_ref[...] = grad_x

    @pl.when(step == pl.num_programs(0) - 1)
    def _():
        gw_ref[:, : 3 * width] = (acc_ref[...] * scale_ref[0]).astype(BF16)
        gvec_ref[:2] = gvec_ref[:2] * scale_ref[0]
        gvec_ref[2:VECTORS] = rest_ref[2:VECTORS]
        gw_ref[:, 3 * width : 3 * width + 128] = jnp.transpose(gvec_ref[...]).astype(BF16)
        gw_ref[:, 3 * width + 128 :] = jnp.zeros((width, gw_ref.shape[1] - 3 * width - 128), BF16)


def attention_backward(scale, rows, qkv, datt, lse, segments, pads, grad_sum, w_qkv, rest):
    seqs, _, length = segments.shape
    count, width = rows.shape
    whole = lambda shape: pl.BlockSpec(shape, lambda i: (0,) * len(shape), pipeline_mode=pl.Buffered(1))
    row = lambda cols: pl.BlockSpec((length, cols), lambda i: (i, 0))
    tokens = pl.BlockSpec((1, 1, length), lambda i: (i, 0, 0))
    shape = jax.ShapeDtypeStruct
    return pl.pallas_call(
        backward_kernel,
        name="attention_backward",
        grid=(seqs,),
        in_specs=[
            pl.BlockSpec(memory_space=pltpu.SMEM),
            row(width),
            row(3 * width),
            row(width),
            pl.BlockSpec((1, 16, length), lambda i: (i, 0, 0)),
            tokens,
            tokens,
            row(width),
            whole((width, 3 * width)),
            whole(rest.shape),
        ],
        out_specs=[row(width), whole(w_qkv.shape)],
        out_shape=[shape((count, width), F32), shape(w_qkv.shape, BF16)],
        scratch_shapes=[
            pltpu.VMEM((width, 3 * width), F32),
            pltpu.VMEM((128, width), F32),
            pltpu.VMEM((length, 3 * width), BF16),
            pltpu.VMEM((length, length), F32),
        ],
        compiler_params=pltpu.CompilerParams(vmem_limit_bytes=VMEM_BYTES),
        cost_estimate=pl.CostEstimate(flops=31_000_000_000, bytes_accessed=35_000_000, transcendentals=12_000_000),
    )(scale, rows, qkv, datt, lse, segments, pads, grad_sum, w_qkv, rest)


def body(
    hidden_in, out_grad, segment_ids, pad_mask, task_weight, w_qkv, b_query, b_value, w_out, b_out,
    gain_one, shift_one, w_in, b_in, w_down, b_down, gain_two, shift_two,
):
    seqs, length, width = hidden_in.shape
    mine = w_qkv.shape[0]
    near = lax.axis_size("task") == 4 and lax.axis_size("batch") == 8 and mine % 8 == 0
    packed = jnp.stack([b_query, b_value, b_out, gain_one, shift_one, b_down, gain_two, shift_two], 1)
    packed = jnp.concatenate([packed, b_in.reshape(mine, -1)], 1)
    packed = jnp.pad(packed, ((0, 0), (0, 256 - packed.shape[1])))
    shards = [jnp.concatenate([w_qkv, packed], 1), w_out, w_in, w_down]
    if near:
        full = gather_all(shards[:1], 0) + gather_all(shards[1:], 1)
        full = [f.reshape(-1, f.shape[-1]) for f in full]
    else:
        full = [lax.all_gather(s, AXES, axis=0, tiled=True) for s in shards]
    early, wo_full, win_full, wd_full = full
    vectors = jnp.transpose(early[:, 3 * width : 3 * width + 8].astype(F32))
    bin_full = early[:, 3 * width + BIN : 3 * width + VECTORS].astype(F32).reshape(1, -1)
    rows = hidden_in.reshape(-1, width)
    segments = segment_ids.reshape(seqs, 1, length)
    pads = pad_mask.reshape(seqs, 1, length)
    qkv, att, lse = attention_forward(rows, early, vectors, segments, pads)
    hidden_out, grad_sum, datt, g_wo, g_win, g_wd, g_vec, g_bin = middle(
        task_weight, rows, att, out_grad.reshape(-1, width), wo_full, win_full, wd_full, vectors, bin_full
    )
    g_rest = jnp.concatenate([g_vec[:8], jnp.transpose(g_bin.reshape(width, -1)), g_vec[8:12]], 0)
    grad_x, g_qkv = attention_backward(
        task_weight, rows, qkv, datt, lse, segments, pads, grad_sum, early, g_rest
    )
    terms = [g_qkv, g_wd, g_win, g_wo]
    if near:
        late, s_wd, s_win, s_wo = scatter_all([t.reshape(16, -1, t.shape[1]) for t in terms[:1]], 2) + scatter_all(
            [t.reshape(16, -1, t.shape[1]) for t in terms[1:]], 3
        )
    else:
        late, s_wd, s_win, s_wo = [
            lax.psum_scatter(t, AXES, scatter_dimension=0, tiled=True).astype(F32) for t in terms
        ]
    vector = lambda row: late[:, 3 * width + row]
    return (
        hidden_out.reshape(hidden_in.shape),
        grad_x.reshape(hidden_in.shape),
        late[:, : 3 * width],
        vector(BQ),
        vector(BV),
        s_wo,
        vector(BO),
        vector(G1),
        vector(S1),
        s_win,
        late[:, 3 * width + BIN : 3 * width + VECTORS].reshape(-1),
        s_wd,
        vector(BD),
        vector(G2),
        vector(S2),
    )


def solution(mesh):
    seq, mat, vec = P(AXES, None, None), P(AXES, None), P(AXES)
    weights = (mat, vec, vec, mat, vec, vec, vec, mat, vec, mat, vec, vec, vec)
    return jax.shard_map(
        body,
        mesh=mesh,
        in_specs=(seq, seq, mat, mat, P("task")) + weights,
        out_specs=(seq, seq) + weights,
        check_vma=False,
    )
```

```python
from functools import partial

import jax
import jax.numpy as jnp
from jax import lax
from jax.experimental import pallas as pl
from jax.experimental.pallas import tpu as pltpu
from jax.sharding import PartitionSpec as P

HEADS = 12
AXES = ("task", "batch")
F32 = jnp.float32
BF16 = jnp.bfloat16
VMEM_BYTES = 66_000_000
BQ, BV, BO, G1, S1, BD, G2, S2, BIN = range(9)
VECTORS = 12


MESH = pl.DeviceIdType.MESH


class Place:
    def __init__(self):
        self.task = lax.axis_index("task")
        self.batch = lax.axis_index("batch")
        self.core = self.batch % 2
        self.z = self.batch // 2
        x, y = self.task % 2, self.task // 2
        flip_x, flip_y = self.task + 1 - 2 * x, self.task + 2 - 4 * y
        self.task_a = (1 - self.core) * flip_x + self.core * flip_y
        self.task_b = (1 - self.core) * flip_y + self.core * flip_x
        self.task_ab = 3 - self.task
        self.partner = (self.task, self.batch + 1 - 2 * self.core)
        self.peer_a = (self.task_a, self.batch)
        self.peer_b = (self.task_b, self.batch)
        self.above = (self.task, self.batch + 2)
        self.below = (self.task, self.batch - 2)

    def device(self, task, z):
        return task * 8 + z * 2

    def meet(self):
        barrier = pltpu.get_barrier_semaphore()
        for peer in (self.partner, self.peer_a, self.peer_b):
            pl.semaphore_signal(barrier, inc=1, device_id=peer, device_id_type=MESH)

        @pl.when(self.z < 3)
        def _():
            pl.semaphore_signal(barrier, inc=1, device_id=self.above, device_id_type=MESH)

        @pl.when(self.z > 0)
        def _():
            pl.semaphore_signal(barrier, inc=1, device_id=self.below, device_id_type=MESH)

        pl.semaphore_wait(barrier, 4 + self.z * (3 - self.z) // 2)


GATHER_SEMS = [
    pltpu.SemaphoreType.DMA((16,)),
    pltpu.SemaphoreType.DMA((16,)),
    pltpu.SemaphoreType.DMA((14,)),
    pltpu.SemaphoreType.DMA((4,)),
]


class Gather:
    def __init__(self, place, shard, full, sems):
        self.place, self.shard, self.full = place, shard, full
        self.send, self.recv, self.recv_b, self.misc = sems
        self.half = shard.shape[1] // 2

    def chunk(self, task, z):
        start = pl.multiple_of(self.place.core * self.half, 128)
        first = self.place.device(task, z)
        return self.full.at[pl.ds(first, 2), :, pl.ds(start, self.half)]

    def copy(self, ref, send, recv, peer):
        return pltpu.make_async_remote_copy(ref, ref, send, recv, device_id=peer, device_id_type=MESH)

    def own(self):
        place = self.place
        return self.full.at[place.task * 8 + place.batch]

    def begin(self):
        place = self.place
        pltpu.make_async_copy(self.shard, self.own(), self.misc.at[0]).start()
        pltpu.make_async_remote_copy(
            self.shard, self.own(), self.send.at[0], self.recv.at[0], device_id=place.partner, device_id_type=MESH
        ).start()

    def to_z(self, task, z, index, up, start):
        slot = 2 + index + (0 if up else 6)
        peer = self.place.above if up else self.place.below
        copy = self.copy(self.chunk(task, z), self.send.at[slot], self.recv.at[slot], peer)
        copy.start() if start else copy.wait_send()

    def to_b(self, task, z, index):
        self.copy(self.chunk(task, z), self.misc.at[1], self.recv_b.at[index], self.place.peer_b).start()

    def hand_over(self, task, z):
        self.copy(self.chunk(task, z), self.misc.at[2], self.misc.at[3], self.place.partner).start()

    def spread(self):
        place = self.place
        pltpu.make_async_copy(self.shard, self.own(), self.misc.at[0]).wait()
        other = self.full.at[place.task * 8 + place.partner[1]]
        self.copy(other, self.send.at[0], self.recv.at[0], place.partner).wait_recv()
        self.copy(self.chunk(place.task, place.z), self.send.at[1], self.recv.at[1], place.peer_a).start()
        self.both_ways(place.task, place.z, 0)
        self.to_b(place.task, place.z, 0)

    def both_ways(self, task, z, index, start=True):
        @pl.when(self.place.z < 3)
        def _():
            self.to_z(task, z, index, True, start)

        @pl.when(self.place.z > 0)
        def _():
            self.to_z(task, z, index, False, start)

    def from_a(self):
        place = self.place
        self.copy(self.chunk(place.task_a, place.z), self.send.at[1], self.recv.at[1], place.peer_a).wait_recv()
        self.both_ways(place.task_a, place.z, 1)
        self.to_b(place.task_a, place.z, 1)
        self.hand_over(place.task_a, place.z)

    def along_z(self, far, which):
        place = self.place
        task = place.task if which == 0 else place.task_a
        index = 2 * (far - 1) + which
        for up in (True, False):
            z = place.z - far if up else place.z + far
            here = (place.z >= far) if up else (place.z + far <= 3)
            more = (place.z < 3) if up else (place.z > 0)
            slot = 2 + index + (0 if up else 6)

            @pl.when(here)
            def _():
                self.copy(self.chunk(task, z), self.send.at[slot], self.recv.at[slot], place.partner).wait_recv()
                if far < 3:

                    @pl.when(more)
                    def _():
                        self.to_z(task, z, index + 2, up, True)

                self.to_b(task, z, 2 + index + (0 if up else 6))
                self.hand_over(task, z)

    def from_b(self, index):
        place = self.place
        if index < 2:
            task = place.task_b if index == 0 else place.task_ab
            self.arrived_b(task, place.z, index)
            return
        up, far, which = index < 8, (index - 2) % 6 // 2 + 1, index % 2
        task = place.task_b if which == 0 else place.task_ab
        z = place.z - far if up else place.z + far

        @pl.when((place.z >= far) if up else (place.z + far <= 3))
        def _():
            self.arrived_b(task, z, index)

    def arrived_b(self, task, z, index):
        self.copy(self.chunk(task, z), self.misc.at[1], self.recv_b.at[index], self.place.peer_b).wait_recv()
        self.hand_over(task, z)

    def finish(self):
        place = self.place
        start = pl.multiple_of(place.core * self.half, 128)
        other = pl.multiple_of((1 - place.core) * self.half, 128)
        rest = self.full.at[pl.ds(0, 30), :, pl.ds(other, self.half)]
        self.copy(rest, self.misc.at[2], self.misc.at[3], place.partner).wait_recv()
        mine = self.full.at[pl.ds(0, 30), :, pl.ds(start, self.half)]
        self.copy(mine, self.misc.at[2], self.misc.at[3], place.partner).wait_send()
        eight = self.full.at[pl.ds(0, 16), :, pl.ds(start, self.half)]
        self.copy(eight, self.misc.at[1], self.recv_b.at[0], place.peer_b).wait_send()
        self.copy(self.shard, self.send.at[0], self.recv.at[0], place.partner).wait_send()
        self.copy(self.chunk(place.task, place.z), self.send.at[1], self.recv.at[1], place.peer_a).wait_send()
        self.both_ways(place.task, place.z, 0, False)
        self.both_ways(place.task_a, place.z, 1, False)
        for far in (1, 2):
            for which in (0, 1):
                task = place.task if which == 0 else place.task_a
                index = 2 * (far - 1) + which

                @pl.when((place.z >= far) & (place.z < 3))
                def _():
                    self.to_z(task, place.z - far, index + 2, True, False)

                @pl.when((place.z + far <= 3) & (place.z > 0))
                def _():
                    self.to_z(task, place.z + far, index + 2, False, False)

    def timed(self):
        z, b = self.along_z, self.from_b
        return [
            (0, self.begin), (1, self.spread), (4, self.from_a), (5, partial(z, 1, 0)), (6, partial(b, 0)),
            (9, partial(z, 1, 1)), (9, partial(b, 1)), (10, partial(b, 2)), (10, partial(b, 8)),
            (13, partial(z, 2, 0)), (13, partial(b, 3)), (13, partial(b, 9)), (17, partial(z, 2, 1)),
            (17, partial(b, 4)), (17, partial(b, 10)), (20, partial(b, 5)), (20, partial(b, 11)),
            (21, partial(z, 3, 0)), (23, partial(b, 6)), (23, partial(b, 12)), (24, partial(z, 3, 1)),
            (24, partial(b, 7)), (24, partial(b, 13)), (24, self.finish),
        ]

    def events(self):
        out = [self.begin, self.spread, self.from_a]
        out += [partial(self.along_z, 1, 0), partial(self.along_z, 1, 1), partial(self.from_b, 0), partial(self.from_b, 1)]
        out += [partial(self.along_z, 2, 0), partial(self.along_z, 2, 1)]
        out += [partial(self.from_b, i) for i in (2, 8, 3, 9)]
        out += [partial(self.along_z, 3, 0), partial(self.along_z, 3, 1)]
        out += [partial(self.from_b, i) for i in (4, 10, 5, 11, 6, 12, 7, 13)]
        return out + [self.finish]


def gather_kernel(count, *refs):
    shards, fulls, sems = refs[:count], refs[count : 2 * count], refs[2 * count :]
    place = Place()
    place.meet()
    jobs = [Gather(place, shards[i], fulls[i], sems[4 * i : 4 * i + 4]).events() for i in range(count)]
    for step in range(len(jobs[0]) + count - 1):
        for i in range(count):
            if 0 <= step - i < len(jobs[i]):
                jobs[i][step - i]()


def gather_all(shards, identity):
    count = len(shards)
    place = pl.BlockSpec(memory_space=pl.ANY)
    return pl.pallas_call(
        partial(gather_kernel, count),
        name="gather",
        in_specs=[place] * count,
        out_specs=[place] * count,
        out_shape=[jax.ShapeDtypeStruct((32, *s.shape), s.dtype) for s in shards],
        scratch_shapes=GATHER_SEMS * count,
        compiler_params=pltpu.CompilerParams(collective_id=identity, has_side_effects=True),
    )(*shards)


SCATTER_SEMS = [
    pltpu.SemaphoreType.DMA((4,)),
    pltpu.SemaphoreType.DMA((4,)),
    pltpu.SemaphoreType.DMA((4,)),
    pltpu.SemaphoreType.DMA((8,)),
    pltpu.SemaphoreType.DMA((8,)),
    pltpu.SemaphoreType.DMA((8,)),
    pltpu.SemaphoreType.DMA((10,)),
    pltpu.SemaphoreType.DMA((4,)),
]


def scatter_buffers(rows, cols):
    half = cols // 2
    return [
        pltpu.VMEM((16, rows, half), BF16),
        pltpu.VMEM((16, rows, half), BF16),
        pltpu.VMEM((8, rows, half), BF16),
        pltpu.VMEM((10, rows, half), BF16),
        pltpu.VMEM((rows, half), BF16),
        pltpu.VMEM((rows, half), F32),
        pltpu.VMEM((rows // 2, half), F32),
    ] + SCATTER_SEMS


class Scatter:
    def __init__(self, place, terms, out, buffers):
        self.place, self.terms, self.out = place, terms, out
        (self.own, self.other, self.got_b, self.got_z, self.got_a, self.total, self.got_f) = buffers[:7]
        (self.s_load, self.s_pair, self.r_pair, self.s_b, self.r_b, self.s_z, self.r_z, self.misc) = buffers[7:]
        self.half = self.own.shape[2]
        place_ = place
        self.tasks = (place_.task_ab, place_.task_b, place_.task_a, place_.task)
        self.tasks_partner = (place_.task_ab, place_.task_a, place_.task_b, place_.task)
        self.low = 1 - place_.z // 2
        self.inner = self.low * place_.z + (1 - self.low) * (3 - place_.z)
        self.far = (place_.task, place_.batch + 4 * self.low - 2)
        self.near = (place_.task, place_.batch + 2 - 4 * self.low)

    def cols(self, core):
        return pl.ds(pl.multiple_of(core * self.half, 128), self.half)

    def remote(self, src, dst, send, recv, peer):
        return pltpu.make_async_remote_copy(src, dst, send, recv, device_id=peer, device_id_type=MESH)

    def load(self, index):
        first = self.tasks[index] * 4
        return pltpu.make_async_copy(
            self.terms.at[pl.ds(first, 4), :, self.cols(self.place.core)],
            self.own.at[pl.ds(first, 4)],
            self.s_load.at[index],
        )

    def pair(self, index, sent=True):
        first = (self.tasks_partner if sent else self.tasks)[index] * 4
        return self.remote(
            self.terms.at[pl.ds(first, 4), :, self.cols(1 - self.place.core)],
            self.other.at[pl.ds(first, 4)],
            self.s_pair.at[index],
            self.r_pair.at[index],
            self.place.partner,
        )

    def begin(self):
        for index in range(4):
            self.load(index).start()
            self.pair(index).start()

    def add(self, at, ref, where):
        self.own[at] = (self.own[at].astype(F32) + ref[where].astype(F32)).astype(BF16)

    def along_b(self, which, z):
        at = self.tasks[which] * 4 + z
        slot = which * 4 + z
        return self.remote(
            self.own.at[at], self.got_b.at[slot], self.s_b.at[slot], self.r_b.at[slot], self.place.peer_b
        )

    def add_pair(self, index):
        self.load(index).wait()
        self.pair(index, False).wait_recv()
        first = self.tasks[index] * 4
        for m in (3, 2, 1, 0):
            z = self.level(m)
            self.add(first + z, self.other, first + z)
            if index < 2:
                self.along_b(index, z).start()

    def add_b(self, which, z):
        self.along_b(which, z).wait_recv()
        self.add(self.tasks[2 + which] * 4 + z, self.got_b, which * 4 + z)

    def level(self, m):
        return self.low * m + (1 - self.low) * (3 - m)

    def along_z(self, which, m, far):
        at = self.tasks[2 + which] * 4 + self.level(m)
        into = 5 * which + ((1 - self.inner) * (m - 1) + self.inner * (6 - m) if far else 3 + m)
        peer = self.far if far else self.near
        return self.remote(
            self.own.at[at], self.got_z.at[into], self.s_z.at[which * 4 + m], self.r_z.at[into], peer
        )

    def add_z(self, which, m, slot):
        into = 5 * which + slot
        self.remote(
            self.got_z.at[into], self.got_z.at[into], self.s_z.at[0], self.r_z.at[into], self.place.partner
        ).wait_recv()
        self.add(self.tasks[2 + which] * 4 + self.level(m), self.got_z, into)

    def step_far(self, which, m):
        self.step_far_out(which, m)
        self.step_far_on(which, m)

    def step_far_out(self, which, m):
        @pl.when(self.inner == 0)
        def _():
            self.along_z(which, m, True).start()

    def step_far_on(self, which, m):
        @pl.when(self.inner == 1)
        def _():
            self.add_z(which, m, m - 1)
            if m > 1:
                self.along_z(which, m, True).start()

    def step_near(self, which, m):
        @pl.when(self.inner >= m)
        def _():
            self.add_z(which, m, 3 + m)

        @pl.when(self.inner > m)
        def _():
            self.along_z(which, m, False).start()

    def along_a(self):
        at = self.tasks[2] * 4 + self.place.z
        return self.remote(self.own.at[at], self.got_a, self.misc.at[0], self.misc.at[1], self.place.peer_a)

    def to_a(self):
        self.along_a().start()

    def last(self):
        rows = self.got_f.shape[0]
        away = pl.multiple_of((1 - self.place.core) * rows, rows)
        return self.remote(
            self.total.at[pl.ds(away, rows)], self.got_f, self.misc.at[2], self.misc.at[3], self.place.partner
        )

    def add_a(self):
        self.along_a().wait_recv()
        self.total[...] = self.own[self.tasks[3] * 4 + self.place.z].astype(F32) + self.got_a[...].astype(F32)
        self.last().start()

    def finish(self):
        rows = self.got_f.shape[0]
        core = self.place.core
        self.last().wait_recv()
        self.out[:, self.cols(core)] = self.total[pl.ds(pl.multiple_of(core * rows, rows), rows), :]
        self.out[:, self.cols(1 - core)] = self.got_f[...]
        for index in range(4):
            self.pair(index).wait_send()
        for which in range(2):
            for z in range(4):
                self.along_b(which, z).wait_send()

                @pl.when(self.inner < z)
                def _():
                    self.along_z(which, z, True).wait_send()

                @pl.when(self.inner > z)
                def _():
                    self.along_z(which, z, False).wait_send()

        self.along_a().wait_send()
        self.last().wait_send()

    def add_b_far(self, which, m):
        self.add_b(which, self.level(m))

    def timed(self):
        pair, b, send, relay, near = self.add_pair, self.add_b_far, self.step_far_out, self.step_far_on, self.step_near
        return [
            (0, self.begin), (2, partial(pair, 0)), (3, partial(pair, 1)), (4, partial(pair, 2)), (4, partial(pair, 3)),
            (5, partial(b, 0, 3)), (5, partial(send, 0, 3)), (6, partial(b, 0, 2)), (6, partial(send, 0, 2)),
            (8, partial(b, 0, 1)), (8, partial(send, 0, 1)), (8, partial(relay, 0, 3)), (9, partial(b, 0, 0)),
            (10, partial(b, 1, 3)), (10, partial(send, 1, 3)), (11, partial(relay, 0, 2)), (11, partial(b, 1, 2)),
            (11, partial(send, 1, 2)), (12, partial(near, 0, 0)), (13, partial(b, 1, 1)), (13, partial(send, 1, 1)),
            (14, partial(relay, 0, 1)), (14, partial(b, 1, 0)), (15, partial(near, 0, 1)), (16, partial(relay, 1, 3)),
            (16, self.to_a), (19, partial(relay, 1, 2)), (20, partial(near, 1, 0)), (22, partial(relay, 1, 1)),
            (23, partial(near, 1, 1)), (24, self.add_a), (24, self.finish),
        ]

    def events(self):
        out = [self.begin] + [partial(self.add_pair, i) for i in range(4)]
        for which in range(2):
            for m in (3, 2, 1):
                out += [partial(self.add_b_far, which, m), partial(self.step_far, which, m)]
            out.append(partial(self.add_b_far, which, 0))
        for which in range(2):
            out += [partial(self.step_near, which, m) for m in range(2)]
            if which == 0:
                out.append(self.to_a)
        return out + [self.add_a, self.finish]


def scatter_kernel(count, *refs):
    terms, outs, scratch = refs[:count], refs[count : 2 * count], refs[2 * count :]
    place = Place()
    place.meet()
    size = len(scratch) // count
    jobs = [Scatter(place, terms[i], outs[i], scratch[size * i : size * i + size]).events() for i in range(count)]
    lag = 6
    for step in range(len(jobs[0]) + lag * (count - 1)):
        for i in range(count):
            if 0 <= step - lag * i < len(jobs[i]):
                jobs[i][step - lag * i]()


def scatter_all(terms, identity):
    count = len(terms)
    scratch = []
    for t in terms:
        scratch += scatter_buffers(*t.shape[1:])
    return pl.pallas_call(
        partial(scatter_kernel, count),
        name="scatter",
        in_specs=[pl.BlockSpec(memory_space=pl.ANY)] * count,
        out_specs=[pl.BlockSpec(memory_space=pltpu.VMEM)] * count,
        out_shape=[jax.ShapeDtypeStruct((t.shape[1] // 2, t.shape[2]), F32) for t in terms],
        scratch_shapes=scratch,
        compiler_params=pltpu.CompilerParams(
            collective_id=identity, has_side_effects=True, vmem_limit_bytes=66_000_000
        ),
    )(*terms)


def dot(left, right):
    return lax.dot_general(left, right, (((1,), (0,)), ((), ())), preferred_element_type=F32)


def dot_right(left, right):
    return lax.dot_general(left, right, (((1,), (1,)), ((), ())), preferred_element_type=F32)


def at_slot(slot, plan):
    def choose(slots):
        if len(slots) == 1:

            @pl.when(slot == slots[0])
            def _():
                for event in plan[slots[0]]:
                    event()

            return
        middle_slot = slots[len(slots) // 2]

        @pl.when(slot < middle_slot)
        def _():
            choose(slots[: len(slots) // 2])

        @pl.when(slot >= middle_slot)
        def _():
            choose(slots[len(slots) // 2 :])

    if plan:
        choose(sorted(plan))


def fill_mask(seg_ref, pad_ref, mask_ref):
    length = mask_ref.shape[0]
    seg_row = seg_ref[0].astype(F32)
    pad_row = pad_ref[0].astype(F32)
    seg_col = jnp.transpose(jnp.broadcast_to(seg_row, (128, length)))
    pad_col = jnp.transpose(jnp.broadcast_to(pad_row, (128, length)))
    key_at = lax.broadcasted_iota(jnp.int32, (length, 128), 0)
    lane = lax.broadcasted_iota(jnp.int32, (length, 128), 1)
    for block in range(length // 128):
        same = seg_col == seg_row[:, 128 * block : 128 * block + 128]
        seen = (pad_col == 1.0) | (key_at == lane + 128 * block)
        mask_ref[:, 128 * block : 128 * block + 128] = jnp.where(same & seen, 0.0, -1e30)


def forward_kernel(count, x_ref, w_ref, vec_ref, seg_ref, pad_ref, *refs):
    shards, refs = refs[:count], refs[count:]
    qkv_ref, att_ref, lse_ref = refs[:3]
    fulls, mask_ref, sems = refs[3 : 3 + count], refs[3 + count], refs[4 + count :]
    step = pl.program_id(0)
    width = x_ref.shape[1]
    plan = {}
    if count:
        place = Place()
        pl.when(step == 0)(place.meet)
        for slot, index, event in sorted(
            [(slot, i, e) for i in range(count) for slot, e in Gather(place, shards[i], fulls[i], sems[4 * i : 4 * i + 4]).timed()],
            key=lambda item: item[0],
        ):
            plan.setdefault(slot, []).append(event)
        ending = plan.pop(24)
    fill_mask(seg_ref, pad_ref, mask_ref)
    for part, row in enumerate((BQ, None, BV)):
        cols = slice(part * width, (part + 1) * width)
        product = dot(x_ref[...], w_ref[:, cols])
        if row is not None:
            product = product + vec_ref[row : row + 1, :]
        qkv_ref[:, cols] = product.astype(BF16)
    half = width // HEADS
    first_half = lax.broadcasted_iota(jnp.int32, (1, 2 * half), 1) < half

    def pair(index, carry):
        at_slot(step * (HEADS // 2) + index, plan)
        base = pl.multiple_of(index * 2 * half, 2 * half)
        queries = qkv_ref[:, pl.ds(base, 2 * half)]
        keys = qkv_ref[:, pl.ds(width + base, 2 * half)]
        values_t = jnp.transpose(qkv_ref[:, pl.ds(2 * width + base, 2 * half)])
        keys = keys * jnp.asarray(0.125, BF16)
        outs = []
        for head in range(2):
            mine = first_half if head == 0 else ~first_half
            scores = dot_right(jnp.where(mine, keys, jnp.zeros_like(keys)), queries)
            scores = scores + mask_ref[...]
            top = jnp.max(scores, 0, keepdims=True)
            expo = jnp.exp(scores - top)
            total = jnp.sum(expo, 0, keepdims=True)
            probs = (expo * (1.0 / total)).astype(BF16)
            outs.append(dot(values_t[head * half : (head + 1) * half], probs))
            lse_ref[0, pl.ds(2 * index + head, 1), :] = top + jnp.log(total)
        att_ref[:, pl.ds(base, 2 * half)] = jnp.transpose(jnp.concatenate(outs, 0)).astype(BF16)
        return carry

    lax.fori_loop(0, HEADS // 2, pair, 0)
    if count:

        @pl.when(step == pl.num_programs(0) - 1)
        def _():
            for event in ending:
                event()


def attention_forward(rows, w_qkv, vectors, segments, pads, shards):
    seqs, _, length = segments.shape
    width = rows.shape[1]
    whole = lambda shape: pl.BlockSpec(shape, lambda i: (0,) * len(shape), pipeline_mode=pl.Buffered(1))
    row = lambda cols: pl.BlockSpec((length, cols), lambda i: (i, 0))
    tokens = pl.BlockSpec((1, 1, length), lambda i: (i, 0, 0))
    anywhere = [pl.BlockSpec(memory_space=pl.ANY)] * len(shards)
    remote = dict(collective_id=1, has_side_effects=True) if shards else {}
    return pl.pallas_call(
        partial(forward_kernel, len(shards)),
        name="attention_forward",
        grid=(seqs,),
        in_specs=[row(width), whole((width, 3 * width)), whole(vectors.shape), tokens, tokens] + anywhere,
        out_specs=[row(3 * width), row(width), pl.BlockSpec((1, 16, length), lambda i: (i, 0, 0))] + anywhere,
        out_shape=[
            jax.ShapeDtypeStruct((rows.shape[0], 3 * width), BF16),
            jax.ShapeDtypeStruct((rows.shape[0], width), BF16),
            jax.ShapeDtypeStruct((seqs, 16, length), F32),
        ]
        + [jax.ShapeDtypeStruct((32, *s.shape), s.dtype) for s in shards],
        scratch_shapes=[pltpu.VMEM((length, length), F32)] + GATHER_SEMS * len(shards),
        compiler_params=pltpu.CompilerParams(vmem_limit_bytes=VMEM_BYTES, **remote),
        cost_estimate=pl.CostEstimate(flops=12_000_000_000, bytes_accessed=20_000_000, transcendentals=12_000_000),
    )(rows, w_qkv, vectors, segments, pads, *shards)


def norm_parts(arr):
    centre = arr - jnp.mean(arr, -1, keepdims=True)
    scale = lax.rsqrt(jnp.mean(centre * centre, -1, keepdims=True) + 1e-12)
    return centre * scale, scale


def norm_back(grad_normal, normal, scale):
    return scale * (
        grad_normal
        - jnp.mean(grad_normal, -1, keepdims=True)
        - normal * jnp.mean(grad_normal * normal, -1, keepdims=True)
    )


def column_sum(arr):
    return jnp.sum(arr.astype(F32), 0, keepdims=True)


def middle_kernel(
    scale_ref, x_ref, att_ref, cot_ref, wo_ref, win_ref, wd_ref, vec_ref, bin_ref,
    out_ref, sum_ref, datt_ref, gwo_ref, gwin_ref, gwd_ref, gvec_ref, gbin_ref,
    acc_wo, acc_win, acc_wd, act_ref, slope_ref,
):
    step = pl.program_id(0)
    width = x_ref.shape[1]
    hidden = win_ref.shape[1]
    chunks = hidden // width

    @pl.when(step == 0)
    def _():
        acc_wo[...] = jnp.zeros_like(acc_wo)
        acc_win[...] = jnp.zeros_like(acc_win)
        acc_wd[...] = jnp.zeros_like(acc_wd)
        gvec_ref[...] = jnp.zeros_like(gvec_ref)
        gbin_ref[...] = jnp.zeros_like(gbin_ref)

    vec = lambda row: vec_ref[row : row + 1, :]
    branch = dot(att_ref[...], wo_ref[...]) + vec(BO)
    normal_one, scale_one = norm_parts(x_ref[...].astype(F32) + branch)
    first = normal_one * vec(G1) + vec(S1)
    first_low = first.astype(BF16)
    second = first + vec(BD)
    for chunk in range(chunks):
        cols = slice(chunk * width, (chunk + 1) * width)
        pre = dot(first_low, win_ref[:, cols]) + bin_ref[:, cols]
        below = 0.5 + 0.5 * lax.erf(pre * 0.7071067811865476)
        act = (pre * below).astype(BF16)
        act_ref[:, cols] = act
        slope_ref[:, cols] = below + pre * (jnp.exp(pre * pre * -0.5) * 0.3989422804014327)
        second = second + dot(act, wd_ref[cols, :])
    normal_two, scale_two = norm_parts(second)
    out_ref[...] = (normal_two * vec(G2) + vec(S2)).astype(BF16)
    cot = cot_ref[...].astype(F32)
    gvec_ref[G2 : G2 + 1, :] += column_sum(cot * normal_two)
    gvec_ref[S2 : S2 + 1, :] += column_sum(cot)
    grad_second = norm_back(cot * vec(G2), normal_two, scale_two)
    grad_low = grad_second.astype(BF16)
    gvec_ref[BD : BD + 1, :] += column_sum(grad_low)
    first_t = jnp.transpose(first_low)
    grad_first = grad_second
    for chunk in range(chunks):
        cols = slice(chunk * width, (chunk + 1) * width)
        grad_pre = (slope_ref[:, cols] * dot_right(grad_low, wd_ref[cols, :])).astype(BF16)
        gbin_ref[:, cols] += column_sum(grad_pre)
        acc_wd[cols, :] += dot(jnp.transpose(act_ref[:, cols]), grad_low)
        acc_win[:, cols] += dot(first_t, grad_pre)
        grad_first = grad_first + dot_right(grad_pre, win_ref[:, cols])
    gvec_ref[G1 : G1 + 1, :] += column_sum(grad_first * normal_one)
    gvec_ref[S1 : S1 + 1, :] += column_sum(grad_first)
    grad_sum = norm_back(grad_first * vec(G1), normal_one, scale_one)
    sum_ref[...] = grad_sum
    grad_one = grad_sum.astype(BF16)
    gvec_ref[BO : BO + 1, :] += column_sum(grad_one)
    acc_wo[...] += dot(jnp.transpose(att_ref[...]), grad_one)
    datt_ref[...] = dot_right(grad_one, wo_ref[...]).astype(BF16)

    @pl.when(step == pl.num_programs(0) - 1)
    def _():
        weight = scale_ref[0]
        gwo_ref[...] = (acc_wo[...] * weight).astype(BF16)
        gwin_ref[...] = (acc_win[...] * weight).astype(BF16)
        gwd_ref[...] = (acc_wd[...] * weight).astype(BF16)
        gvec_ref[...] = gvec_ref[...] * weight
        gbin_ref[...] = gbin_ref[...] * weight


def middle(scale, rows, att, cot, w_out, w_in, w_down, vectors, b_in):
    count, width = rows.shape
    hidden = w_in.shape[1]
    tile = 256
    whole = lambda shape: pl.BlockSpec(shape, lambda i: (0,) * len(shape), pipeline_mode=pl.Buffered(1))
    row = pl.BlockSpec((tile, width), lambda i: (i, 0))
    shape = jax.ShapeDtypeStruct
    return pl.pallas_call(
        middle_kernel,
        name="middle",
        grid=(count // tile,),
        in_specs=[pl.BlockSpec(memory_space=pltpu.SMEM), row, row, row]
        + [whole(a.shape) for a in (w_out, w_in, w_down, vectors, b_in)],
        out_specs=[row, row, row]
        + [whole(s) for s in (w_out.shape, w_in.shape, w_down.shape, (16, width), (1, hidden))],
        out_shape=[
            shape((count, width), BF16),
            shape((count, width), F32),
            shape((count, width), BF16),
            shape(w_out.shape, BF16),
            shape(w_in.shape, BF16),
            shape(w_down.shape, BF16),
            shape((16, width), F32),
            shape((1, hidden), F32),
        ],
        scratch_shapes=[
            pltpu.VMEM(w_out.shape, F32),
            pltpu.VMEM(w_in.shape, F32),
            pltpu.VMEM(w_down.shape, F32),
            pltpu.VMEM((tile, hidden), BF16),
            pltpu.VMEM((tile, hidden), F32),
        ],
        compiler_params=pltpu.CompilerParams(vmem_limit_bytes=VMEM_BYTES),
        cost_estimate=pl.CostEstimate(flops=65_000_000_000, bytes_accessed=60_000_000, transcendentals=12_000_000),
    )(scale, rows, att, cot, w_out, w_in, w_down, vectors, b_in)


def backward_kernel(
    count, scale_ref, x_ref, qkv_ref, datt_ref, lse_ref, seg_ref, pad_ref, sum_ref, w_ref, rest_ref, *refs
):
    terms, refs = refs[:count], refs[count:]
    gx_ref, gw_ref = refs[:2]
    sums, refs = refs[2 : 2 + count], refs[2 + count :]
    acc_ref, gvec_ref, dqkv_ref, mask_ref = refs[:4]
    step = pl.program_id(0)
    plan = {}
    if count:
        place = Place()
        pl.when(step == 0)(place.meet)
        each = (len(refs) - 4) // count
        for slot, index, event in sorted(
            [
                (slot, i, e)
                for i in range(count)
                for slot, e in Scatter(place, terms[i], sums[i], refs[4 + each * i : 4 + each * (i + 1)]).timed()
            ],
            key=lambda item: item[0],
        ):
            plan.setdefault(slot, []).append(event)
        ending = plan.pop(24)
    width = x_ref.shape[1]
    half = width // HEADS
    fill_mask(seg_ref, pad_ref, mask_ref)
    first_half = lax.broadcasted_iota(jnp.int32, (1, 2 * half), 1) < half

    @pl.when(step == 0)
    def _():
        acc_ref[...] = jnp.zeros_like(acc_ref)
        gvec_ref[...] = jnp.zeros_like(gvec_ref)

    def pair(index, carry):
        at_slot(step * (HEADS // 2) + index, plan)
        base = pl.multiple_of(index * 2 * half, 2 * half)
        queries = qkv_ref[:, pl.ds(base, 2 * half)]
        keys = qkv_ref[:, pl.ds(width + base, 2 * half)]
        values = qkv_ref[:, pl.ds(2 * width + base, 2 * half)]
        grads = datt_ref[:, pl.ds(base, 2 * half)]
        keys_t = jnp.transpose(keys)
        keys = keys * jnp.asarray(0.125, BF16)
        grad_k = jnp.zeros(keys.shape, F32)
        grad_v = jnp.zeros(keys.shape, F32)
        grad_q = []
        for head in range(2):
            mine = first_half if head == 0 else ~first_half
            only = lambda arr: jnp.where(mine, arr, jnp.zeros_like(arr))
            scores = dot_right(only(keys), queries) + mask_ref[...]
            probs = jnp.exp(scores - lse_ref[0, pl.ds(2 * index + head, 1), :])
            grad_probs = dot_right(only(values), grads)
            inner = jnp.sum(probs * grad_probs, 0, keepdims=True)
            grad_scores = (probs * (grad_probs - inner)).astype(BF16)
            grad_v = grad_v + dot(probs.astype(BF16), only(grads))
            grad_k = grad_k + dot(grad_scores, only(queries))
            grad_q.append(dot(keys_t[head * half : (head + 1) * half], grad_scores))
        grad_q = jnp.transpose(jnp.concatenate(grad_q, 0))
        dqkv_ref[:, pl.ds(base, 2 * half)] = (grad_q * 0.125).astype(BF16)
        dqkv_ref[:, pl.ds(width + base, 2 * half)] = (grad_k * 0.125).astype(BF16)
        dqkv_ref[:, pl.ds(2 * width + base, 2 * half)] = grad_v.astype(BF16)
        return carry

    lax.fori_loop(0, HEADS // 2, pair, 0)
    x_t = jnp.transpose(x_ref[...])
    grad_x = sum_ref[...]
    for part in range(3):
        cols = slice(part * width, (part + 1) * width)
        grad = dqkv_ref[:, cols]
        acc_ref[:, cols] += dot(x_t, grad)
        grad_x = grad_x + dot_right(grad, w_ref[:, cols])
        if part != 1:
            row = BQ if part == 0 else BV
            gvec_ref[row : row + 1, :] += column_sum(grad)
    gx_ref[...] = grad_x

    @pl.when(step == pl.num_programs(0) - 1)
    def _():
        gw_ref[:, : 3 * width] = (acc_ref[...] * scale_ref[0]).astype(BF16)
        gvec_ref[:2] = gvec_ref[:2] * scale_ref[0]
        gvec_ref[2:VECTORS] = rest_ref[2:VECTORS]
        gw_ref[:, 3 * width : 3 * width + 128] = jnp.transpose(gvec_ref[...]).astype(BF16)
        gw_ref[:, 3 * width + 128 :] = jnp.zeros((width, gw_ref.shape[1] - 3 * width - 128), BF16)
        if count:
            for event in ending:
                event()


def attention_backward(scale, rows, qkv, datt, lse, segments, pads, grad_sum, w_qkv, rest, terms):
    seqs, _, length = segments.shape
    count, width = rows.shape
    whole = lambda shape: pl.BlockSpec(shape, lambda i: (0,) * len(shape), pipeline_mode=pl.Buffered(1))
    row = lambda cols: pl.BlockSpec((length, cols), lambda i: (i, 0))
    tokens = pl.BlockSpec((1, 1, length), lambda i: (i, 0, 0))
    shape = jax.ShapeDtypeStruct
    anywhere = [pl.BlockSpec(memory_space=pl.ANY)] * len(terms)
    remote = dict(collective_id=3, has_side_effects=True) if terms else {}
    sums = [(t.shape[1] // 2, t.shape[2]) for t in terms]
    buffers = [b for t in terms for b in scatter_buffers(*t.shape[1:])]
    return pl.pallas_call(
        partial(backward_kernel, len(terms)),
        name="attention_backward",
        grid=(seqs,),
        in_specs=[
            pl.BlockSpec(memory_space=pltpu.SMEM),
            row(width),
            row(3 * width),
            row(width),
            pl.BlockSpec((1, 16, length), lambda i: (i, 0, 0)),
            tokens,
            tokens,
            row(width),
            whole((width, 3 * width)),
            whole(rest.shape),
        ]
        + anywhere,
        out_specs=[row(width), whole(w_qkv.shape)] + [whole(s) for s in sums],
        out_shape=[shape((count, width), F32), shape(w_qkv.shape, BF16)] + [shape(s, F32) for s in sums],
        scratch_shapes=[
            pltpu.VMEM((width, 3 * width), F32),
            pltpu.VMEM((128, width), F32),
            pltpu.VMEM((length, 3 * width), BF16),
            pltpu.VMEM((length, length), F32),
        ]
        + buffers,
        compiler_params=pltpu.CompilerParams(vmem_limit_bytes=VMEM_BYTES, **remote),
        cost_estimate=pl.CostEstimate(flops=31_000_000_000, bytes_accessed=35_000_000, transcendentals=12_000_000),
    )(scale, rows, qkv, datt, lse, segments, pads, grad_sum, w_qkv, rest, *terms)


def body(
    hidden_in, out_grad, segment_ids, pad_mask, task_weight, w_qkv, b_query, b_value, w_out, b_out,
    gain_one, shift_one, w_in, b_in, w_down, b_down, gain_two, shift_two,
):
    seqs, length, width = hidden_in.shape
    mine = w_qkv.shape[0]
    near = lax.axis_size("task") == 4 and lax.axis_size("batch") == 8 and mine % 8 == 0
    packed = jnp.stack([b_query, b_value, b_out, gain_one, shift_one, b_down, gain_two, shift_two], 1)
    packed = jnp.concatenate([packed, b_in.reshape(mine, -1)], 1)
    packed = jnp.pad(packed, ((0, 0), (0, 256 - packed.shape[1])))
    shards = [jnp.concatenate([w_qkv, packed], 1), w_out, w_in, w_down]
    flat = lambda arr: arr.reshape(-1, arr.shape[-1])
    if near:
        early, later = flat(gather_all(shards[:1], 0)[0]), []
    else:
        early, *later = [lax.all_gather(s, AXES, axis=0, tiled=True) for s in shards]
    vectors = jnp.transpose(early[:, 3 * width : 3 * width + 8].astype(F32))
    bin_full = early[:, 3 * width + BIN : 3 * width + VECTORS].astype(F32).reshape(1, -1)
    rows = hidden_in.reshape(-1, width)
    segments = segment_ids.reshape(seqs, 1, length)
    pads = pad_mask.reshape(seqs, 1, length)
    qkv, att, lse, *gathered = attention_forward(rows, early, vectors, segments, pads, shards[1:] if near else [])
    wo_full, win_full, wd_full = later or map(flat, gathered)
    hidden_out, grad_sum, datt, g_wo, g_win, g_wd, g_vec, g_bin = middle(
        task_weight, rows, att, out_grad.reshape(-1, width), wo_full, win_full, wd_full, vectors, bin_full
    )
    g_rest = jnp.concatenate([g_vec[:8], jnp.transpose(g_bin.reshape(width, -1)), g_vec[8:12]], 0)
    blocks = lambda arr: arr.reshape(16, -1, arr.shape[1])
    rest = (g_wd, g_win, g_wo)
    grad_x, g_qkv, *sums = attention_backward(
        task_weight, rows, qkv, datt, lse, segments, pads, grad_sum, early, g_rest, list(map(blocks, rest)) if near else []
    )
    if near:
        (late,) = scatter_all([blocks(g_qkv)], 2)
    else:
        late, *sums = [
            lax.psum_scatter(t, AXES, scatter_dimension=0, tiled=True).astype(F32) for t in (g_qkv, *rest)
        ]
    s_wd, s_win, s_wo = sums
    vector = lambda row: late[:, 3 * width + row]
    return (
        hidden_out.reshape(hidden_in.shape),
        grad_x.reshape(hidden_in.shape),
        late[:, : 3 * width],
        vector(BQ),
        vector(BV),
        s_wo,
        vector(BO),
        vector(G1),
        vector(S1),
        s_win,
        late[:, 3 * width + BIN : 3 * width + VECTORS].reshape(-1),
        s_wd,
        vector(BD),
        vector(G2),
        vector(S2),
    )


def solution(mesh):
    seq, mat, vec = P(AXES, None, None), P(AXES, None), P(AXES)
    weights = (mat, vec, vec, mat, vec, vec, vec, mat, vec, mat, vec, vec, vec)
    return jax.shard_map(
        body,
        mesh=mesh,
        in_specs=(seq, seq, mat, mat, P("task")) + weights,
        out_specs=(seq, seq) + weights,
        check_vma=False,
    )
```

```python
from functools import partial

import jax
import jax.numpy as jnp
from jax import lax
from jax.experimental import pallas as pl
from jax.experimental.pallas import tpu as pltpu
from jax.sharding import PartitionSpec as P

HEADS = 12
GROUPS = 3
AXES = ("task", "batch")
F32 = jnp.float32
BF16 = jnp.bfloat16
VMEM_BYTES = 66_900_000
BQ, BV, BO, G1, S1, BD, G2, S2, BIN = range(9)
VECTORS = 12

GATHER_TABLE = [
    (0, 0, 0), (0, 1, 0), (0, 0, 1), (0, 1, 1), (0, 0, 2), (0, 0, 3), (0, 0, 4), (0, 0, 5), (0, 1, 2), (0, 1, 3),
    (0, 1, 4), (0, 1, 5), (0, 0, 6), (0, 0, 7), (0, 0, 8), (0, 0, 9), (0, 0, 10), (0, 0, 11), (0, 2, 0), (0, 0, 14),
    (0, 0, 12), (0, 0, 13), (0, 1, 6), (0, 1, 7), (0, 1, 8), (0, 1, 10), (0, 2, 1), (0, 3, 0), (0, 0, 15), (0, 0, 16),
    (0, 0, 17), (0, 0, 18), (0, 0, 21), (0, 0, 22), (0, 1, 9), (0, 1, 11), (0, 1, 14), (0, 0, 19), (0, 0, 20),
    (0, 0, 23), (0, 0, 24), (0, 3, 1), (0, 4, 0), (0, 5, 0), (0, 6, 0), (0, 1, 12), (0, 1, 13), (0, 1, 15),
    (0, 1, 16), (0, 1, 17), (0, 1, 18), (0, 1, 21), (0, 0, 26), (0, 2, 2), (0, 2, 3), (0, 4, 1), (0, 5, 1),
    (0, 0, 25), (0, 2, 4), (0, 2, 5), (0, 6, 1), (0, 0, 27), (0, 0, 28), (0, 1, 22), (0, 0, 29), (0, 3, 2), (0, 3, 3),
    (0, 3, 4), (0, 3, 5), (0, 1, 23), (0, 1, 24), (0, 1, 19), (0, 1, 20), (0, 1, 25), (0, 1, 26), (0, 2, 6),
    (0, 2, 7), (0, 1, 27), (0, 1, 28), (0, 2, 8), (0, 2, 9), (0, 2, 10), (0, 2, 11), (0, 2, 12), (0, 2, 13),
    (0, 2, 14), (0, 3, 6), (0, 3, 7), (0, 3, 8), (0, 3, 10), (0, 3, 11), (0, 4, 2), (0, 4, 3), (0, 4, 4), (0, 4, 5),
    (0, 5, 2), (0, 5, 3), (0, 5, 4), (0, 5, 5), (0, 6, 2), (0, 6, 3), (0, 6, 4), (0, 6, 5), (0, 1, 29), (0, 3, 9),
    (0, 3, 14), (1, 2, 15), (1, 2, 16), (1, 2, 17), (1, 2, 18), (1, 2, 21), (1, 2, 22), (1, 3, 12), (1, 3, 13),
    (2, 2, 19), (2, 2, 20), (2, 2, 23), (2, 2, 24), (2, 3, 15), (2, 3, 16), (2, 3, 17), (2, 3, 18), (2, 4, 7),
    (2, 4, 8), (3, 3, 21), (3, 4, 6), (3, 4, 9), (3, 4, 10), (3, 4, 11), (3, 4, 12), (4, 5, 6), (5, 5, 7), (5, 5, 8),
    (6, 5, 9), (7, 5, 10), (7, 5, 11), (7, 5, 12), (8, 6, 6), (9, 2, 27), (9, 2, 28), (9, 3, 19), (9, 3, 20),
    (9, 3, 23), (9, 3, 24), (9, 6, 9), (10, 6, 7), (10, 6, 8), (10, 6, 10), (11, 2, 25), (11, 2, 26), (11, 3, 22),
    (11, 3, 25), (11, 3, 26), (11, 4, 13), (12, 2, 29), (12, 4, 14), (12, 4, 17), (12, 4, 18), (12, 6, 11),
    (12, 6, 12), (13, 3, 27), (13, 3, 28), (13, 4, 15), (13, 4, 16), (13, 4, 19), (13, 4, 20), (13, 5, 13),
    (14, 3, 29), (14, 5, 14), (16, 4, 25), (16, 4, 26), (16, 5, 15), (16, 5, 16), (16, 5, 17), (16, 5, 18),
    (17, 6, 13), (18, 5, 19), (18, 5, 20), (18, 6, 14), (19, 4, 21), (19, 4, 22), (19, 6, 17), (19, 6, 18),
    (20, 6, 15), (20, 6, 16), (21, 5, 21), (21, 5, 22), (21, 5, 25), (21, 5, 26), (23, 4, 23), (23, 4, 24),
    (23, 6, 19), (23, 6, 20), (23, 6, 21), (23, 6, 22), (25, 4, 27), (25, 4, 28), (26, 4, 29), (26, 5, 23),
    (26, 5, 24), (26, 6, 25), (26, 6, 26), (28, 6, 23), (28, 6, 24), (29, 5, 27), (29, 5, 28), (30, 5, 29),
    (31, 6, 27), (31, 6, 28), (32, 6, 29),
]
SCATTER_TABLE = [
    (0, 0, 0), (0, 1, 0), (0, 2, 0), (1, 0, 1), (2, 0, 2), (2, 0, 3), (3, 0, 4), (3, 0, 5), (3, 0, 6), (3, 0, 7),
    (3, 0, 8), (3, 1, 1), (4, 0, 9), (4, 0, 10), (4, 1, 2), (4, 1, 3), (5, 0, 11), (5, 0, 12), (5, 0, 15), (5, 0, 16),
    (5, 1, 4), (5, 2, 1), (5, 2, 2), (5, 2, 3), (5, 2, 4), (6, 0, 17), (6, 0, 18), (7, 0, 13), (7, 0, 19), (7, 0, 20),
    (7, 0, 21), (7, 0, 25), (8, 3, 0), (8, 0, 14), (8, 0, 22), (8, 0, 26), (8, 0, 27), (8, 0, 28), (8, 1, 5),
    (8, 1, 6), (8, 1, 7), (8, 1, 8), (8, 1, 9), (8, 1, 10), (9, 3, 1), (9, 3, 2), (9, 3, 3), (9, 3, 4), (9, 0, 23),
    (9, 1, 11), (9, 1, 15), (9, 1, 16), (10, 0, 29), (10, 1, 17), (10, 1, 18), (11, 0, 24), (11, 1, 19), (11, 1, 20),
    (11, 1, 21), (11, 2, 5), (11, 2, 6), (12, 0, 30), (12, 0, 31), (12, 1, 12), (12, 2, 7), (12, 2, 8), (12, 2, 9),
    (12, 2, 10), (12, 2, 11), (12, 2, 15), (12, 2, 16), (12, 2, 17), (12, 2, 18), (12, 2, 19), (12, 2, 20),
    (13, 3, 5), (13, 3, 6), (13, 0, 32), (13, 1, 13), (13, 2, 21), (14, 3, 7), (14, 3, 8), (14, 3, 9), (14, 3, 10),
    (14, 3, 11), (14, 3, 15), (14, 3, 16), (14, 3, 17), (14, 3, 18), (14, 3, 19), (14, 3, 20), (14, 0, 33),
    (14, 1, 25), (15, 3, 21), (15, 1, 14), (16, 4, 0), (16, 1, 22), (16, 1, 23), (16, 1, 26), (16, 1, 27),
    (16, 1, 28), (17, 4, 1), (17, 4, 2), (17, 4, 3), (17, 4, 4), (17, 1, 24), (17, 2, 12), (18, 4, 5), (18, 4, 6),
    (18, 4, 7), (18, 4, 8), (18, 1, 29), (18, 2, 13), (18, 2, 14), (18, 2, 22), (19, 3, 12), (19, 4, 9), (19, 4, 10),
    (19, 4, 11), (19, 4, 15), (19, 4, 16), (19, 4, 17), (19, 4, 18), (19, 4, 19), (19, 4, 20), (19, 4, 21),
    (19, 2, 23), (19, 2, 24), (20, 3, 13), (20, 3, 14), (20, 3, 22), (20, 1, 30), (20, 1, 31), (20, 1, 32),
    (20, 2, 25), (20, 2, 26), (21, 3, 23), (21, 3, 24), (21, 3, 25), (21, 4, 12), (21, 1, 33), (21, 2, 27),
    (21, 2, 28), (21, 2, 29), (21, 2, 30), (22, 3, 26), (22, 3, 27), (22, 3, 28), (22, 3, 29), (22, 3, 30),
    (22, 4, 13), (22, 4, 14), (22, 4, 22), (23, 3, 31), (23, 3, 32), (23, 4, 23), (23, 4, 24), (23, 4, 25),
    (23, 4, 26), (23, 2, 31), (23, 2, 32), (24, 3, 33), (24, 4, 27), (24, 4, 28), (24, 4, 29), (24, 4, 30),
    (24, 5, 0), (24, 6, 0), (24, 2, 33), (25, 4, 31), (25, 4, 32), (25, 5, 1), (25, 5, 2), (25, 5, 3), (25, 5, 4),
    (25, 6, 1), (25, 6, 2), (25, 6, 3), (25, 6, 4), (27, 4, 33), (27, 5, 5), (27, 5, 6), (27, 5, 7), (27, 5, 8),
    (29, 5, 9), (29, 5, 10), (29, 5, 11), (29, 5, 12), (29, 5, 15), (29, 5, 16), (29, 5, 17), (29, 5, 18),
    (29, 5, 19), (29, 5, 20), (29, 5, 21), (29, 6, 5), (29, 6, 6), (29, 6, 7), (29, 6, 8), (29, 6, 9), (29, 6, 10),
    (29, 6, 11), (31, 5, 13), (31, 5, 14), (31, 5, 25), (31, 6, 15), (31, 6, 16), (31, 6, 17), (31, 6, 18),
    (31, 6, 19), (31, 6, 20), (31, 6, 21), (32, 5, 22), (32, 5, 23), (32, 5, 24), (32, 5, 26), (32, 5, 27),
    (32, 5, 28), (32, 6, 12), (32, 6, 13), (32, 6, 14), (32, 5, 29), (32, 6, 22), (32, 6, 23), (32, 6, 24),
    (32, 5, 30), (32, 6, 25), (32, 6, 26), (32, 6, 29), (32, 6, 30), (32, 5, 31), (32, 5, 32), (32, 6, 27),
    (32, 6, 28), (32, 5, 33), (32, 6, 31), (32, 6, 32), (32, 6, 33),
]
GATHER_LINE_FIRST = [True, True, True, True, False, False, False]
SCATTER_LINE_LAST = [False, False, False, False, False, False, False]


MESH = pl.DeviceIdType.MESH


class Place:
    def __init__(self):
        self.task = lax.axis_index("task")
        self.batch = lax.axis_index("batch")
        self.core = self.batch % 2
        self.z = self.batch // 2
        x, y = self.task % 2, self.task // 2
        flip_x, flip_y = self.task + 1 - 2 * x, self.task + 2 - 4 * y
        self.task_a = (1 - self.core) * flip_x + self.core * flip_y
        self.task_b = (1 - self.core) * flip_y + self.core * flip_x
        self.task_ab = 3 - self.task
        self.partner = (self.task, self.batch + 1 - 2 * self.core)
        self.peer_a = (self.task_a, self.batch)
        self.peer_b = (self.task_b, self.batch)
        self.above = (self.task, self.batch + 2)
        self.below = (self.task, self.batch - 2)
        self.low = 1 - self.z // 2
        self.inner = self.low * self.z + (1 - self.low) * (3 - self.z)
        self.far = (self.task, self.batch + 4 * self.low - 2)
        self.near = (self.task, self.batch + 2 - 4 * self.low)

    def meet(self):
        barrier = pltpu.get_barrier_semaphore()
        for peer in (self.partner, self.peer_a, self.peer_b):
            pl.semaphore_signal(barrier, inc=1, device_id=peer, device_id_type=MESH)

        @pl.when(self.z < 3)
        def _():
            pl.semaphore_signal(barrier, inc=1, device_id=self.above, device_id_type=MESH)

        @pl.when(self.z > 0)
        def _():
            pl.semaphore_signal(barrier, inc=1, device_id=self.below, device_id_type=MESH)

        pl.semaphore_wait(barrier, 4 + self.z * (3 - self.z) // 2)


def remote(src, dst, send, recv, peer):
    return pltpu.make_async_remote_copy(src, dst, send, recv, device_id=peer, device_id_type=MESH)


GATHER_SEMS = [
    pltpu.SemaphoreType.DMA((12,)),
    pltpu.SemaphoreType.DMA((7,)),
    pltpu.SemaphoreType.DMA((14,)),
    pltpu.SemaphoreType.DMA((14,)),
    pltpu.SemaphoreType.DMA((6,)),
]


class Gather:
    def __init__(self, place, windows, full, sems, line_first=False):
        self.place, self.windows, self.full, self.line_first = place, windows, full, line_first
        self.send_z, self.send_a, self.recv, self.recv_b, self.misc = sems
        self.half = full.shape[1] // 2
        self.r = full.shape[0] // 32

    def rows(self, task, batch, count):
        return pl.ds(pl.multiple_of((task * 8 + batch) * self.r, 8), count * self.r)

    def cols(self, core):
        return pl.ds(pl.multiple_of(core * self.half, 128), self.half)

    def task(self, which):
        return self.place.task if which == 0 else self.place.task_a

    def level(self, spot):
        return self.place.z - spot if spot < 4 else self.place.z + spot - 3

    def here(self, spot):
        return self.place.z >= spot if spot < 4 else self.place.z + spot <= 6

    def chunk(self, task, spot):
        return self.full.at[self.rows(task, 2 * self.level(spot), 2), self.cols(self.place.core)]

    def begin(self):
        place, at = self.place, 0
        for window in self.windows:
            into = self.full.at[self.rows(place.task, place.batch, 1), pl.ds(at, window.shape[1])]
            pltpu.make_async_copy(window, into, self.misc.at[0]).start()
            remote(window, into, self.misc.at[1], self.misc.at[2], place.partner).start()
            at += window.shape[1]

    def along_z(self, which, spot, up):
        step = spot if up else max(spot - 3, 0)
        slot = which * 6 + step + (0 if up else 3)
        chunk = self.chunk(self.task(which), spot)
        into = which * 7 + step + (1 if up else 4)
        return remote(chunk, chunk, self.send_z.at[slot], self.recv.at[into], self.place.above if up else self.place.below)

    def along_a(self, spot):
        chunk = self.chunk(self.place.task, spot)
        return remote(chunk, chunk, self.send_a.at[spot], self.recv.at[7 + spot], self.place.peer_a)

    def along_b(self, which, spot):
        chunk = self.chunk(self.task(which), spot)
        return remote(chunk, chunk, self.misc.at[3], self.recv_b.at[which * 7 + spot], self.place.peer_b)

    def hand_over(self, task, spot):
        chunk = self.chunk(task, spot)
        remote(chunk, chunk, self.misc.at[4], self.misc.at[5], self.place.partner).start()

    def arrived(self, task, spot, sem):
        chunk = self.chunk(task, spot)
        remote(chunk, chunk, self.misc.at[1], sem, self.place.partner).wait_recv()

    def onward(self, which, spot):
        place = self.place
        if which == 0 or not self.line_first:
            for up in (True, False):
                if spot == 0 or (spot < 3 if up else 3 < spot < 6):
                    more = place.z < 3 if up else place.z > 0

                    @pl.when(more)
                    def _():
                        self.along_z(which, spot, up).start()

        if which == 0 and (spot == 0 or self.line_first):
            self.along_a(spot).start()
        self.along_b(which, spot).start()
        if which or spot:
            self.hand_over(self.task(which), spot)

    def spread(self):
        place = self.place
        mine = self.full.at[self.rows(place.task, place.batch, 1), :]
        pltpu.make_async_copy(mine, mine, self.misc.at[0]).wait()
        other = self.full.at[self.rows(place.task, place.partner[1], 1), :]
        remote(other, other, self.misc.at[1], self.misc.at[2], place.partner).wait_recv()
        self.onward(0, 0)

    def line(self, which, spot):
        @pl.when(self.here(spot))
        def _():
            self.arrived(self.task(which), spot, self.recv.at[which * 7 + spot])
            self.onward(which, spot)

    def from_b(self, which, spot):
        task = self.place.task_b if which == 0 else self.place.task_ab

        @pl.when(self.here(spot))
        def _():
            self.arrived(task, spot, self.recv_b.at[which * 7 + spot])
            self.hand_over(task, spot)

    def finish(self):
        place, full, r = self.place, self.full, self.r
        rest = full.at[pl.ds(0, 30 * r), self.cols(1 - place.core)]
        remote(rest, rest, self.misc.at[4], self.misc.at[5], place.partner).wait_recv()
        mine = full.at[pl.ds(0, 30 * r), self.cols(place.core)]
        remote(mine, mine, self.misc.at[4], self.misc.at[5], place.partner).wait_send()
        eight = full.at[pl.ds(0, 16 * r), self.cols(place.core)]
        remote(eight, eight, self.misc.at[3], self.recv_b.at[0], place.peer_b).wait_send()
        own = full.at[self.rows(place.task, place.batch, 1), :]
        remote(own, own, self.misc.at[1], self.misc.at[2], place.partner).wait_send()
        for spot in range(7 if self.line_first else 1):

            @pl.when(self.here(spot))
            def _():
                self.along_a(spot).wait_send()

        for which in range(1 if self.line_first else 2):
            for spot in (0, 1, 2):

                @pl.when(self.here(spot) & (place.z < 3))
                def _():
                    self.along_z(which, spot, True).wait_send()

            for spot in (0, 4, 5):

                @pl.when(self.here(spot) & (place.z > 0))
                def _():
                    self.along_z(which, spot, False).wait_send()

    def events(self):
        line, b = self.line, self.from_b
        out = [self.begin, self.spread]
        if self.line_first:
            out += [partial(line, 0, 1), partial(line, 0, 4), partial(line, 1, 0), partial(b, 0, 0)]
            out += [partial(line, 0, 2), partial(line, 0, 5), partial(line, 1, 1), partial(line, 1, 4)]
            out += [partial(b, 0, 1), partial(b, 0, 4), partial(line, 0, 3), partial(line, 0, 6), partial(b, 1, 0)]
            out += [partial(line, 1, 2), partial(line, 1, 5), partial(b, 0, 2), partial(b, 0, 5)]
            out += [partial(line, 1, 3), partial(line, 1, 6), partial(b, 1, 1), partial(b, 1, 4)]
            out += [partial(b, w, s) for w, s in ((0, 3), (0, 6), (1, 2), (1, 5), (1, 3), (1, 6))]
        else:
            out += [partial(line, 1, 0), partial(line, 0, 1), partial(line, 0, 4), partial(b, 0, 0), partial(b, 1, 0)]
            out += [partial(line, 1, 1), partial(line, 1, 4), partial(b, 0, 1), partial(b, 0, 4)]
            out += [partial(line, 0, 2), partial(line, 0, 5), partial(b, 1, 1), partial(b, 1, 4)]
            out += [partial(line, 1, 2), partial(line, 1, 5), partial(b, 0, 2), partial(b, 0, 5)]
            out += [partial(line, 0, 3), partial(line, 0, 6), partial(b, 1, 2), partial(b, 1, 5)]
            out += [partial(line, 1, 3), partial(line, 1, 6), partial(b, 0, 3), partial(b, 0, 6)]
            out += [partial(b, 1, 3), partial(b, 1, 6)]
        return out + [self.finish]


SCATTER_SEMS = [
    pltpu.SemaphoreType.DMA((4,)),
    pltpu.SemaphoreType.DMA((4,)),
    pltpu.SemaphoreType.DMA((4,)),
    pltpu.SemaphoreType.DMA((8,)),
    pltpu.SemaphoreType.DMA((8,)),
    pltpu.SemaphoreType.DMA((8,)),
    pltpu.SemaphoreType.DMA((10,)),
    pltpu.SemaphoreType.DMA((4,)),
    pltpu.SemaphoreType.DMA((4,)),
    pltpu.SemaphoreType.DMA((2,)),
]


def scatter_buffers(rows, cols, line_last=False):
    half = cols // 2
    return [
        pltpu.VMEM((16, rows, half), BF16),
        pltpu.VMEM((16, rows, half), BF16),
        pltpu.VMEM((8, rows, half), BF16),
        pltpu.VMEM((5 if line_last else 10, rows, half), BF16),
        pltpu.VMEM((4 if line_last else 1, rows, half), BF16),
        pltpu.VMEM((rows, half), F32),
        pltpu.VMEM((rows // 2, half), F32),
    ] + SCATTER_SEMS


class Scatter:
    def __init__(self, place, terms, out, buffers, line_last=False):
        self.place, self.terms, self.out, self.line_last = place, terms, out, line_last
        (self.own, self.other, self.got_b, self.got_z, self.got_a, self.total, self.got_f) = buffers[:7]
        (
            self.s_load, self.s_pair, self.r_pair, self.s_b, self.r_b, self.s_z, self.r_z, self.s_a, self.r_a, self.misc
        ) = buffers[7:]
        self.half = self.own.shape[2]
        self.tasks = (place.task_ab, place.task_b, place.task_a, place.task)
        self.tasks_partner = (place.task_ab, place.task_a, place.task_b, place.task)

    def cols(self, core):
        return pl.ds(pl.multiple_of(core * self.half, 128), self.half)

    def level(self, m):
        return self.place.low * m + (1 - self.place.low) * (3 - m)

    def load(self, index):
        first = self.tasks[index] * 4
        return pltpu.make_async_copy(
            self.terms.at[pl.ds(first, 4), :, self.cols(self.place.core)],
            self.own.at[pl.ds(first, 4)],
            self.s_load.at[index],
        )

    def pair(self, index, sent=True):
        first = (self.tasks_partner if sent else self.tasks)[index] * 4
        return remote(
            self.terms.at[pl.ds(first, 4), :, self.cols(1 - self.place.core)],
            self.other.at[pl.ds(first, 4)],
            self.s_pair.at[index],
            self.r_pair.at[index],
            self.place.partner,
        )

    def begin(self):
        for index in range(4):
            self.load(index).start()
            self.pair(index).start()

    def add(self, at, ref, where):
        self.own[at] = (self.own[at].astype(F32) + ref[where].astype(F32)).astype(BF16)

    def along_b(self, which, z):
        slot = which * 4 + z
        return remote(
            self.own.at[self.tasks[which] * 4 + z], self.got_b.at[slot], self.s_b.at[slot], self.r_b.at[slot],
            self.place.peer_b,
        )

    def add_pair(self, index):
        self.load(index).wait()
        self.pair(index, False).wait_recv()
        first = self.tasks[index] * 4
        for m in (3, 2, 1, 0):
            z = self.level(m)
            self.add(first + z, self.other, first + z)
            if index < 2:
                self.along_b(index, z).start()

    def add_b(self, which, m):
        z = self.level(m)
        self.along_b(which, z).wait_recv()
        self.add(self.tasks[2 + which] * 4 + z, self.got_b, which * 4 + z)
        if which == 0 and self.line_last:
            self.along_a(z).start()

    def along_z(self, which, m, far):
        place = self.place
        at = self.tasks[2 + which] * 4 + self.level(m)
        line = 0 if self.line_last else 5 * which
        into = line + ((1 - place.inner) * (m - 1) + place.inner * (6 - m) if far else 3 + m)
        peer = place.far if far else place.near
        return remote(self.own.at[at], self.got_z.at[into], self.s_z.at[which * 4 + m], self.r_z.at[into], peer)

    def add_z(self, which, m, slot):
        into = slot + (0 if self.line_last else 5 * which)
        got = self.got_z.at[into]
        remote(got, got, self.s_z.at[0], self.r_z.at[into], self.place.partner).wait_recv()
        self.add(self.tasks[2 + which] * 4 + self.level(m), self.got_z, into)

    def far_out(self, which, m):
        @pl.when(self.place.inner == 0)
        def _():
            self.along_z(which, m, True).start()

    def far_on(self, which, m):
        @pl.when(self.place.inner == 1)
        def _():
            self.add_z(which, m, m - 1)
            if m > 1:
                self.along_z(which, m, True).start()

    def near_on(self, which, m):
        @pl.when(self.place.inner == 1)
        def _():
            self.add_z(which, m, 3 + m)
            if m == 0:
                self.along_z(which, m, False).start()

    def near_in(self, which):
        @pl.when(self.place.inner == 0)
        def _():
            self.add_z(which, 0, 3)

    def along_a(self, z):
        slot = z if self.line_last else 0
        return remote(
            self.own.at[self.tasks[2] * 4 + z], self.got_a.at[slot], self.s_a.at[slot], self.r_a.at[slot],
            self.place.peer_a,
        )

    def to_a(self):
        self.along_a(self.place.z).start()

    def add_a(self, m):
        z = self.level(m)
        self.along_a(z).wait_recv()
        self.add(self.tasks[3] * 4 + z, self.got_a, z)

    def last(self):
        rows = self.got_f.shape[0]
        away = pl.multiple_of((1 - self.place.core) * rows, rows)
        return remote(
            self.total.at[pl.ds(away, rows)], self.got_f, self.misc.at[0], self.misc.at[1], self.place.partner
        )

    def close(self):
        total = self.own[self.tasks[3] * 4 + self.place.z].astype(F32)
        if not self.line_last:
            self.along_a(self.place.z).wait_recv()
            total = total + self.got_a[0].astype(F32)
        self.total[...] = total
        self.last().start()

    def finish(self):
        rows = self.got_f.shape[0]
        core = self.place.core
        self.last().wait_recv()
        self.out[:, self.cols(core)] = self.total[pl.ds(pl.multiple_of(core * rows, rows), rows), :]
        self.out[:, self.cols(1 - core)] = self.got_f[...]
        for index in range(4):
            self.pair(index).wait_send()
        for which in range(2):
            for z in range(4):
                self.along_b(which, z).wait_send()
        for which in range(1 if self.line_last else 0, 2):
            for m in range(4):

                @pl.when(self.place.inner < m)
                def _():
                    self.along_z(which, m, True).wait_send()

                @pl.when(self.place.inner > m)
                def _():
                    self.along_z(which, m, False).wait_send()

        for z in range(4 if self.line_last else 1):
            self.along_a(z if self.line_last else self.place.z).wait_send()
        self.last().wait_send()

    def events(self):
        out = [self.begin] + [partial(self.add_pair, i) for i in range(4)]
        if self.line_last:
            out += [partial(self.add_b, which, m) for which in range(2) for m in (3, 2, 1, 0)]
            for m in (3, 2, 1):
                out += [partial(self.add_a, m), partial(self.far_out, 1, m)]
            out.append(partial(self.add_a, 0))
            out += [partial(self.far_on, 1, m) for m in (3, 2, 1)]
            out += [partial(self.near_on, 1, 0), partial(self.near_on, 1, 1), partial(self.near_in, 1)]
        else:
            for which in range(2):
                for m in (3, 2, 1):
                    out += [partial(self.add_b, which, m), partial(self.far_out, which, m)]
                out.append(partial(self.add_b, which, 0))
                out += [partial(self.far_on, which, m) for m in (3, 2, 1)]
            for which in range(2):
                out += [partial(self.near_on, which, 0), partial(self.near_on, which, 1), partial(self.near_in, which)]
                if which == 0:
                    out.append(self.to_a)
        return out + [self.close, self.finish]


def dot(left, right):
    return lax.dot_general(left, right, (((1,), (0,)), ((), ())), preferred_element_type=F32)


def dot_right(left, right):
    return lax.dot_general(left, right, (((1,), (1,)), ((), ())), preferred_element_type=F32)


def at_slot(slot, plan):
    def choose(slots):
        if len(slots) == 1:

            @pl.when(slot == slots[0])
            def _():
                for event in plan[slots[0]]:
                    event()

            return
        middle_slot = slots[len(slots) // 2]

        @pl.when(slot < middle_slot)
        def _():
            choose(slots[: len(slots) // 2])

        @pl.when(slot >= middle_slot)
        def _():
            choose(slots[len(slots) // 2 :])

    if plan:
        choose(sorted(plan))


def fill_mask(seg_ref, pad_ref, mask_ref):
    length = mask_ref.shape[0]
    seg_row = seg_ref[0].astype(F32)
    pad_row = pad_ref[0].astype(F32)
    seg_col = jnp.transpose(jnp.broadcast_to(seg_row, (128, length)))
    pad_col = jnp.transpose(jnp.broadcast_to(pad_row, (128, length)))
    key_at = lax.broadcasted_iota(jnp.int32, (length, 128), 0)
    lane = lax.broadcasted_iota(jnp.int32, (length, 128), 1)
    for block in range(length // 128):
        same = seg_col == seg_row[:, 128 * block : 128 * block + 128]
        seen = (pad_col == 1.0) | (key_at == lane + 128 * block)
        mask_ref[:, 128 * block : 128 * block + 128] = jnp.where(same & seen, 0.0, -1e30)


def planned(table, jobs):
    plan = {}
    events = [job.events() for job in jobs]
    for slot, job, event in table:
        plan.setdefault(slot, []).append(events[job][event])
    return plan


def run_now(plan, slot):
    for event in plan.get(slot, []):
        event()


def every(plan, per_step, part, last):
    return {slot // per_step: e for slot, e in plan.items() if slot % per_step == part and slot < last}


def forward_kernel(near, x_ref, seg_ref, pad_ref, *refs):
    if near:
        rows_ref, wqkv_ref, wo_ref, win_ref, wd_ref = refs[:5]
        qkv_ref, att_ref, lse_ref, vec_ref = refs[5:9]
        fulls = refs[9:16]
        mask_ref, w_ref, small_ref, load_sem, shard_ref = refs[16:21]
        sems = refs[21:]
    else:
        fulls = refs[:4]
        qkv_ref, att_ref, lse_ref, vec_ref = refs[4:8]
        mask_ref, w_ref, small_ref, load_sem = refs[8:]
    step = pl.program_id(0)
    length, width = x_ref.shape
    part = width // GROUPS
    half = width // HEADS
    steps = GROUPS * SEQS
    plan = {}
    if near:
        place = Place()
        windows = [[shard_ref]]
        for group in range(GROUPS):
            windows.append([wqkv_ref.at[:, pl.ds(third * width + group * part, part)] for third in range(3)])
        windows += [[wo_ref], [win_ref], [wd_ref]]
        jobs = [
            Gather(place, windows[i], fulls[i], sems[5 * i : 5 * i + 5], GATHER_LINE_FIRST[i]) for i in range(7)
        ]
        plan = planned(GATHER_TABLE, jobs)

    @pl.when(step == 0)
    def _():
        if near:
            rows = rows_ref[...].astype(F32)
            rows = jnp.concatenate([rows, jnp.zeros((128 - rows.shape[0], 128), F32)], 0)
            shard_ref[:, :128] = jnp.transpose(rows)[: shard_ref.shape[0]].astype(BF16)
            shard_ref[:, 128:] = jnp.zeros((shard_ref.shape[0], 128), BF16)
            place.meet()
            run_now(plan, 0)
        copy = pltpu.make_async_copy(fulls[0].at[:, pl.ds(0, 128)], small_ref, load_sem.at[0])
        copy.start()
        copy.wait()
        vec_ref[...] = jnp.transpose(small_ref[...].astype(F32))[:16]

    if near:
        at_slot(step, {k: v for k, v in every(plan, 3, 0, 3 * steps).items() if k})
    for group in range(GROUPS):

        @pl.when(step == group * SEQS)
        def _():
            copy = pltpu.make_async_copy(fulls[1 + group], w_ref, load_sem.at[1])
            copy.start()
            copy.wait()

    fill_mask(seg_ref, pad_ref, mask_ref)
    at = pl.multiple_of(step // SEQS * part, part)
    for third, row in enumerate((BQ, None, BV)):
        cols = slice(third * part, (third + 1) * part)
        product = dot(x_ref[...], w_ref[:, cols])
        if row is not None:
            product = product + vec_ref[row : row + 1, pl.ds(at, part)]
        qkv_ref[:, cols] = product.astype(BF16)
    first_half = lax.broadcasted_iota(jnp.int32, (1, 2 * half), 1) < half
    for pair in range(part // (2 * half)):
        if near:
            at_slot(step, every(plan, 3, 1 + pair, 3 * steps))
        cols = slice(pair * 2 * half, (pair + 1) * 2 * half)
        queries = qkv_ref[:, cols]
        keys = qkv_ref[:, part + cols.start : part + cols.stop] * jnp.asarray(0.125, BF16)
        values_t = jnp.transpose(qkv_ref[:, 2 * part + cols.start : 2 * part + cols.stop])
        outs = []
        for head in range(2):
            mine = first_half if head == 0 else ~first_half
            scores = dot_right(jnp.where(mine, keys, jnp.zeros_like(keys)), queries) + mask_ref[...]
            top = jnp.max(scores, 0, keepdims=True)
            expo = jnp.exp(scores - top)
            total = jnp.sum(expo, 0, keepdims=True)
            probs = (expo * (1.0 / total)).astype(BF16)
            outs.append(dot(values_t[head * half : (head + 1) * half], probs))
            row = 2 * pair + head
            lse_ref[0, row : row + 1, :] = top + jnp.log(total)
        att_ref[:, cols] = jnp.transpose(jnp.concatenate(outs, 0)).astype(BF16)
    if near:

        @pl.when(step == steps - 1)
        def _():
            run_now(plan, 3 * steps)


SEQS = 4


def attention_forward(near, rows, segments, pads, weights):
    seqs, _, length = segments.shape
    width = rows.shape[1]
    part = width // GROUPS
    anywhere = lambda count: [pl.BlockSpec(memory_space=pl.ANY)] * count
    tokens = pl.BlockSpec((1, 1, length), lambda i: (i % seqs, 0, 0))
    shape = jax.ShapeDtypeStruct
    out_specs = [
        pl.BlockSpec((length, width), lambda i: (i % seqs, i // seqs)),
        pl.BlockSpec((length, part), lambda i: (i % seqs, i // seqs)),
        pl.BlockSpec((1, 8, length), lambda i: (i, 0, 0)),
        pl.BlockSpec((16, width), lambda i: (0, 0)),
    ]
    out_shape = [
        shape((rows.shape[0], 3 * width), BF16),
        shape((rows.shape[0], width), BF16),
        shape((GROUPS * seqs, 8, length), F32),
        shape((16, width), F32),
    ]
    in_specs = [pl.BlockSpec((length, width), lambda i: (i % seqs, 0)), tokens, tokens]
    scratch = [
        pltpu.VMEM((length, length), F32),
        pltpu.VMEM((width, width), BF16),
        pltpu.VMEM((width, 128), BF16),
        pltpu.SemaphoreType.DMA((2,)),
    ]
    remotely = {}
    if near:
        packed, w_qkv, w_out, w_in, w_down = weights
        in_specs += [pl.BlockSpec(packed.shape, lambda i: (0, 0))] + anywhere(4)
        mine = w_qkv.shape[0]
        fulls = [(mine, 256)] + [(mine, width)] * GROUPS + [w.shape for w in (w_out, w_in, w_down)]
        out_specs += anywhere(7)
        out_shape += [shape((32 * r, c), BF16) for r, c in fulls]
        scratch += [pltpu.VMEM((mine, 256), BF16)] + GATHER_SEMS * 7
        remotely = dict(collective_id=0, has_side_effects=True)
    else:
        in_specs += anywhere(4)
    return pl.pallas_call(
        partial(forward_kernel, near),
        name="attention_forward",
        grid=(GROUPS * seqs,),
        in_specs=in_specs,
        out_specs=out_specs,
        out_shape=out_shape,
        scratch_shapes=scratch,
        compiler_params=pltpu.CompilerParams(vmem_limit_bytes=VMEM_BYTES, **remotely),
    )(rows, segments, pads, *weights)


def norm_parts(arr):
    centre = arr - jnp.mean(arr, -1, keepdims=True)
    scale = lax.rsqrt(jnp.mean(centre * centre, -1, keepdims=True) + 1e-12)
    return centre * scale, scale


def norm_back(grad_normal, normal, scale):
    return scale * (
        grad_normal
        - jnp.mean(grad_normal, -1, keepdims=True)
        - normal * jnp.mean(grad_normal * normal, -1, keepdims=True)
    )


def column_sum(arr):
    return jnp.sum(arr.astype(F32), 0, keepdims=True)


def middle_kernel(
    scale_ref, x_ref, att_ref, cot_ref, wo_ref, win_ref, wd_ref, vec_ref, bin_ref,
    out_ref, sum_ref, datt_ref, gwo_ref, gwin_ref, gwd_ref, gvec_ref, gbin_ref,
    acc_wo, acc_win, acc_wd, act_ref, slope_ref,
):
    step = pl.program_id(0)
    width = x_ref.shape[1]
    hidden = win_ref.shape[1]
    chunks = hidden // width

    @pl.when(step == 0)
    def _():
        acc_wo[...] = jnp.zeros_like(acc_wo)
        acc_win[...] = jnp.zeros_like(acc_win)
        acc_wd[...] = jnp.zeros_like(acc_wd)
        gvec_ref[...] = jnp.zeros_like(gvec_ref)
        gbin_ref[...] = jnp.zeros_like(gbin_ref)

    vec = lambda row: vec_ref[row : row + 1, :]
    branch = dot(att_ref[...], wo_ref[...]) + vec(BO)
    normal_one, scale_one = norm_parts(x_ref[...].astype(F32) + branch)
    first = normal_one * vec(G1) + vec(S1)
    first_low = first.astype(BF16)
    second = first + vec(BD)
    for chunk in range(chunks):
        cols = slice(chunk * width, (chunk + 1) * width)
        pre = dot(first_low, win_ref[:, cols]) + bin_ref[:, cols]
        below = 0.5 + 0.5 * lax.erf(pre * 0.7071067811865476)
        act = (pre * below).astype(BF16)
        act_ref[:, cols] = act
        slope_ref[:, cols] = below + pre * (jnp.exp(pre * pre * -0.5) * 0.3989422804014327)
        second = second + dot(act, wd_ref[cols, :])
    normal_two, scale_two = norm_parts(second)
    out_ref[...] = (normal_two * vec(G2) + vec(S2)).astype(BF16)
    cot = cot_ref[...].astype(F32)
    gvec_ref[G2 : G2 + 1, :] += column_sum(cot * normal_two)
    gvec_ref[S2 : S2 + 1, :] += column_sum(cot)
    grad_second = norm_back(cot * vec(G2), normal_two, scale_two)
    grad_low = grad_second.astype(BF16)
    gvec_ref[BD : BD + 1, :] += column_sum(grad_low)
    first_t = jnp.transpose(first_low)
    grad_first = grad_second
    for chunk in range(chunks):
        cols = slice(chunk * width, (chunk + 1) * width)
        grad_pre = (slope_ref[:, cols] * dot_right(grad_low, wd_ref[cols, :])).astype(BF16)
        gbin_ref[:, cols] += column_sum(grad_pre)
        acc_wd[cols, :] += dot(jnp.transpose(act_ref[:, cols]), grad_low)
        acc_win[:, cols] += dot(first_t, grad_pre)
        grad_first = grad_first + dot_right(grad_pre, win_ref[:, cols])
    gvec_ref[G1 : G1 + 1, :] += column_sum(grad_first * normal_one)
    gvec_ref[S1 : S1 + 1, :] += column_sum(grad_first)
    grad_sum = norm_back(grad_first * vec(G1), normal_one, scale_one)
    sum_ref[...] = grad_sum
    grad_one = grad_sum.astype(BF16)
    gvec_ref[BO : BO + 1, :] += column_sum(grad_one)
    acc_wo[...] += dot(jnp.transpose(att_ref[...]), grad_one)
    datt_ref[...] = dot_right(grad_one, wo_ref[...]).astype(BF16)

    @pl.when(step == pl.num_programs(0) - 1)
    def _():
        weight = scale_ref[0]
        gwo_ref[...] = (acc_wo[...] * weight).astype(BF16)
        gwin_ref[...] = (acc_win[...] * weight).astype(BF16)
        gwd_ref[...] = (acc_wd[...] * weight).astype(BF16)
        gvec_ref[...] = gvec_ref[...] * weight
        gbin_ref[...] = gbin_ref[...] * weight


def middle(scale, rows, att, cot, w_out, w_in, w_down, vectors, b_in):
    count, width = rows.shape
    hidden = w_in.shape[1]
    tile = 256
    whole = lambda shape: pl.BlockSpec(shape, lambda i: (0,) * len(shape), pipeline_mode=pl.Buffered(1))
    row = pl.BlockSpec((tile, width), lambda i: (i, 0))
    shape = jax.ShapeDtypeStruct
    return pl.pallas_call(
        middle_kernel,
        name="middle",
        grid=(count // tile,),
        in_specs=[pl.BlockSpec(memory_space=pltpu.SMEM), row, row, row]
        + [whole(a.shape) for a in (w_out, w_in, w_down, vectors, b_in)],
        out_specs=[row, row, row]
        + [whole(s) for s in (w_out.shape, w_in.shape, w_down.shape, (16, width), (1, hidden))],
        out_shape=[
            shape((count, width), BF16),
            shape((count, width), F32),
            shape((count, width), BF16),
            shape(w_out.shape, BF16),
            shape(w_in.shape, BF16),
            shape(w_down.shape, BF16),
            shape((16, width), F32),
            shape((1, hidden), F32),
        ],
        scratch_shapes=[
            pltpu.VMEM(w_out.shape, F32),
            pltpu.VMEM(w_in.shape, F32),
            pltpu.VMEM(w_down.shape, F32),
            pltpu.VMEM((tile, hidden), BF16),
            pltpu.VMEM((tile, hidden), F32),
        ],
        compiler_params=pltpu.CompilerParams(vmem_limit_bytes=VMEM_BYTES),
        cost_estimate=pl.CostEstimate(flops=65_000_000_000, bytes_accessed=60_000_000, transcendentals=12_000_000),
    )(scale, rows, att, cot, w_out, w_in, w_down, vectors, b_in)


def backward_kernel(near, scale_ref, x_ref, qkv_ref, datt_ref, lse_ref, seg_ref, pad_ref, sum_ref, rest_ref, *refs):
    w_refs, refs = refs[:GROUPS], refs[GROUPS:]
    step = pl.program_id(0)
    length, width = x_ref.shape
    part = width // GROUPS
    half = width // HEADS
    steps = GROUPS * SEQS
    plan = {}
    if near:
        given, gx_ref, sums, refs = refs[:3], refs[3], refs[4:11], refs[11:]
        xt_ref, dqkv_ref, gvec_ref, mask_ref = refs[:4]
        terms = refs[4 : 5 + GROUPS]
        refs = refs[5 + GROUPS :]
        each = len(refs) // 7
        place = Place()
        jobs = [
            Scatter(place, t, sums[i], refs[each * i : each * (i + 1)], SCATTER_LINE_LAST[i])
            for i, t in enumerate(given + terms)
        ]
        plan = planned(SCATTER_TABLE, jobs)
        put = lambda ref, value: ref.__setitem__(..., value.reshape(ref.shape))
    else:
        gx_ref, terms, refs = refs[0], refs[1 : 2 + GROUPS], refs[2 + GROUPS :]
        xt_ref, dqkv_ref, gvec_ref, mask_ref = refs
        put = lambda ref, value: ref.__setitem__(..., value)

    @pl.when(step == 0)
    def _():
        if near:
            place.meet()
        gvec_ref[...] = jnp.zeros_like(gvec_ref)

    @pl.when(step < SEQS)
    def _():
        xt_ref[:, pl.ds(pl.multiple_of(step * length, length), length)] = jnp.transpose(x_ref[...])

    at = pl.multiple_of(step % SEQS * length, length)

    @pl.when(step < steps)
    def _():
        group = step // SEQS
        fill_mask(seg_ref, pad_ref, mask_ref)
        first_half = lax.broadcasted_iota(jnp.int32, (1, 2 * half), 1) < half
        for pair in range(part // (2 * half)):
            if near:
                at_slot(step, every(plan, 2, pair, 2 * steps))
            cols = slice(pair * 2 * half, (pair + 1) * 2 * half)
            queries = qkv_ref[:, cols]
            keys = qkv_ref[:, part + cols.start : part + cols.stop]
            values = qkv_ref[:, 2 * part + cols.start : 2 * part + cols.stop]
            grads = datt_ref[:, cols]
            keys_t = jnp.transpose(keys)
            keys = keys * jnp.asarray(0.125, BF16)
            grad_k = jnp.zeros(keys.shape, F32)
            grad_v = jnp.zeros(keys.shape, F32)
            grad_q = []
            for head in range(2):
                mine = first_half if head == 0 else ~first_half
                only = lambda arr: jnp.where(mine, arr, jnp.zeros_like(arr))
                scores = dot_right(only(keys), queries) + mask_ref[...]
                row = 2 * pair + head
                probs = jnp.exp(scores - lse_ref[0, row : row + 1, :])
                grad_probs = dot_right(only(values), grads)
                inner = jnp.sum(probs * grad_probs, 0, keepdims=True)
                grad_scores = (probs * (grad_probs - inner)).astype(BF16)
                grad_v = grad_v + dot(probs.astype(BF16), only(grads))
                grad_k = grad_k + dot(grad_scores, only(queries))
                grad_q.append(dot(keys_t[head * half : (head + 1) * half], grad_scores))
            grad_q = jnp.transpose(jnp.concatenate(grad_q, 0))
            for third, value in enumerate((grad_q * 0.125, grad_k * 0.125, grad_v)):
                to = slice(third * part + cols.start, third * part + cols.stop)
                dqkv_ref[group, pl.ds(at, length), to] = value.astype(BF16)
                if third != 1:
                    row = BQ if third == 0 else BV
                    into = pl.ds(pl.multiple_of(group * part + cols.start, 2 * half), 2 * half)
                    gvec_ref[row : row + 1, into] += column_sum(value.astype(BF16))

    for group in range(GROUPS):

        @pl.when(step == group * SEQS + SEQS - 1)
        def _():
            for third in range(3):
                cols = slice(third * part, (third + 1) * part)
                grad = dot(xt_ref[...], dqkv_ref[group, :, cols]) * scale_ref[0]
                if near:
                    terms[group][:, :, cols] = grad.astype(BF16).reshape(*terms[group].shape[:2], part)
                else:
                    terms[group][:, cols] = grad.astype(BF16)

    @pl.when(step == steps - 1)
    def _():
        gvec_ref[:2] = gvec_ref[:2] * scale_ref[0]
        gvec_ref[2:VECTORS] = rest_ref[2:VECTORS]
        packed = jnp.transpose(gvec_ref[...]).astype(BF16)
        put(terms[GROUPS], jnp.concatenate([packed, jnp.zeros_like(packed)], 1))

    @pl.when(step >= steps)
    def _():
        if near:
            at_slot(step, {k: v for k, v in every(plan, 2, 0, 2 * (steps + SEQS)).items() if k >= steps})
        grad_x = sum_ref[...]
        for group in range(GROUPS):
            grad_x = grad_x + dot_right(dqkv_ref[group, pl.ds(at, length), :], w_refs[group][...])
        gx_ref[...] = grad_x
        if near:
            at_slot(step, {k: v for k, v in every(plan, 2, 1, 2 * (steps + SEQS)).items() if k >= steps})

    if near:

        @pl.when(step == steps + SEQS - 1)
        def _():
            run_now(plan, 2 * (steps + SEQS))


def attention_backward(near, scale, rows, qkv, datt, lse, segments, pads, grad_sum, rest, w_groups, given):
    seqs, _, length = segments.shape
    count, width = rows.shape
    part = width // GROUPS
    steps = GROUPS * seqs
    whole = lambda shape: pl.BlockSpec(shape, lambda i: (0,) * len(shape), pipeline_mode=pl.Buffered(1))
    now = lambda i: jnp.minimum(i, steps - 1)
    tokens = pl.BlockSpec((1, 1, length), lambda i: (now(i) % seqs, 0, 0))
    late = pl.BlockSpec((length, width), lambda i: (jnp.maximum(i - steps, 0), 0))
    shape = jax.ShapeDtypeStruct
    in_specs = [
        pl.BlockSpec(memory_space=pltpu.SMEM),
        pl.BlockSpec((length, width), lambda i: (jnp.minimum(i, seqs - 1), 0)),
        pl.BlockSpec((length, width), lambda i: (now(i) % seqs, now(i) // seqs)),
        pl.BlockSpec((length, part), lambda i: (now(i) % seqs, now(i) // seqs)),
        pl.BlockSpec((1, 8, length), lambda i: (now(i), 0, 0)),
        tokens,
        tokens,
        late,
        whole(rest.shape),
    ] + [whole(w.shape) for w in w_groups]
    scratch = [
        pltpu.VMEM((width, count), BF16),
        pltpu.VMEM((GROUPS, count, width), BF16),
        pltpu.VMEM((128, width), F32),
        pltpu.VMEM((length, length), F32),
    ]
    out_shape = [shape((count, width), F32)]
    remotely = {}
    if near:
        in_specs += [pl.BlockSpec(memory_space=pl.ANY)] * 3
        made = [(16, width // 16, width)] * GROUPS + [(16, width // 16, 256)]
        scratch += [pltpu.VMEM(m, BF16) for m in made]
        every_shape = [g.shape for g in given] + made
        out_shape += [shape((s[1] // 2, s[2]), F32) for s in every_shape]
        for s, line_last in zip(every_shape, SCATTER_LINE_LAST):
            scratch += scatter_buffers(s[1], s[2], line_last)
        remotely = dict(collective_id=1, has_side_effects=True)
    else:
        out_shape += [shape((width, width), BF16)] * GROUPS + [shape((width, 256), BF16)]
    return pl.pallas_call(
        partial(backward_kernel, near),
        name="attention_backward",
        grid=(steps + seqs,),
        in_specs=in_specs,
        out_specs=[late] + [whole(s.shape) for s in out_shape[1:]],
        out_shape=out_shape,
        scratch_shapes=scratch,
        compiler_params=pltpu.CompilerParams(vmem_limit_bytes=VMEM_BYTES, **remotely),
    )(scale, rows, qkv, datt, lse, segments, pads, grad_sum, rest, *w_groups, *given)


def join_groups(parts, width):
    part = width // GROUPS
    cut = [p[:, third * part : (third + 1) * part] for third in range(3) for p in parts]
    return jnp.concatenate(cut, 1)


def finish_kernel(wd_ref, win_ref, wo_ref, *refs):
    parts, small_ref, outs = refs[:GROUPS], refs[GROUPS], refs[GROUPS + 1 :]
    qkv_ref, o_wd, o_win, o_wo = outs[:4]
    width = parts[0].shape[1]
    part = width // GROUPS
    for third in range(3):
        for group in range(GROUPS):
            cols = slice(third * width + group * part, third * width + (group + 1) * part)
            qkv_ref[:, cols] = parts[group][:, third * part : (third + 1) * part]
    o_wd[...] = wd_ref[...]
    o_win[...] = win_ref[...]
    o_wo[...] = wo_ref[...]
    mine = small_ref.shape[0]
    square = jnp.concatenate([small_ref[:, :128], jnp.zeros((128 - mine, 128), F32)], 0)
    vectors = jnp.transpose(square)
    for row in range(BIN):
        outs[4 + row][...] = vectors[row : row + 1, :mine]
    outs[4 + BIN][...] = vectors[BIN:VECTORS, :mine]


def finish(sums):
    wd, win, wo, *rest = sums
    mine, width = rest[0].shape
    shape = jax.ShapeDtypeStruct
    vmem = pl.BlockSpec(memory_space=pltpu.VMEM)
    outs = pl.pallas_call(
        finish_kernel,
        name="finish",
        in_specs=[vmem] * 7,
        out_specs=[vmem] * (5 + BIN),
        out_shape=[shape((mine, 3 * width), F32)]
        + [shape(a.shape, F32) for a in (wd, win, wo)]
        + [shape((1, mine), F32)] * BIN
        + [shape((VECTORS - BIN, mine), F32)],
    )(*sums)
    return outs[0], outs[1:4], [v.reshape(-1) for v in outs[4:]]


def body(
    hidden_in, out_grad, segment_ids, pad_mask, task_weight, w_qkv, b_query, b_value, w_out, b_out,
    gain_one, shift_one, w_in, b_in, w_down, b_down, gain_two, shift_two,
):
    seqs, length, width = hidden_in.shape
    mine = w_qkv.shape[0]
    part = width // GROUPS
    near = lax.axis_size("task") == 4 and lax.axis_size("batch") == 8 and mine % 8 == 0
    packed = jnp.concatenate([b_query, b_value, b_out, gain_one, shift_one, b_down, gain_two, shift_two, b_in])
    packed = packed.reshape(VECTORS, mine)
    rows = hidden_in.reshape(-1, width)
    segments = segment_ids.reshape(seqs, 1, length)
    pads = pad_mask.reshape(seqs, 1, length)
    if near:
        weights = [jnp.pad(packed, ((0, 16 - VECTORS), (0, 128 - mine))), w_qkv, w_out, w_in, w_down]
        qkv, att, lse, vectors, _, *full = attention_forward(True, rows, segments, pads, weights)
    else:
        packed = jnp.pad(jnp.transpose(packed), ((0, 0), (0, 256 - VECTORS)))
        cut = w_qkv.reshape(mine, 3, GROUPS, part)
        groups = [cut[:, :, g].reshape(mine, width) for g in range(GROUPS)]
        full = [lax.all_gather(w, AXES, axis=0, tiled=True) for w in (packed, *groups, w_out, w_in, w_down)]
        qkv, att, lse, vectors = attention_forward(False, rows, segments, pads, full[:4])
        full = full[1:]
    *w_groups, wo_full, win_full, wd_full = full
    bin_full = jnp.swapaxes(vectors[BIN:VECTORS].reshape(VECTORS - BIN, -1, mine), 0, 1).reshape(1, -1)
    hidden_out, grad_sum, datt, g_wo, g_win, g_wd, g_vec, g_bin = middle(
        task_weight, rows, att, out_grad.reshape(-1, width), wo_full, win_full, wd_full, vectors, bin_full
    )
    g_bin = jnp.swapaxes(g_bin.reshape(-1, VECTORS - BIN, mine), 0, 1).reshape(VECTORS - BIN, -1)
    g_rest = jnp.concatenate([g_vec[:BIN], g_bin, g_vec[VECTORS:]], 0)
    given = [g.reshape(16, -1, g.shape[1]) for g in (g_wd, g_win, g_wo)] if near else []
    grad_x, *terms = attention_backward(
        near, task_weight, rows, qkv, datt, lse, segments, pads, grad_sum, g_rest, w_groups, given
    )
    if near:
        s_qkv, (s_wd, s_win, s_wo), s_vec = finish(terms)
    else:
        s_wd, s_win, s_wo, *parts, small = [
            lax.psum_scatter(t, AXES, scatter_dimension=0, tiled=True).astype(F32) for t in (g_wd, g_win, g_wo, *terms)
        ]
        s_qkv = join_groups(parts, width)
        s_vec = [small[:, row] for row in range(BIN)] + [jnp.transpose(small[:, BIN:VECTORS]).reshape(-1)]
    return (
        hidden_out.reshape(hidden_in.shape),
        grad_x.reshape(hidden_in.shape),
        s_qkv,
        s_vec[BQ],
        s_vec[BV],
        s_wo,
        s_vec[BO],
        s_vec[G1],
        s_vec[S1],
        s_win,
        s_vec[BIN],
        s_wd,
        s_vec[BD],
        s_vec[G2],
        s_vec[S2],
    )


def solution(mesh):
    seq, mat, vec = P(AXES, None, None), P(AXES, None), P(AXES)
    weights = (mat, vec, vec, mat, vec, vec, vec, mat, vec, mat, vec, vec, vec)
    return jax.shard_map(
        body,
        mesh=mesh,
        in_specs=(seq, seq, mat, mat, P("task")) + weights,
        out_specs=(seq, seq) + weights,
        check_vma=False,
    )
```

```python
from functools import partial

import jax
import jax.numpy as jnp
from jax import lax
from jax.experimental import pallas as pl
from jax.experimental.pallas import tpu as pltpu
from jax.sharding import PartitionSpec as P

HEADS = 12
GROUPS = 3
SEQS = 4
AXES = ("task", "batch")
F32 = jnp.float32
BF16 = jnp.bfloat16
VMEM_BYTES = 66_900_000
BQ, BV, BO, G1, S1, BD, G2, S2, BIN = range(9)
VECTORS = 12

GATHER_TABLE = [
    (0, 0, 0), (0, 1, 0), (0, 2, 0), (0, 0, 1), (0, 1, 1), (0, 2, 1), (0, 3, 0), (0, 0, 3), (0, 0, 4), (0, 0, 5),
    (0, 3, 1), (0, 0, 2), (0, 1, 2), (0, 1, 3), (0, 1, 4), (0, 1, 5), (0, 0, 9), (0, 0, 10), (0, 0, 11), (0, 0, 12),
    (0, 2, 2), (0, 2, 3), (0, 2, 4), (0, 2, 5), (0, 6, 0), (0, 0, 6), (0, 0, 7), (0, 0, 8), (0, 3, 2), (0, 3, 3),
    (0, 3, 4), (0, 3, 5), (0, 1, 6), (0, 0, 17), (0, 0, 18), (0, 1, 7), (0, 1, 8), (0, 1, 9), (0, 1, 10), (0, 1, 11),
    (0, 1, 12), (0, 6, 1), (0, 0, 19), (0, 0, 20), (0, 2, 6), (0, 2, 7), (0, 2, 8), (0, 2, 9), (0, 2, 10), (0, 4, 0),
    (0, 0, 13), (0, 0, 14), (0, 0, 15), (0, 0, 16), (0, 2, 11), (0, 2, 12), (0, 3, 6), (0, 3, 9), (0, 1, 13),
    (0, 3, 7), (0, 3, 8), (0, 3, 10), (0, 3, 11), (0, 3, 12), (0, 4, 1), (0, 1, 14), (0, 1, 15), (0, 1, 16),
    (0, 1, 17), (0, 1, 18), (0, 5, 0), (0, 1, 19), (0, 1, 20), (0, 0, 25), (0, 0, 26), (0, 5, 1), (0, 0, 21),
    (0, 0, 22), (0, 2, 13), (0, 2, 14), (0, 6, 2), (0, 6, 3), (0, 6, 4), (0, 6, 5), (0, 0, 23), (0, 2, 15),
    (0, 2, 16), (0, 2, 17), (0, 2, 18), (0, 0, 24), (0, 1, 25), (0, 3, 13), (0, 3, 14), (0, 1, 26), (0, 1, 21),
    (0, 1, 22), (0, 2, 19), (0, 2, 20), (0, 3, 15), (0, 3, 16), (0, 3, 17), (0, 3, 18), (0, 3, 19), (0, 3, 20),
    (0, 4, 4), (0, 4, 5), (0, 1, 23), (0, 4, 2), (0, 4, 3), (0, 1, 24), (0, 0, 27), (0, 6, 8), (0, 6, 10), (0, 5, 2),
    (0, 5, 3), (0, 5, 4), (0, 5, 5), (0, 0, 28), (0, 0, 29), (0, 2, 23), (0, 2, 24), (0, 2, 25), (0, 2, 26),
    (0, 3, 23), (0, 3, 24), (0, 3, 25), (0, 3, 26), (0, 6, 6), (0, 6, 7), (0, 1, 27), (0, 1, 28), (0, 6, 9),
    (0, 6, 11), (0, 4, 6), (0, 4, 7), (0, 1, 29), (1, 2, 21), (1, 2, 22), (1, 2, 28), (1, 3, 21), (1, 3, 22),
    (1, 6, 14), (1, 4, 8), (1, 4, 10), (1, 4, 14), (1, 5, 7), (1, 5, 8), (1, 3, 28), (2, 2, 27), (2, 3, 27),
    (2, 6, 21), (2, 4, 9), (2, 4, 11), (2, 5, 6), (2, 5, 11), (2, 5, 12), (3, 2, 29), (3, 3, 29), (3, 6, 12),
    (3, 6, 13), (3, 4, 12), (3, 4, 13), (3, 5, 9), (3, 5, 10), (4, 6, 15), (4, 6, 16), (4, 6, 17), (4, 6, 18),
    (4, 5, 15), (4, 5, 16), (4, 5, 19), (4, 5, 20), (5, 6, 19), (5, 6, 20), (5, 6, 22), (5, 6, 23), (5, 6, 24),
    (5, 4, 15), (5, 4, 16), (5, 4, 17), (5, 4, 18), (5, 4, 19), (5, 4, 20), (5, 4, 21), (5, 4, 23), (5, 4, 24),
    (6, 4, 22), (6, 5, 13), (6, 5, 14), (6, 5, 23), (6, 5, 24), (7, 6, 25), (7, 6, 26), (7, 6, 27), (7, 6, 28),
    (7, 4, 27), (7, 4, 28), (7, 5, 17), (7, 5, 18), (7, 5, 21), (7, 5, 22), (7, 5, 25), (7, 5, 26), (8, 6, 29),
    (8, 4, 25), (8, 4, 26), (8, 5, 27), (8, 5, 28), (9, 4, 29), (9, 5, 29),
]
SCATTER_TABLE = [
    (0, 0, 0), (0, 1, 0), (1, 0, 1), (1, 0, 2), (2, 0, 3), (2, 0, 4), (2, 0, 5), (2, 1, 1), (2, 2, 0), (3, 0, 6),
    (3, 0, 7), (3, 1, 2), (3, 1, 3), (3, 1, 4), (3, 2, 1), (3, 2, 2), (3, 2, 3), (3, 2, 4), (4, 3, 0), (4, 0, 8),
    (4, 0, 9), (4, 0, 10), (4, 0, 11), (4, 0, 12), (5, 3, 1), (5, 3, 2), (5, 3, 3), (5, 3, 4), (5, 0, 13), (5, 0, 14),
    (5, 1, 5), (6, 1, 6), (6, 1, 7), (6, 1, 8), (7, 0, 15), (7, 0, 16), (7, 0, 17), (7, 0, 18), (7, 0, 20), (8, 4, 0),
    (8, 0, 21), (8, 1, 9), (8, 1, 10), (8, 1, 11), (8, 1, 12), (8, 2, 5), (8, 2, 6), (8, 2, 7), (8, 2, 8), (8, 2, 9),
    (9, 4, 1), (9, 4, 2), (9, 4, 3), (9, 4, 4), (9, 3, 5), (9, 3, 6), (9, 3, 7), (9, 3, 8), (9, 0, 19), (9, 0, 22),
    (9, 0, 23), (9, 2, 10), (9, 2, 11), (9, 2, 12), (9, 3, 9), (9, 0, 24), (10, 3, 10), (10, 3, 11), (10, 3, 12),
    (10, 1, 13), (10, 1, 14), (11, 0, 25), (11, 0, 26), (11, 1, 15), (11, 1, 16), (11, 1, 17), (11, 1, 18),
    (11, 1, 19), (11, 2, 13), (11, 2, 14), (12, 5, 0), (12, 6, 0), (12, 4, 5), (12, 4, 6), (12, 4, 7), (12, 4, 8),
    (12, 4, 9), (12, 4, 10), (12, 4, 11), (12, 4, 12), (12, 3, 13), (12, 3, 14), (12, 3, 15), (12, 3, 16),
    (12, 3, 17), (12, 3, 18), (12, 3, 19), (12, 0, 27), (12, 1, 20), (12, 1, 21), (12, 1, 22), (12, 2, 15),
    (12, 2, 16), (12, 2, 17), (12, 2, 18), (12, 2, 19), (12, 2, 20), (13, 5, 1), (13, 5, 2), (13, 5, 3), (13, 5, 4),
    (13, 6, 1), (13, 6, 2), (13, 6, 3), (13, 6, 4), (13, 4, 13), (13, 4, 14), (13, 4, 15), (13, 4, 16), (13, 4, 17),
    (13, 4, 18), (13, 4, 19), (13, 3, 20), (13, 3, 21), (14, 5, 5), (14, 5, 6), (14, 5, 7), (14, 4, 20), (14, 3, 22),
    (14, 1, 23), (14, 2, 21), (14, 2, 22), (14, 5, 8), (15, 5, 9), (15, 5, 10), (15, 5, 11), (15, 5, 12), (15, 6, 5),
    (15, 6, 6), (15, 6, 7), (15, 6, 8), (15, 6, 9), (15, 6, 10), (15, 6, 11), (15, 6, 15), (15, 6, 16), (15, 6, 17),
    (15, 6, 18), (15, 6, 19), (15, 6, 20), (15, 6, 21), (15, 4, 21), (15, 4, 22), (15, 3, 23), (15, 3, 24),
    (15, 1, 24), (15, 2, 23), (15, 5, 13), (15, 5, 14), (15, 5, 15), (15, 5, 16), (16, 5, 17), (16, 5, 18),
    (16, 5, 19), (16, 6, 12), (16, 6, 13), (16, 6, 14), (16, 6, 22), (16, 6, 23), (16, 6, 24), (16, 4, 23),
    (16, 4, 24), (16, 3, 25), (16, 3, 26), (16, 1, 25), (16, 1, 26), (16, 2, 24), (16, 2, 25), (16, 2, 26),
    (16, 5, 20), (16, 5, 21), (16, 3, 27), (16, 6, 25), (16, 1, 27), (16, 2, 27), (16, 6, 26), (16, 5, 22),
    (16, 6, 29), (16, 6, 30), (16, 4, 25), (16, 4, 26), (16, 5, 23), (16, 6, 27), (16, 6, 28), (16, 4, 27),
    (16, 5, 24), (16, 6, 31), (16, 6, 32), (16, 5, 25), (16, 5, 26), (16, 6, 33), (16, 5, 27),
]
GATHER_LINE_FIRST = [False, False, False, False, True, False, True]
SCATTER_LINE_LAST = [True, True, True, True, True, True, False]
GATHER_SLOTS, SCATTER_SLOTS = 1, 1


MESH = pl.DeviceIdType.MESH


class Place:
    def __init__(self):
        self.task = lax.axis_index("task")
        self.batch = lax.axis_index("batch")
        self.core = self.batch % 2
        self.z = self.batch // 2
        x, y = self.task % 2, self.task // 2
        flip_x, flip_y = self.task + 1 - 2 * x, self.task + 2 - 4 * y
        self.task_a = (1 - self.core) * flip_x + self.core * flip_y
        self.task_b = (1 - self.core) * flip_y + self.core * flip_x
        self.task_ab = 3 - self.task
        self.partner = (self.task, self.batch + 1 - 2 * self.core)
        self.peer_a = (self.task_a, self.batch)
        self.peer_b = (self.task_b, self.batch)
        self.above = (self.task, self.batch + 2)
        self.below = (self.task, self.batch - 2)
        self.low = 1 - self.z // 2
        self.inner = self.low * self.z + (1 - self.low) * (3 - self.z)
        self.far = (self.task, self.batch + 4 * self.low - 2)
        self.near = (self.task, self.batch + 2 - 4 * self.low)

    def meet(self):
        barrier = pltpu.get_barrier_semaphore()
        for peer in (self.partner, self.peer_a, self.peer_b):
            pl.semaphore_signal(barrier, inc=1, device_id=peer, device_id_type=MESH)

        @pl.when(self.z < 3)
        def _():
            pl.semaphore_signal(barrier, inc=1, device_id=self.above, device_id_type=MESH)

        @pl.when(self.z > 0)
        def _():
            pl.semaphore_signal(barrier, inc=1, device_id=self.below, device_id_type=MESH)

        pl.semaphore_wait(barrier, 4 + self.z * (3 - self.z) // 2)


def remote(src, dst, send, recv, peer):
    return pltpu.make_async_remote_copy(src, dst, send, recv, device_id=peer, device_id_type=MESH)


GATHER_SEMS = [
    pltpu.SemaphoreType.DMA((12,)),
    pltpu.SemaphoreType.DMA((7,)),
    pltpu.SemaphoreType.DMA((14,)),
    pltpu.SemaphoreType.DMA((14,)),
    pltpu.SemaphoreType.DMA((6,)),
]


class Gather:
    def __init__(self, place, windows, full, sems, line_first=False):
        self.place, self.windows, self.full, self.line_first = place, windows, full, line_first
        self.send_z, self.send_a, self.recv, self.recv_b, self.misc = sems
        self.half = full.shape[1] // 2
        self.r = full.shape[0] // 32

    def rows(self, task, batch, count):
        return pl.ds(pl.multiple_of((task * 8 + batch) * self.r, 8), count * self.r)

    def cols(self, core):
        return pl.ds(pl.multiple_of(core * self.half, 128), self.half)

    def task(self, which):
        return self.place.task if which == 0 else self.place.task_a

    def level(self, spot):
        return self.place.z - spot if spot < 4 else self.place.z + spot - 3

    def here(self, spot):
        return self.place.z >= spot if spot < 4 else self.place.z + spot <= 6

    def chunk(self, task, spot):
        return self.full.at[self.rows(task, 2 * self.level(spot), 2), self.cols(self.place.core)]

    def begin(self):
        place, at = self.place, 0
        for window in self.windows:
            into = self.full.at[self.rows(place.task, place.batch, 1), pl.ds(at, window.shape[1])]
            pltpu.make_async_copy(window, into, self.misc.at[0]).start()
            remote(window, into, self.misc.at[1], self.misc.at[2], place.partner).start()
            at += window.shape[1]

    def along_z(self, which, spot, up):
        step = spot if up else max(spot - 3, 0)
        slot = which * 6 + step + (0 if up else 3)
        chunk = self.chunk(self.task(which), spot)
        into = which * 7 + step + (1 if up else 4)
        return remote(chunk, chunk, self.send_z.at[slot], self.recv.at[into], self.place.above if up else self.place.below)

    def along_a(self, spot):
        chunk = self.chunk(self.place.task, spot)
        return remote(chunk, chunk, self.send_a.at[spot], self.recv.at[7 + spot], self.place.peer_a)

    def along_b(self, which, spot):
        chunk = self.chunk(self.task(which), spot)
        return remote(chunk, chunk, self.misc.at[3], self.recv_b.at[which * 7 + spot], self.place.peer_b)

    def hand_over(self, task, spot):
        chunk = self.chunk(task, spot)
        remote(chunk, chunk, self.misc.at[4], self.misc.at[5], self.place.partner).start()

    def arrived(self, task, spot, sem):
        chunk = self.chunk(task, spot)
        remote(chunk, chunk, self.misc.at[1], sem, self.place.partner).wait_recv()

    def onward(self, which, spot):
        place = self.place
        if which == 0 or not self.line_first:
            for up in (True, False):
                if spot == 0 or (spot < 3 if up else 3 < spot < 6):
                    more = place.z < 3 if up else place.z > 0

                    @pl.when(more)
                    def _():
                        self.along_z(which, spot, up).start()

        if which == 0 and (spot == 0 or self.line_first):
            self.along_a(spot).start()
        self.along_b(which, spot).start()
        if which or spot:
            self.hand_over(self.task(which), spot)

    def spread(self):
        place = self.place
        mine = self.full.at[self.rows(place.task, place.batch, 1), :]
        pltpu.make_async_copy(mine, mine, self.misc.at[0]).wait()
        other = self.full.at[self.rows(place.task, place.partner[1], 1), :]
        remote(other, other, self.misc.at[1], self.misc.at[2], place.partner).wait_recv()
        self.onward(0, 0)

    def line(self, which, spot):
        @pl.when(self.here(spot))
        def _():
            self.arrived(self.task(which), spot, self.recv.at[which * 7 + spot])
            self.onward(which, spot)

    def from_b(self, which, spot):
        task = self.place.task_b if which == 0 else self.place.task_ab

        @pl.when(self.here(spot))
        def _():
            self.arrived(task, spot, self.recv_b.at[which * 7 + spot])
            self.hand_over(task, spot)

    def finish(self):
        place, full, r = self.place, self.full, self.r
        rest = full.at[pl.ds(0, 30 * r), self.cols(1 - place.core)]
        remote(rest, rest, self.misc.at[4], self.misc.at[5], place.partner).wait_recv()
        mine = full.at[pl.ds(0, 30 * r), self.cols(place.core)]
        remote(mine, mine, self.misc.at[4], self.misc.at[5], place.partner).wait_send()
        eight = full.at[pl.ds(0, 16 * r), self.cols(place.core)]
        remote(eight, eight, self.misc.at[3], self.recv_b.at[0], place.peer_b).wait_send()
        own = full.at[self.rows(place.task, place.batch, 1), :]
        remote(own, own, self.misc.at[1], self.misc.at[2], place.partner).wait_send()
        for spot in range(7 if self.line_first else 1):

            @pl.when(self.here(spot))
            def _():
                self.along_a(spot).wait_send()

        for which in range(1 if self.line_first else 2):
            for spot in (0, 1, 2):

                @pl.when(self.here(spot) & (place.z < 3))
                def _():
                    self.along_z(which, spot, True).wait_send()

            for spot in (0, 4, 5):

                @pl.when(self.here(spot) & (place.z > 0))
                def _():
                    self.along_z(which, spot, False).wait_send()

    def events(self):
        line, b = self.line, self.from_b
        out = [self.begin, self.spread]
        if self.line_first:
            out += [partial(line, 0, 1), partial(line, 0, 4), partial(line, 1, 0), partial(b, 0, 0)]
            out += [partial(line, 0, 2), partial(line, 0, 5), partial(line, 1, 1), partial(line, 1, 4)]
            out += [partial(b, 0, 1), partial(b, 0, 4), partial(line, 0, 3), partial(line, 0, 6), partial(b, 1, 0)]
            out += [partial(line, 1, 2), partial(line, 1, 5), partial(b, 0, 2), partial(b, 0, 5)]
            out += [partial(line, 1, 3), partial(line, 1, 6), partial(b, 1, 1), partial(b, 1, 4)]
            out += [partial(b, w, s) for w, s in ((0, 3), (0, 6), (1, 2), (1, 5), (1, 3), (1, 6))]
        else:
            out += [partial(line, 1, 0), partial(line, 0, 1), partial(line, 0, 4), partial(b, 0, 0), partial(b, 1, 0)]
            out += [partial(line, 1, 1), partial(line, 1, 4), partial(b, 0, 1), partial(b, 0, 4)]
            out += [partial(line, 0, 2), partial(line, 0, 5), partial(b, 1, 1), partial(b, 1, 4)]
            out += [partial(line, 1, 2), partial(line, 1, 5), partial(b, 0, 2), partial(b, 0, 5)]
            out += [partial(line, 0, 3), partial(line, 0, 6), partial(b, 1, 2), partial(b, 1, 5)]
            out += [partial(line, 1, 3), partial(line, 1, 6), partial(b, 0, 3), partial(b, 0, 6)]
            out += [partial(b, 1, 3), partial(b, 1, 6)]
        return out + [self.finish]


SCATTER_SEMS = [
    pltpu.SemaphoreType.DMA((4,)),
    pltpu.SemaphoreType.DMA((4,)),
    pltpu.SemaphoreType.DMA((4,)),
    pltpu.SemaphoreType.DMA((8,)),
    pltpu.SemaphoreType.DMA((8,)),
    pltpu.SemaphoreType.DMA((8,)),
    pltpu.SemaphoreType.DMA((10,)),
    pltpu.SemaphoreType.DMA((4,)),
    pltpu.SemaphoreType.DMA((4,)),
    pltpu.SemaphoreType.DMA((2,)),
]


def scatter_buffers(rows, cols, line_last=False):
    half = cols // 2
    return [
        pltpu.VMEM((16, rows, half), BF16),
        pltpu.VMEM((16, rows, half), BF16),
        pltpu.VMEM((8, rows, half), BF16),
        pltpu.VMEM((5 if line_last else 10, rows, half), BF16),
        pltpu.VMEM((4 if line_last else 1, rows, half), BF16),
        pltpu.VMEM((rows, half), F32),
        pltpu.VMEM((rows // 2, half), F32),
    ] + SCATTER_SEMS


class Scatter:
    def __init__(self, place, terms, out, buffers, line_last=False):
        self.place, self.terms, self.out, self.line_last = place, terms, out, line_last
        (self.own, self.other, self.got_b, self.got_z, self.got_a, self.total, self.got_f) = buffers[:7]
        (
            self.s_load, self.s_pair, self.r_pair, self.s_b, self.r_b, self.s_z, self.r_z, self.s_a, self.r_a, self.misc
        ) = buffers[7:]
        self.half = self.own.shape[2]
        self.tasks = (place.task_ab, place.task_b, place.task_a, place.task)
        self.tasks_partner = (place.task_ab, place.task_a, place.task_b, place.task)

    def cols(self, core):
        return pl.ds(pl.multiple_of(core * self.half, 128), self.half)

    def level(self, m):
        return self.place.low * m + (1 - self.place.low) * (3 - m)

    def load(self, index):
        first = self.tasks[index] * 4
        return pltpu.make_async_copy(
            self.terms.at[pl.ds(first, 4), :, self.cols(self.place.core)],
            self.own.at[pl.ds(first, 4)],
            self.s_load.at[index],
        )

    def pair(self, index, sent=True):
        first = (self.tasks_partner if sent else self.tasks)[index] * 4
        return remote(
            self.terms.at[pl.ds(first, 4), :, self.cols(1 - self.place.core)],
            self.other.at[pl.ds(first, 4)],
            self.s_pair.at[index],
            self.r_pair.at[index],
            self.place.partner,
        )

    def begin(self):
        for index in range(4):
            self.load(index).start()
            self.pair(index).start()

    def add(self, at, ref, where):
        size = 48 if self.half <= 512 else 16

        def some(index, carry):
            rows = pl.ds(pl.multiple_of(index * size, size), size)
            self.own[at, rows] = self.own[at, rows] + ref[where, rows]
            return carry

        lax.fori_loop(0, self.own.shape[1] // size, some, 0)

    def along_b(self, which, z):
        slot = which * 4 + z
        return remote(
            self.own.at[self.tasks[which] * 4 + z], self.got_b.at[slot], self.s_b.at[slot], self.r_b.at[slot],
            self.place.peer_b,
        )

    def add_pair(self, index):
        self.load(index).wait()
        self.pair(index, False).wait_recv()
        first = self.tasks[index] * 4

        def chunk(count, carry):
            z = self.level(3 - count)
            self.add(first + z, self.other, first + z)
            if index < 2:
                self.along_b(index, z).start()
            return carry

        lax.fori_loop(0, 4, chunk, 0)

    def add_b(self, which, m):
        z = self.level(m)
        self.along_b(which, z).wait_recv()
        self.add(self.tasks[2 + which] * 4 + z, self.got_b, which * 4 + z)
        if which == 0 and self.line_last:
            self.along_a(z).start()

    def along_z(self, which, m, far):
        place = self.place
        at = self.tasks[2 + which] * 4 + self.level(m)
        line = 0 if self.line_last else 5 * which
        into = line + ((1 - place.inner) * (m - 1) + place.inner * (6 - m) if far else 3 + m)
        peer = place.far if far else place.near
        return remote(self.own.at[at], self.got_z.at[into], self.s_z.at[which * 4 + m], self.r_z.at[into], peer)

    def add_z(self, which, m, slot):
        into = slot + (0 if self.line_last else 5 * which)
        got = self.got_z.at[into]
        remote(got, got, self.s_z.at[0], self.r_z.at[into], self.place.partner).wait_recv()
        self.add(self.tasks[2 + which] * 4 + self.level(m), self.got_z, into)

    def far_out(self, which, m):
        @pl.when(self.place.inner == 0)
        def _():
            self.along_z(which, m, True).start()

    def far_on(self, which, m):
        @pl.when(self.place.inner == 1)
        def _():
            self.add_z(which, m, m - 1)
            if m > 1:
                self.along_z(which, m, True).start()

    def near_on(self, which, m):
        @pl.when(self.place.inner == 1)
        def _():
            self.add_z(which, m, 3 + m)
            if m == 0:
                self.along_z(which, m, False).start()

    def near_in(self, which):
        @pl.when(self.place.inner == 0)
        def _():
            self.add_z(which, 0, 3)

    def along_a(self, z):
        slot = z if self.line_last else 0
        return remote(
            self.own.at[self.tasks[2] * 4 + z], self.got_a.at[slot], self.s_a.at[slot], self.r_a.at[slot],
            self.place.peer_a,
        )

    def to_a(self):
        self.along_a(self.place.z).start()

    def add_a(self, m):
        z = self.level(m)
        self.along_a(z).wait_recv()
        self.add(self.tasks[3] * 4 + z, self.got_a, z)

    def last(self):
        rows = self.got_f.shape[0]
        away = pl.multiple_of((1 - self.place.core) * rows, rows)
        return remote(
            self.total.at[pl.ds(away, rows)], self.got_f, self.misc.at[0], self.misc.at[1], self.place.partner
        )

    def close(self):
        total = self.own[self.tasks[3] * 4 + self.place.z].astype(F32)
        if not self.line_last:
            self.along_a(self.place.z).wait_recv()
            total = total + self.got_a[0].astype(F32)
        self.total[...] = total
        self.last().start()

    def finish(self):
        rows = self.got_f.shape[0]
        core = self.place.core
        self.last().wait_recv()
        self.out[:, self.cols(core)] = self.total[pl.ds(pl.multiple_of(core * rows, rows), rows), :]
        self.out[:, self.cols(1 - core)] = self.got_f[...]
        for index in range(4):
            self.pair(index).wait_send()
        for which in range(2):
            for z in range(4):
                self.along_b(which, z).wait_send()
        for which in range(1 if self.line_last else 0, 2):
            for m in range(4):

                @pl.when(self.place.inner < m)
                def _():
                    self.along_z(which, m, True).wait_send()

                @pl.when(self.place.inner > m)
                def _():
                    self.along_z(which, m, False).wait_send()

        for z in range(4 if self.line_last else 1):
            self.along_a(z if self.line_last else self.place.z).wait_send()
        self.last().wait_send()

    def events(self):
        out = [self.begin] + [partial(self.add_pair, i) for i in range(4)]
        if self.line_last:
            out += [partial(self.add_b, which, m) for which in range(2) for m in (3, 2, 1, 0)]
            for m in (3, 2, 1):
                out += [partial(self.add_a, m), partial(self.far_out, 1, m)]
            out.append(partial(self.add_a, 0))
            out += [partial(self.far_on, 1, m) for m in (3, 2, 1)]
            out += [partial(self.near_on, 1, 0), partial(self.near_on, 1, 1), partial(self.near_in, 1)]
        else:
            for which in range(2):
                for m in (3, 2, 1):
                    out += [partial(self.add_b, which, m), partial(self.far_out, which, m)]
                out.append(partial(self.add_b, which, 0))
                out += [partial(self.far_on, which, m) for m in (3, 2, 1)]
            for which in range(2):
                out += [partial(self.near_on, which, 0), partial(self.near_on, which, 1), partial(self.near_in, which)]
                if which == 0:
                    out.append(self.to_a)
        return out + [self.close, self.finish]


def dot(left, right):
    return lax.dot_general(left, right, (((1,), (0,)), ((), ())), preferred_element_type=F32)


def dot_right(left, right):
    return lax.dot_general(left, right, (((1,), (1,)), ((), ())), preferred_element_type=F32)


def at_slot(slot, plan):
    def choose(slots):
        if len(slots) == 1:

            @pl.when(slot == slots[0])
            def _():
                for event in plan[slots[0]]:
                    event()

            return
        middle_slot = slots[len(slots) // 2]

        @pl.when(slot < middle_slot)
        def _():
            choose(slots[: len(slots) // 2])

        @pl.when(slot >= middle_slot)
        def _():
            choose(slots[len(slots) // 2 :])

    if plan:
        choose(sorted(plan))


def fill_mask(seg_ref, pad_ref, row, mask_ref):
    length = mask_ref.shape[0]
    seg_row = seg_ref[pl.ds(row, 1), :].astype(F32)
    pad_row = pad_ref[pl.ds(row, 1), :].astype(F32)
    seg_col = jnp.transpose(jnp.broadcast_to(seg_row, (128, length)))
    pad_col = jnp.transpose(jnp.broadcast_to(pad_row, (128, length)))
    key_at = lax.broadcasted_iota(jnp.int32, (length, 128), 0)
    lane = lax.broadcasted_iota(jnp.int32, (length, 128), 1)
    for block in range(length // 128):
        same = seg_col == seg_row[:, 128 * block : 128 * block + 128]
        seen = (pad_col == 1.0) | (key_at == lane + 128 * block)
        mask_ref[:, 128 * block : 128 * block + 128] = jnp.where(same & seen, 0.0, -1e30)


def planned(table, jobs):
    plan = {}
    events = [job.events() for job in jobs]
    for slot, job, event in table:
        plan.setdefault(slot, []).append(events[job][event])
    return plan


def run_now(plan, slot):
    for event in plan.get(slot, []):
        event()


def forward_kernel(near, devices, x_ref, seg_ref, pad_ref, *refs):
    if near:
        vector_refs, refs = refs[: BIN + 1], refs[BIN + 1 :]
        wqkv_ref, wo_ref, win_ref, wd_ref = refs[:4]
        qkv_ref, att_ref, lse_ref, vec_ref, bin_ref = refs[4:9]
        fulls = refs[9:16]
        mask_ref, w_ref, small_ref, load_sem, shard_ref, square_ref = refs[16:22]
        sems = refs[22:]
    else:
        fulls = refs[:4]
        qkv_ref, att_ref, lse_ref, vec_ref, bin_ref = refs[4:9]
        mask_ref, w_ref, small_ref, load_sem = refs[9:]
    step = pl.program_id(0)
    length, width = x_ref.shape
    part = width // GROUPS
    half = width // HEADS
    steps = GROUPS * SEQS
    per = GATHER_SLOTS
    last = per * steps
    plan = {}
    if near:
        place = Place()
        windows = [[shard_ref]]
        for group in range(GROUPS):
            windows.append([wqkv_ref.at[:, pl.ds(third * width + group * part, part)] for third in range(3)])
        windows += [[wo_ref], [win_ref], [wd_ref]]
        jobs = [
            Gather(place, windows[i], fulls[i], sems[5 * i : 5 * i + 5], GATHER_LINE_FIRST[i]) for i in range(7)
        ]
        plan = planned(GATHER_TABLE, jobs)

    @pl.when(step == 0)
    def _():
        if near:
            mine = shard_ref.shape[0]
            square_ref[...] = jnp.zeros_like(square_ref)
            for row, ref in enumerate(vector_refs):
                vector = ref[...].astype(F32).reshape(1, ref.shape[0])
                for j in range(ref.shape[0] // mine):
                    square_ref[row + j : row + j + 1, :mine] = vector[:, j * mine : (j + 1) * mine]
            shard_ref[:, :128] = jnp.transpose(square_ref[...])[:mine].astype(BF16)
            shard_ref[:, 128:] = jnp.zeros((shard_ref.shape[0], 128), BF16)
            place.meet()
            run_now(plan, 0)
        copy = pltpu.make_async_copy(fulls[0].at[:, pl.ds(0, 128)], small_ref, load_sem.at[0])
        copy.start()
        copy.wait()
        vec_ref[...] = jnp.transpose(small_ref[...].astype(F32))[:16]
        mine = small_ref.shape[0] // devices
        for d in range(devices):
            for j in range(VECTORS - BIN):
                start = (d * (VECTORS - BIN) + j) * mine
                bin_ref[:, start : start + mine] = vec_ref[BIN + j : BIN + j + 1, d * mine : (d + 1) * mine]

    if near:
        at_slot(per * step, {s: e for s, e in plan.items() if s % per == 0 and 0 < s < last})
    for group in range(GROUPS):

        @pl.when(step == group * SEQS)
        def _():
            copy = pltpu.make_async_copy(fulls[1 + group], w_ref, load_sem.at[1])
            copy.start()
            copy.wait()

    fill_mask(seg_ref, pad_ref, step % SEQS, mask_ref)
    at = pl.multiple_of(step // SEQS * part, part)
    for third, row in enumerate((BQ, None, BV)):
        cols = slice(third * part, (third + 1) * part)
        product = dot(x_ref[...], w_ref[:, cols])
        if row is not None:
            product = product + vec_ref[row : row + 1, pl.ds(at, part)]
        qkv_ref[:, cols] = product.astype(BF16)
    first_half = lax.broadcasted_iota(jnp.int32, (1, 2 * half), 1) < half
    pairs = part // (2 * half)

    def attend(pair):
        if near and 0 < pair < per:
            at_slot(per * step + pair, {s: e for s, e in plan.items() if s % per == pair and s < last})
        base = pair * 2 * half
        queries = qkv_ref[:, pl.ds(base, 2 * half)]
        keys = qkv_ref[:, pl.ds(part + base, 2 * half)] * jnp.asarray(0.125, BF16)
        values_t = jnp.transpose(qkv_ref[:, pl.ds(2 * part + base, 2 * half)])
        outs = []
        for head in range(2):
            mine = first_half if head == 0 else ~first_half
            scores = dot_right(jnp.where(mine, keys, jnp.zeros_like(keys)), queries) + mask_ref[...]
            top = jnp.max(scores, 0, keepdims=True)
            expo = jnp.exp(scores - top)
            total = jnp.sum(expo, 0, keepdims=True)
            probs = (expo * (1.0 / total)).astype(BF16)
            outs.append(dot(values_t[head * half : (head + 1) * half], probs))
            lse_ref[0, pl.ds(2 * pair + head, 1), :] = top + jnp.log(total)
        att_ref[:, pl.ds(base, 2 * half)] = jnp.transpose(jnp.concatenate(outs, 0)).astype(BF16)

    for pair in range(pairs):
        attend(pair)
    if near:

        @pl.when(step == steps - 1)
        def _():
            run_now(plan, last)


def attention_forward(near, rows, segments, pads, weights):
    seqs, length = segments.shape
    width = rows.shape[1]
    part = width // GROUPS
    anywhere = lambda count: [pl.BlockSpec(memory_space=pl.ANY)] * count
    tokens = pl.BlockSpec((seqs, length), lambda i: (0, 0))
    shape = jax.ShapeDtypeStruct
    out_specs = [
        pl.BlockSpec((length, width), lambda i: (i % seqs, i // seqs)),
        pl.BlockSpec((length, part), lambda i: (i % seqs, i // seqs)),
        pl.BlockSpec((1, 8, length), lambda i: (i, 0, 0)),
        pl.BlockSpec((16, width), lambda i: (0, 0)),
        pl.BlockSpec((1, (VECTORS - BIN) * width), lambda i: (0, 0)),
    ]
    out_shape = [
        shape((rows.shape[0], 3 * width), BF16),
        shape((rows.shape[0], width), BF16),
        shape((GROUPS * seqs, 8, length), F32),
        shape((16, width), F32),
        shape((1, (VECTORS - BIN) * width), F32),
    ]
    in_specs = [pl.BlockSpec((length, width), lambda i: (i % seqs, 0)), tokens, tokens]
    scratch = [
        pltpu.VMEM((length, length), F32),
        pltpu.VMEM((width, width), BF16),
        pltpu.VMEM((width, 128), BF16),
        pltpu.SemaphoreType.DMA((2,)),
    ]
    remotely = {}
    if near:
        *vectors, w_qkv, w_out, w_in, w_down = weights
        in_specs += [pl.BlockSpec(v.shape, lambda i: (0,)) for v in vectors]
        in_specs += [pl.BlockSpec(w.shape, lambda i: (0, 0)) for w in (w_qkv, w_out, w_in, w_down)]
        mine = w_qkv.shape[0]
        fulls = [(mine, 256)] + [(mine, width)] * GROUPS + [w.shape for w in (w_out, w_in, w_down)]
        out_specs += anywhere(7)
        out_shape += [shape((32 * r, c), BF16) for r, c in fulls]
        scratch += [pltpu.VMEM((mine, 256), BF16), pltpu.VMEM((128, 128), F32)] + GATHER_SEMS * 7
        remotely = dict(collective_id=0, has_side_effects=True)
    else:
        in_specs += anywhere(4)
    return pl.pallas_call(
        partial(forward_kernel, near, lax.axis_size(AXES)),
        name="attention_forward",
        grid=(GROUPS * seqs,),
        in_specs=in_specs,
        out_specs=out_specs,
        out_shape=out_shape,
        scratch_shapes=scratch,
        compiler_params=pltpu.CompilerParams(vmem_limit_bytes=VMEM_BYTES, **remotely),
    )(rows, segments, pads, *weights)


def norm_parts(arr):
    centre = arr - jnp.mean(arr, -1, keepdims=True)
    scale = lax.rsqrt(jnp.mean(centre * centre, -1, keepdims=True) + 1e-12)
    return centre * scale, scale


def norm_back(grad_normal, normal, scale):
    return scale * (
        grad_normal
        - jnp.mean(grad_normal, -1, keepdims=True)
        - normal * jnp.mean(grad_normal * normal, -1, keepdims=True)
    )


def column_sum(arr):
    return jnp.sum(arr.astype(F32), 0, keepdims=True)


def middle_kernel(
    mine, scale_ref, x_ref, att_ref, cot_ref, wo_ref, win_ref, wd_ref, vec_ref, bin_ref,
    out_ref, sum_ref, datt_ref, gwo_ref, gwin_ref, gwd_ref, gvec_ref,
    gbin_ref, acc_wo, acc_win, acc_wd, act_ref, slope_ref,
):
    step = pl.program_id(0)
    width = x_ref.shape[1]
    hidden = win_ref.shape[1]
    chunks = hidden // width

    @pl.when(step == 0)
    def _():
        acc_wo[...] = jnp.zeros_like(acc_wo)
        acc_win[...] = jnp.zeros_like(acc_win)
        acc_wd[...] = jnp.zeros_like(acc_wd)
        gvec_ref[...] = jnp.zeros_like(gvec_ref)
        gbin_ref[...] = jnp.zeros_like(gbin_ref)

    vec = lambda row: vec_ref[row : row + 1, :]
    branch = dot(att_ref[...], wo_ref[...]) + vec(BO)
    normal_one, scale_one = norm_parts(x_ref[...].astype(F32) + branch)
    first = normal_one * vec(G1) + vec(S1)
    first_low = first.astype(BF16)
    second = first + vec(BD)
    for chunk in range(chunks):
        cols = slice(chunk * width, (chunk + 1) * width)
        pre = dot(first_low, win_ref[:, cols]) + bin_ref[:, cols]
        below = 0.5 + 0.5 * lax.erf(pre * 0.7071067811865476)
        act = (pre * below).astype(BF16)
        act_ref[:, cols] = act
        slope_ref[:, cols] = below + pre * (jnp.exp(pre * pre * -0.5) * 0.3989422804014327)
        second = second + dot(act, wd_ref[cols, :])
    normal_two, scale_two = norm_parts(second)
    out_ref[...] = (normal_two * vec(G2) + vec(S2)).astype(BF16)
    cot = cot_ref[...].astype(F32)
    gvec_ref[G2 : G2 + 1, :] += column_sum(cot * normal_two)
    gvec_ref[S2 : S2 + 1, :] += column_sum(cot)
    grad_second = norm_back(cot * vec(G2), normal_two, scale_two)
    grad_low = grad_second.astype(BF16)
    gvec_ref[BD : BD + 1, :] += column_sum(grad_low)
    first_t = jnp.transpose(first_low)
    grad_first = grad_second
    for chunk in range(chunks):
        cols = slice(chunk * width, (chunk + 1) * width)
        grad_pre = (slope_ref[:, cols] * dot_right(grad_low, wd_ref[cols, :])).astype(BF16)
        gbin_ref[:, cols] += column_sum(grad_pre)
        acc_wd[cols, :] += dot(jnp.transpose(act_ref[:, cols]), grad_low)
        acc_win[:, cols] += dot(first_t, grad_pre)
        grad_first = grad_first + dot_right(grad_pre, win_ref[:, cols])
    gvec_ref[G1 : G1 + 1, :] += column_sum(grad_first * normal_one)
    gvec_ref[S1 : S1 + 1, :] += column_sum(grad_first)
    grad_sum = norm_back(grad_first * vec(G1), normal_one, scale_one)
    sum_ref[...] = grad_sum
    grad_one = grad_sum.astype(BF16)
    gvec_ref[BO : BO + 1, :] += column_sum(grad_one)
    acc_wo[...] += dot(jnp.transpose(att_ref[...]), grad_one)
    datt_ref[...] = dot_right(grad_one, wo_ref[...]).astype(BF16)

    @pl.when(step == pl.num_programs(0) - 1)
    def _():
        weight = scale_ref[0]

        def cast(index, carry):
            for ref, acc in ((gwo_ref, acc_wo), (gwin_ref, acc_win), (gwd_ref, acc_wd)):
                size = acc.shape[0] // 24
                some = pl.ds(pl.multiple_of(index * size, size), size)
                ref[some, :] = (acc[some, :] * weight).astype(BF16)
            return carry

        lax.fori_loop(0, 24, cast, 0)
        gvec_ref[...] = gvec_ref[...] * weight
        for row in range(VECTORS - BIN):
            for d in range(width // mine):
                start = (d * (VECTORS - BIN) + row) * mine
                piece = gbin_ref[:, start : start + mine] * weight
                gvec_ref[BIN + row : BIN + row + 1, d * mine : (d + 1) * mine] = piece


def middle(scale, rows, att, cot, w_out, w_in, w_down, vectors, b_in, mine):
    count, width = rows.shape
    hidden = w_in.shape[1]
    tile = 256
    whole = lambda shape: pl.BlockSpec(shape, lambda i: (0,) * len(shape), pipeline_mode=pl.Buffered(1))
    row = pl.BlockSpec((tile, width), lambda i: (i, 0))
    shape = jax.ShapeDtypeStruct
    return pl.pallas_call(
        partial(middle_kernel, mine),
        name="middle",
        grid=(count // tile,),
        in_specs=[pl.BlockSpec(memory_space=pltpu.SMEM), row, row, row]
        + [whole(a.shape) for a in (w_out, w_in, w_down, vectors, b_in)],
        out_specs=[row, row, row]
        + [whole(s) for s in (w_out.shape, w_in.shape, w_down.shape, (16, width))],
        out_shape=[
            shape((count, width), BF16),
            shape((count, width), F32),
            shape((count, width), BF16),
            shape(w_out.shape, BF16),
            shape(w_in.shape, BF16),
            shape(w_down.shape, BF16),
            shape((16, width), F32),
        ],
        scratch_shapes=[
            pltpu.VMEM((1, hidden), F32),
            pltpu.VMEM(w_out.shape, F32),
            pltpu.VMEM(w_in.shape, F32),
            pltpu.VMEM(w_down.shape, F32),
            pltpu.VMEM((tile, hidden), BF16),
            pltpu.VMEM((tile, hidden), F32),
        ],
        compiler_params=pltpu.CompilerParams(vmem_limit_bytes=VMEM_BYTES),
        cost_estimate=pl.CostEstimate(flops=65_000_000_000, bytes_accessed=60_000_000, transcendentals=12_000_000),
    )(scale, rows, att, cot, w_out, w_in, w_down, vectors, b_in)


def backward_kernel(near, scale_ref, x_ref, qkv_ref, datt_ref, lse_ref, seg_ref, pad_ref, sum_ref, rest_ref, *refs):
    w_refs, refs = refs[:GROUPS], refs[GROUPS:]
    step = pl.program_id(0)
    length, width = x_ref.shape
    part = width // GROUPS
    half = width // HEADS
    steps = GROUPS * SEQS
    per = SCATTER_SLOTS
    last = per * (steps + SEQS)
    plan = {}
    if near:
        given, gx_ref, sums, refs = refs[:3], refs[3], refs[4:11], refs[11:]
        xt_ref, dqkv_ref, gvec_ref, mask_ref = refs[:4]
        terms = refs[4 : 5 + GROUPS]
        refs = refs[5 + GROUPS :]
        each = len(refs) // 7
        place = Place()
        jobs = [
            Scatter(place, t, sums[i], refs[each * i : each * (i + 1)], SCATTER_LINE_LAST[i])
            for i, t in enumerate(given + terms)
        ]
        plan = planned(SCATTER_TABLE, jobs)
        put = lambda ref, value: ref.__setitem__(..., value.reshape(ref.shape))
    else:
        gx_ref, terms, refs = refs[0], refs[1 : 2 + GROUPS], refs[2 + GROUPS :]
        xt_ref, dqkv_ref, gvec_ref, mask_ref = refs
        put = lambda ref, value: ref.__setitem__(..., value)

    @pl.when(step == 0)
    def _():
        if near:
            place.meet()
        gvec_ref[...] = jnp.zeros_like(gvec_ref)

    @pl.when(step < SEQS)
    def _():
        xt_ref[:, pl.ds(pl.multiple_of(step * length, length), length)] = jnp.transpose(x_ref[...])

    at = pl.multiple_of(step % SEQS * length, length)

    @pl.when(step < steps)
    def _():
        group = step // SEQS
        fill_mask(seg_ref, pad_ref, step % SEQS, mask_ref)
        first_half = lax.broadcasted_iota(jnp.int32, (1, 2 * half), 1) < half
        pairs = part // (2 * half)

        def back(pair):
            if near and pair < per:
                at_slot(per * step + pair, {s: e for s, e in plan.items() if s % per == pair and s < per * steps})
            base = pair * 2 * half
            pick = lambda ref, start: ref[:, pl.ds(start + base, 2 * half)]
            queries, keys, values = (pick(qkv_ref, third * part) for third in range(3))
            grads = pick(datt_ref, 0)
            keys_t = jnp.transpose(keys)
            keys = keys * jnp.asarray(0.125, BF16)
            grad_k = jnp.zeros(keys.shape, F32)
            grad_v = jnp.zeros(keys.shape, F32)
            grad_q = []
            for head in range(2):
                mine = first_half if head == 0 else ~first_half
                only = lambda arr: jnp.where(mine, arr, jnp.zeros_like(arr))
                scores = dot_right(only(keys), queries) + mask_ref[...]
                probs = jnp.exp(scores - lse_ref[0, pl.ds(2 * pair + head, 1), :])
                grad_probs = dot_right(only(values), grads)
                inner = jnp.sum(probs * grad_probs, 0, keepdims=True)
                grad_scores = (probs * (grad_probs - inner)).astype(BF16)
                grad_v = grad_v + dot(probs.astype(BF16), only(grads))
                grad_k = grad_k + dot(grad_scores, only(queries))
                grad_q.append(dot(keys_t[head * half : (head + 1) * half], grad_scores))
            grad_q = jnp.transpose(jnp.concatenate(grad_q, 0))
            for third, value in enumerate((grad_q * 0.125, grad_k * 0.125, grad_v)):
                dqkv_ref[group, pl.ds(at, length), pl.ds(third * part + base, 2 * half)] = value.astype(BF16)
                if third != 1:
                    row = BQ if third == 0 else BV
                    into = pl.ds(pl.multiple_of(group * part + base, 2 * half), 2 * half)
                    gvec_ref[row : row + 1, into] += column_sum(value.astype(BF16))

        for pair in range(pairs):
            back(pair)

    for group in range(GROUPS):

        @pl.when(step == group * SEQS + SEQS - 1)
        def _():
            for third in range(3):
                cols = slice(third * part, (third + 1) * part)
                grad = dot(xt_ref[...], dqkv_ref[group, :, cols]) * scale_ref[0]
                if near:
                    terms[group][:, :, cols] = grad.astype(BF16).reshape(*terms[group].shape[:2], part)
                else:
                    terms[group][:, cols] = grad.astype(BF16)

    @pl.when(step == steps - 1)
    def _():
        gvec_ref[:2] = gvec_ref[:2] * scale_ref[0]
        gvec_ref[2:VECTORS] = rest_ref[2:VECTORS]
        packed = jnp.transpose(gvec_ref[...]).astype(BF16)
        put(terms[GROUPS], jnp.concatenate([packed, jnp.zeros_like(packed)], 1))

    @pl.when(step >= steps)
    def _():
        if near:
            at_slot(per * step, {s: e for s, e in plan.items() if s % per == 0 and per * steps <= s < last})
        grad_x = sum_ref[...]
        for group in range(GROUPS):
            grad_x = grad_x + dot_right(dqkv_ref[group, pl.ds(at, length), :], w_refs[group][...])
        gx_ref[...] = grad_x
        if near and per > 1:
            at_slot(per * step, {s - 1: e for s, e in plan.items() if s % per and per * steps < s < last})

    if near:

        @pl.when(step == steps + SEQS - 1)
        def _():
            run_now(plan, last)


def attention_backward(near, scale, rows, qkv, datt, lse, segments, pads, grad_sum, rest, w_groups, given):
    seqs, length = segments.shape
    count, width = rows.shape
    part = width // GROUPS
    steps = GROUPS * seqs
    whole = lambda shape: pl.BlockSpec(shape, lambda i: (0,) * len(shape), pipeline_mode=pl.Buffered(1))
    now = lambda i: jnp.minimum(i, steps - 1)
    tokens = whole((seqs, length))
    late = pl.BlockSpec((length, width), lambda i: (jnp.maximum(i - steps, 0), 0))
    shape = jax.ShapeDtypeStruct
    in_specs = [
        pl.BlockSpec(memory_space=pltpu.SMEM),
        pl.BlockSpec((length, width), lambda i: (jnp.minimum(i, seqs - 1), 0)),
        pl.BlockSpec((length, width), lambda i: (now(i) % seqs, now(i) // seqs)),
        pl.BlockSpec((length, part), lambda i: (now(i) % seqs, now(i) // seqs)),
        pl.BlockSpec((1, 8, length), lambda i: (now(i), 0, 0)),
        tokens,
        tokens,
        late,
        whole(rest.shape),
    ] + [whole(w.shape) for w in w_groups]
    scratch = [
        pltpu.VMEM((width, count), BF16),
        pltpu.VMEM((GROUPS, count, width), BF16),
        pltpu.VMEM((128, width), F32),
        pltpu.VMEM((length, length), F32),
    ]
    out_shape = [shape((count, width), F32)]
    remotely = {}
    if near:
        in_specs += [pl.BlockSpec(memory_space=pl.ANY)] * 3
        made = [(16, width // 16, width)] * GROUPS + [(16, width // 16, 256)]
        scratch += [pltpu.VMEM(m, BF16) for m in made]
        every_shape = [g.shape for g in given] + made
        out_shape += [shape((s[1] // 2, s[2]), F32) for s in every_shape]
        for s, line_last in zip(every_shape, SCATTER_LINE_LAST):
            scratch += scatter_buffers(s[1], s[2], line_last)
        remotely = dict(collective_id=1, has_side_effects=True)
    else:
        out_shape += [shape((width, width), BF16)] * GROUPS + [shape((width, 256), BF16)]
    return pl.pallas_call(
        partial(backward_kernel, near),
        name="attention_backward",
        grid=(steps + seqs,),
        in_specs=in_specs,
        out_specs=[late] + [whole(s.shape) for s in out_shape[1:]],
        out_shape=out_shape,
        scratch_shapes=scratch,
        compiler_params=pltpu.CompilerParams(vmem_limit_bytes=VMEM_BYTES, **remotely),
    )(scale, rows, qkv, datt, lse, segments, pads, grad_sum, rest, *w_groups, *given)


def join_groups(parts, width):
    part = width // GROUPS
    cut = [p[:, third * part : (third + 1) * part] for third in range(3) for p in parts]
    return jnp.concatenate(cut, 1)


def finish_kernel(wd_ref, win_ref, wo_ref, *refs):
    parts, small_ref, outs = refs[:GROUPS], refs[GROUPS], refs[GROUPS + 1 :]
    qkv_ref, o_wd, o_win, o_wo = outs[:4]
    width = parts[0].shape[1]
    part = width // GROUPS
    for third in range(3):
        for group in range(GROUPS):
            cols = slice(third * width + group * part, third * width + (group + 1) * part)
            qkv_ref[:, cols] = parts[group][:, third * part : (third + 1) * part]
    o_wd[...] = wd_ref[...]
    o_win[...] = win_ref[...]
    o_wo[...] = wo_ref[...]
    mine = small_ref.shape[0]
    square = jnp.concatenate([small_ref[:, :128], jnp.zeros((128 - mine, 128), F32)], 0)
    vectors = jnp.transpose(square)
    for row in range(BIN):
        outs[4 + row][...] = vectors[row : row + 1, :mine]
    outs[4 + BIN][...] = jnp.concatenate([vectors[row : row + 1, :mine] for row in range(BIN, VECTORS)], 1)


def finish(sums):
    wd, win, wo, *rest = sums
    mine, width = rest[0].shape
    shape = jax.ShapeDtypeStruct
    vmem = pl.BlockSpec(memory_space=pltpu.VMEM)
    outs = pl.pallas_call(
        finish_kernel,
        name="finish",
        in_specs=[vmem] * 7,
        out_specs=[vmem] * (5 + BIN),
        out_shape=[shape((mine, 3 * width), F32)]
        + [shape(a.shape, F32) for a in (wd, win, wo)]
        + [shape((1, mine), F32)] * BIN
        + [shape((1, (VECTORS - BIN) * mine), F32)],
    )(*sums)
    return outs[0], outs[1:4], [v.reshape(-1) for v in outs[4:]]


def body(
    hidden_in, out_grad, segment_ids, pad_mask, task_weight, w_qkv, b_query, b_value, w_out, b_out,
    gain_one, shift_one, w_in, b_in, w_down, b_down, gain_two, shift_two,
):
    seqs, length, width = hidden_in.shape
    mine = w_qkv.shape[0]
    part = width // GROUPS
    near = lax.axis_size("task") == 4 and lax.axis_size("batch") == 8 and mine % 8 == 0
    vectors = [b_query, b_value, b_out, gain_one, shift_one, b_down, gain_two, shift_two, b_in]
    rows = hidden_in.reshape(-1, width)
    if near:
        weights = [*vectors, w_qkv, w_out, w_in, w_down]
        qkv, att, lse, vectors, bin_full, _, *full = attention_forward(True, rows, segment_ids, pad_mask, weights)
    else:
        packed = jnp.transpose(jnp.concatenate(vectors).reshape(VECTORS, mine))
        packed = jnp.pad(packed, ((0, 0), (0, 256 - VECTORS)))
        cut = w_qkv.reshape(mine, 3, GROUPS, part)
        groups = [cut[:, :, g].reshape(mine, width) for g in range(GROUPS)]
        full = [lax.all_gather(w, AXES, axis=0, tiled=True) for w in (packed, *groups, w_out, w_in, w_down)]
        qkv, att, lse, vectors, bin_full = attention_forward(False, rows, segment_ids, pad_mask, full[:4])
        full = full[1:]
    *w_groups, wo_full, win_full, wd_full = full
    hidden_out, grad_sum, datt, g_wo, g_win, g_wd, g_rest = middle(
        task_weight, rows, att, out_grad.reshape(-1, width), wo_full, win_full, wd_full, vectors, bin_full, mine
    )
    given = [g.reshape(16, -1, g.shape[1]) for g in (g_wd, g_win, g_wo)] if near else []
    grad_x, *terms = attention_backward(
        near, task_weight, rows, qkv, datt, lse, segment_ids, pad_mask, grad_sum, g_rest, w_groups, given
    )
    if near:
        s_qkv, (s_wd, s_win, s_wo), s_vec = finish(terms)
    else:
        s_wd, s_win, s_wo, *parts, small = [
            lax.psum_scatter(t, AXES, scatter_dimension=0, tiled=True).astype(F32) for t in (g_wd, g_win, g_wo, *terms)
        ]
        s_qkv = join_groups(parts, width)
        s_vec = [small[:, row] for row in range(BIN)] + [jnp.transpose(small[:, BIN:VECTORS]).reshape(-1)]
    return (
        hidden_out.reshape(hidden_in.shape),
        grad_x.reshape(hidden_in.shape),
        s_qkv,
        s_vec[BQ],
        s_vec[BV],
        s_wo,
        s_vec[BO],
        s_vec[G1],
        s_vec[S1],
        s_win,
        s_vec[BIN],
        s_wd,
        s_vec[BD],
        s_vec[G2],
        s_vec[S2],
    )


def solution(mesh):
    seq, mat, vec = P(AXES, None, None), P(AXES, None), P(AXES)
    weights = (mat, vec, vec, mat, vec, vec, vec, mat, vec, mat, vec, vec, vec)
    return jax.shard_map(
        body,
        mesh=mesh,
        in_specs=(seq, seq, mat, mat, P("task")) + weights,
        out_specs=(seq, seq) + weights,
        check_vma=False,
    )
```

```python
from functools import partial

import jax
import jax.numpy as jnp
from jax import lax
from jax.experimental import pallas as pl
from jax.experimental.pallas import tpu as pltpu
from jax.sharding import PartitionSpec as P

HEADS = 12
GROUPS = 3
SEQS = 4
AXES = ("task", "batch")
F32 = jnp.float32
BF16 = jnp.bfloat16
VMEM_BYTES = 66_900_000
BQ, BV, BO, G1, S1, BD, G2, S2, BIN = range(9)
VECTORS = 12

GATHER_TABLE = [
    (0, 0, 0), (0, 0, 1), (0, 1, 0), (0, 1, 1), (0, 0, 2), (0, 0, 3), (0, 0, 4), (0, 0, 5), (0, 2, 0), (0, 3, 0),
    (0, 1, 2), (0, 1, 3), (0, 1, 4), (0, 1, 5), (0, 0, 6), (0, 0, 7), (0, 0, 8), (0, 0, 9), (0, 2, 1), (0, 3, 1),
    (0, 0, 10), (0, 0, 11), (0, 0, 12), (0, 1, 6), (0, 4, 0), (0, 1, 7), (0, 1, 8), (0, 1, 9), (0, 1, 10), (0, 1, 11),
    (0, 1, 12), (0, 0, 13), (0, 0, 14), (0, 0, 15), (0, 0, 16), (0, 4, 1), (0, 2, 2), (0, 2, 3), (0, 2, 4), (0, 2, 5),
    (0, 0, 19), (0, 3, 2), (0, 3, 3), (0, 3, 4), (0, 3, 5), (0, 0, 17), (0, 0, 18), (0, 0, 20), (0, 0, 21),
    (0, 0, 22), (0, 1, 13), (0, 1, 14), (0, 1, 15), (0, 1, 16), (0, 1, 17), (0, 1, 18), (0, 1, 19), (0, 1, 20),
    (0, 0, 23), (0, 0, 24), (0, 0, 25), (0, 4, 2), (0, 4, 5), (0, 0, 26), (0, 1, 23), (0, 1, 24), (0, 2, 6),
    (0, 2, 7), (0, 2, 8), (0, 2, 9), (0, 2, 10), (0, 2, 11), (0, 2, 12), (0, 4, 3), (0, 4, 4), (0, 3, 6), (0, 3, 7),
    (0, 3, 8), (0, 3, 10), (0, 0, 27), (0, 1, 25), (0, 1, 26), (0, 0, 28), (0, 0, 29), (0, 4, 7), (0, 4, 8),
    (1, 1, 21), (1, 1, 22), (1, 1, 27), (1, 1, 28), (1, 2, 15), (1, 2, 16), (1, 2, 19), (1, 2, 20), (1, 3, 9),
    (1, 3, 11), (1, 3, 14), (2, 1, 29), (2, 2, 13), (2, 2, 14), (2, 2, 17), (2, 2, 18), (2, 4, 6), (2, 4, 11),
    (2, 4, 12), (3, 2, 26), (3, 4, 9), (3, 4, 10), (3, 3, 12), (3, 3, 13), (4, 2, 23), (4, 2, 24), (4, 2, 25),
    (4, 4, 15), (4, 4, 16), (4, 3, 15), (4, 3, 16), (4, 3, 17), (4, 3, 18), (5, 4, 13), (5, 4, 19), (5, 4, 20),
    (5, 3, 21), (6, 2, 21), (6, 2, 22), (6, 2, 27), (6, 2, 28), (6, 4, 14), (6, 4, 23), (6, 4, 24), (6, 3, 19),
    (6, 3, 20), (6, 3, 22), (6, 3, 23), (6, 3, 24), (7, 2, 29), (7, 4, 17), (7, 4, 18), (7, 4, 21), (7, 4, 22),
    (7, 4, 25), (7, 4, 26), (8, 4, 27), (8, 4, 28), (8, 3, 25), (8, 3, 26), (8, 3, 27), (8, 3, 28), (9, 4, 29),
    (9, 3, 29),
]
SCATTER_TABLE = [
    (0, 1, 0), (1, 1, 1), (1, 0, 0), (2, 1, 2), (2, 1, 3), (2, 1, 4), (3, 1, 5), (3, 1, 6), (3, 1, 7), (3, 1, 8),
    (3, 0, 1), (3, 0, 2), (3, 0, 3), (3, 0, 4), (3, 1, 9), (3, 1, 10), (4, 2, 0), (4, 1, 11), (4, 1, 12), (4, 1, 15),
    (4, 1, 16), (4, 1, 17), (4, 1, 18), (5, 2, 1), (5, 2, 2), (5, 2, 3), (5, 2, 4), (5, 1, 13), (5, 1, 19),
    (5, 1, 20), (5, 1, 21), (5, 0, 5), (5, 0, 6), (6, 1, 14), (6, 1, 25), (6, 0, 7), (6, 0, 8), (6, 0, 9), (6, 0, 10),
    (7, 1, 22), (7, 1, 23), (7, 1, 26), (7, 0, 11), (7, 0, 15), (7, 0, 16), (7, 0, 17), (7, 0, 18), (8, 3, 0),
    (8, 2, 5), (8, 2, 6), (8, 2, 7), (8, 2, 8), (8, 2, 9), (8, 2, 10), (8, 2, 11), (8, 2, 12), (8, 1, 24), (8, 1, 27),
    (8, 1, 28), (8, 1, 29), (8, 0, 12), (8, 0, 19), (8, 0, 20), (8, 0, 21), (9, 3, 1), (9, 3, 2), (9, 3, 3),
    (9, 3, 4), (9, 2, 13), (9, 2, 14), (9, 2, 15), (9, 2, 16), (9, 2, 17), (9, 2, 18), (9, 2, 19), (9, 1, 30),
    (9, 0, 13), (9, 0, 14), (10, 3, 5), (10, 3, 6), (10, 3, 7), (10, 3, 8), (10, 3, 9), (10, 3, 10), (10, 3, 11),
    (10, 1, 31), (10, 1, 32), (10, 0, 22), (10, 0, 25), (10, 3, 12), (11, 3, 13), (11, 3, 14), (11, 3, 15),
    (11, 3, 16), (11, 3, 17), (11, 3, 18), (11, 3, 19), (11, 2, 20), (11, 1, 33), (11, 0, 23), (11, 0, 24),
    (11, 0, 26), (12, 4, 0), (12, 3, 20), (12, 3, 21), (12, 3, 22), (12, 2, 21), (12, 2, 22), (12, 2, 23),
    (12, 0, 27), (12, 0, 28), (12, 0, 29), (12, 0, 30), (14, 4, 1), (14, 4, 2), (15, 4, 3), (15, 4, 4), (15, 3, 23),
    (15, 2, 25), (16, 3, 24), (16, 2, 24), (16, 2, 26), (17, 4, 5), (18, 4, 6), (18, 4, 7), (18, 2, 27), (18, 0, 31),
    (18, 0, 32), (19, 4, 8), (19, 4, 9), (19, 3, 25), (19, 3, 26), (20, 4, 10), (20, 4, 11), (20, 0, 33), (21, 4, 12),
    (21, 4, 13), (21, 4, 14), (21, 3, 27), (22, 4, 15), (22, 4, 16), (22, 4, 17), (22, 4, 18), (23, 4, 19),
    (24, 4, 20), (24, 4, 21), (24, 4, 22), (24, 4, 23), (24, 4, 24), (24, 4, 25), (24, 4, 26), (24, 4, 27),
]
GATHER_LINE_FIRST = [False, False, False, True, False]
SCATTER_LINE_LAST = [False, False, True, True, True]
GATHER_SLOTS, SCATTER_SLOTS = 1, 1


MESH = pl.DeviceIdType.MESH


class Place:
    def __init__(self):
        self.task = lax.axis_index("task")
        self.batch = lax.axis_index("batch")
        self.core = self.batch % 2
        self.z = self.batch // 2
        x, y = self.task % 2, self.task // 2
        flip_x, flip_y = self.task + 1 - 2 * x, self.task + 2 - 4 * y
        self.task_a = (1 - self.core) * flip_x + self.core * flip_y
        self.task_b = (1 - self.core) * flip_y + self.core * flip_x
        self.task_ab = 3 - self.task
        self.partner = (self.task, self.batch + 1 - 2 * self.core)
        self.peer_a = (self.task_a, self.batch)
        self.peer_b = (self.task_b, self.batch)
        self.above = (self.task, self.batch + 2)
        self.below = (self.task, self.batch - 2)
        self.low = 1 - self.z // 2
        self.inner = self.low * self.z + (1 - self.low) * (3 - self.z)
        self.far = (self.task, self.batch + 4 * self.low - 2)
        self.near = (self.task, self.batch + 2 - 4 * self.low)

    def meet(self):
        barrier = pltpu.get_barrier_semaphore()
        for peer in (self.partner, self.peer_a, self.peer_b):
            pl.semaphore_signal(barrier, inc=1, device_id=peer, device_id_type=MESH)

        @pl.when(self.z < 3)
        def _():
            pl.semaphore_signal(barrier, inc=1, device_id=self.above, device_id_type=MESH)

        @pl.when(self.z > 0)
        def _():
            pl.semaphore_signal(barrier, inc=1, device_id=self.below, device_id_type=MESH)

        pl.semaphore_wait(barrier, 4 + self.z * (3 - self.z) // 2)


def remote(src, dst, send, recv, peer):
    return pltpu.make_async_remote_copy(src, dst, send, recv, device_id=peer, device_id_type=MESH)


GATHER_SEMS = [
    pltpu.SemaphoreType.DMA((12,)),
    pltpu.SemaphoreType.DMA((7,)),
    pltpu.SemaphoreType.DMA((14,)),
    pltpu.SemaphoreType.DMA((14,)),
    pltpu.SemaphoreType.DMA((6,)),
]


class Gather:
    def __init__(self, place, windows, full, sems, line_first=False):
        self.place, self.windows, self.full, self.line_first = place, windows, full, line_first
        self.send_z, self.send_a, self.recv, self.recv_b, self.misc = sems
        self.half = full.shape[1] // 2
        self.r = full.shape[0] // 32

    def rows(self, task, batch, count):
        return pl.ds(pl.multiple_of((task * 8 + batch) * self.r, 8), count * self.r)

    def cols(self, core):
        return pl.ds(pl.multiple_of(core * self.half, 128), self.half)

    def task(self, which):
        return self.place.task if which == 0 else self.place.task_a

    def level(self, spot):
        return self.place.z - spot if spot < 4 else self.place.z + spot - 3

    def here(self, spot):
        return self.place.z >= spot if spot < 4 else self.place.z + spot <= 6

    def chunk(self, task, spot):
        return self.full.at[self.rows(task, 2 * self.level(spot), 2), self.cols(self.place.core)]

    def begin(self):
        place, at = self.place, 0
        for window in self.windows:
            into = self.full.at[self.rows(place.task, place.batch, 1), pl.ds(at, window.shape[1])]
            pltpu.make_async_copy(window, into, self.misc.at[0]).start()
            remote(window, into, self.misc.at[1], self.misc.at[2], place.partner).start()
            at += window.shape[1]

    def along_z(self, which, spot, up):
        step = spot if up else max(spot - 3, 0)
        slot = which * 6 + step + (0 if up else 3)
        chunk = self.chunk(self.task(which), spot)
        into = which * 7 + step + (1 if up else 4)
        return remote(chunk, chunk, self.send_z.at[slot], self.recv.at[into], self.place.above if up else self.place.below)

    def along_a(self, spot):
        chunk = self.chunk(self.place.task, spot)
        return remote(chunk, chunk, self.send_a.at[spot], self.recv.at[7 + spot], self.place.peer_a)

    def along_b(self, which, spot):
        chunk = self.chunk(self.task(which), spot)
        return remote(chunk, chunk, self.misc.at[3], self.recv_b.at[which * 7 + spot], self.place.peer_b)

    def hand_over(self, task, spot):
        chunk = self.chunk(task, spot)
        remote(chunk, chunk, self.misc.at[4], self.misc.at[5], self.place.partner).start()

    def arrived(self, task, spot, sem):
        chunk = self.chunk(task, spot)
        remote(chunk, chunk, self.misc.at[1], sem, self.place.partner).wait_recv()

    def onward(self, which, spot):
        place = self.place
        if which == 0 or not self.line_first:
            for up in (True, False):
                if spot == 0 or (spot < 3 if up else 3 < spot < 6):
                    more = place.z < 3 if up else place.z > 0

                    @pl.when(more)
                    def _():
                        self.along_z(which, spot, up).start()

        if which == 0 and (spot == 0 or self.line_first):
            self.along_a(spot).start()
        self.along_b(which, spot).start()
        if which or spot:
            self.hand_over(self.task(which), spot)

    def spread(self):
        place = self.place
        mine = self.full.at[self.rows(place.task, place.batch, 1), :]
        pltpu.make_async_copy(mine, mine, self.misc.at[0]).wait()
        other = self.full.at[self.rows(place.task, place.partner[1], 1), :]
        remote(other, other, self.misc.at[1], self.misc.at[2], place.partner).wait_recv()
        self.onward(0, 0)

    def line(self, which, spot):
        @pl.when(self.here(spot))
        def _():
            self.arrived(self.task(which), spot, self.recv.at[which * 7 + spot])
            self.onward(which, spot)

    def from_b(self, which, spot):
        task = self.place.task_b if which == 0 else self.place.task_ab

        @pl.when(self.here(spot))
        def _():
            self.arrived(task, spot, self.recv_b.at[which * 7 + spot])
            self.hand_over(task, spot)

    def finish(self):
        place, full, r = self.place, self.full, self.r
        rest = full.at[pl.ds(0, 30 * r), self.cols(1 - place.core)]
        remote(rest, rest, self.misc.at[4], self.misc.at[5], place.partner).wait_recv()
        mine = full.at[pl.ds(0, 30 * r), self.cols(place.core)]
        remote(mine, mine, self.misc.at[4], self.misc.at[5], place.partner).wait_send()
        eight = full.at[pl.ds(0, 16 * r), self.cols(place.core)]
        remote(eight, eight, self.misc.at[3], self.recv_b.at[0], place.peer_b).wait_send()
        own = full.at[self.rows(place.task, place.batch, 1), :]
        remote(own, own, self.misc.at[1], self.misc.at[2], place.partner).wait_send()
        for spot in range(7 if self.line_first else 1):

            @pl.when(self.here(spot))
            def _():
                self.along_a(spot).wait_send()

        for which in range(1 if self.line_first else 2):
            for spot in (0, 1, 2):

                @pl.when(self.here(spot) & (place.z < 3))
                def _():
                    self.along_z(which, spot, True).wait_send()

            for spot in (0, 4, 5):

                @pl.when(self.here(spot) & (place.z > 0))
                def _():
                    self.along_z(which, spot, False).wait_send()

    def events(self):
        line, b = self.line, self.from_b
        out = [self.begin, self.spread]
        if self.line_first:
            out += [partial(line, 0, 1), partial(line, 0, 4), partial(line, 1, 0), partial(b, 0, 0)]
            out += [partial(line, 0, 2), partial(line, 0, 5), partial(line, 1, 1), partial(line, 1, 4)]
            out += [partial(b, 0, 1), partial(b, 0, 4), partial(line, 0, 3), partial(line, 0, 6), partial(b, 1, 0)]
            out += [partial(line, 1, 2), partial(line, 1, 5), partial(b, 0, 2), partial(b, 0, 5)]
            out += [partial(line, 1, 3), partial(line, 1, 6), partial(b, 1, 1), partial(b, 1, 4)]
            out += [partial(b, w, s) for w, s in ((0, 3), (0, 6), (1, 2), (1, 5), (1, 3), (1, 6))]
        else:
            out += [partial(line, 1, 0), partial(line, 0, 1), partial(line, 0, 4), partial(b, 0, 0), partial(b, 1, 0)]
            out += [partial(line, 1, 1), partial(line, 1, 4), partial(b, 0, 1), partial(b, 0, 4)]
            out += [partial(line, 0, 2), partial(line, 0, 5), partial(b, 1, 1), partial(b, 1, 4)]
            out += [partial(line, 1, 2), partial(line, 1, 5), partial(b, 0, 2), partial(b, 0, 5)]
            out += [partial(line, 0, 3), partial(line, 0, 6), partial(b, 1, 2), partial(b, 1, 5)]
            out += [partial(line, 1, 3), partial(line, 1, 6), partial(b, 0, 3), partial(b, 0, 6)]
            out += [partial(b, 1, 3), partial(b, 1, 6)]
        return out + [self.finish]


SCATTER_SEMS = [
    pltpu.SemaphoreType.DMA((4,)),
    pltpu.SemaphoreType.DMA((4,)),
    pltpu.SemaphoreType.DMA((4,)),
    pltpu.SemaphoreType.DMA((8,)),
    pltpu.SemaphoreType.DMA((8,)),
    pltpu.SemaphoreType.DMA((8,)),
    pltpu.SemaphoreType.DMA((10,)),
    pltpu.SemaphoreType.DMA((4,)),
    pltpu.SemaphoreType.DMA((4,)),
    pltpu.SemaphoreType.DMA((2,)),
]


def scatter_buffers(rows, cols, line_last=False):
    half = cols // 2
    return [
        pltpu.VMEM((16, rows, half), BF16),
        pltpu.VMEM((16, rows, half), BF16),
        pltpu.VMEM((8, rows, half), BF16),
        pltpu.VMEM((5 if line_last else 10, rows, half), BF16),
        pltpu.VMEM((4 if line_last else 1, rows, half), BF16),
        pltpu.VMEM((rows, half), F32),
        pltpu.VMEM((rows // 2, half), F32),
    ] + SCATTER_SEMS


class Scatter:
    def __init__(self, place, terms, out, buffers, line_last=False):
        self.place, self.terms, self.out, self.line_last = place, terms, out, line_last
        (self.own, self.other, self.got_b, self.got_z, self.got_a, self.total, self.got_f) = buffers[:7]
        (
            self.s_load, self.s_pair, self.r_pair, self.s_b, self.r_b, self.s_z, self.r_z, self.s_a, self.r_a, self.misc
        ) = buffers[7:]
        self.half = self.own.shape[2]
        self.tasks = (place.task_ab, place.task_b, place.task_a, place.task)
        self.tasks_partner = (place.task_ab, place.task_a, place.task_b, place.task)

    def cols(self, core):
        return pl.ds(pl.multiple_of(core * self.half, 128), self.half)

    def level(self, m):
        return self.place.low * m + (1 - self.place.low) * (3 - m)

    def load(self, index):
        first = self.tasks[index] * 4
        return pltpu.make_async_copy(
            self.terms.at[pl.ds(first, 4), :, self.cols(self.place.core)],
            self.own.at[pl.ds(first, 4)],
            self.s_load.at[index],
        )

    def pair(self, index, sent=True):
        first = (self.tasks_partner if sent else self.tasks)[index] * 4
        return remote(
            self.terms.at[pl.ds(first, 4), :, self.cols(1 - self.place.core)],
            self.other.at[pl.ds(first, 4)],
            self.s_pair.at[index],
            self.r_pair.at[index],
            self.place.partner,
        )

    def begin(self):
        for index in range(4):
            self.load(index).start()
            self.pair(index).start()

    def add(self, at, ref, where):
        size = 48 if self.half <= 512 else 16

        def some(index, carry):
            rows = pl.ds(pl.multiple_of(index * size, size), size)
            self.own[at, rows] = self.own[at, rows] + ref[where, rows]
            return carry

        lax.fori_loop(0, self.own.shape[1] // size, some, 0)

    def along_b(self, which, z):
        slot = which * 4 + z
        return remote(
            self.own.at[self.tasks[which] * 4 + z], self.got_b.at[slot], self.s_b.at[slot], self.r_b.at[slot],
            self.place.peer_b,
        )

    def add_pair(self, index):
        self.load(index).wait()
        self.pair(index, False).wait_recv()
        first = self.tasks[index] * 4

        def chunk(count, carry):
            z = self.level(3 - count)
            self.add(first + z, self.other, first + z)
            if index < 2:
                self.along_b(index, z).start()
            return carry

        lax.fori_loop(0, 4, chunk, 0)

    def add_b(self, which, m):
        z = self.level(m)
        self.along_b(which, z).wait_recv()
        self.add(self.tasks[2 + which] * 4 + z, self.got_b, which * 4 + z)
        if which == 0 and self.line_last:
            self.along_a(z).start()

    def along_z(self, which, m, far):
        place = self.place
        at = self.tasks[2 + which] * 4 + self.level(m)
        line = 0 if self.line_last else 5 * which
        into = line + ((1 - place.inner) * (m - 1) + place.inner * (6 - m) if far else 3 + m)
        peer = place.far if far else place.near
        return remote(self.own.at[at], self.got_z.at[into], self.s_z.at[which * 4 + m], self.r_z.at[into], peer)

    def add_z(self, which, m, slot):
        into = slot + (0 if self.line_last else 5 * which)
        got = self.got_z.at[into]
        remote(got, got, self.s_z.at[0], self.r_z.at[into], self.place.partner).wait_recv()
        self.add(self.tasks[2 + which] * 4 + self.level(m), self.got_z, into)

    def far_out(self, which, m):
        @pl.when(self.place.inner == 0)
        def _():
            self.along_z(which, m, True).start()

    def far_on(self, which, m):
        @pl.when(self.place.inner == 1)
        def _():
            self.add_z(which, m, m - 1)
            if m > 1:
                self.along_z(which, m, True).start()

    def near_on(self, which, m):
        @pl.when(self.place.inner == 1)
        def _():
            self.add_z(which, m, 3 + m)
            if m == 0:
                self.along_z(which, m, False).start()

    def near_in(self, which):
        @pl.when(self.place.inner == 0)
        def _():
            self.add_z(which, 0, 3)

    def along_a(self, z):
        slot = z if self.line_last else 0
        return remote(
            self.own.at[self.tasks[2] * 4 + z], self.got_a.at[slot], self.s_a.at[slot], self.r_a.at[slot],
            self.place.peer_a,
        )

    def to_a(self):
        self.along_a(self.place.z).start()

    def add_a(self, m):
        z = self.level(m)
        self.along_a(z).wait_recv()
        self.add(self.tasks[3] * 4 + z, self.got_a, z)

    def last(self):
        rows = self.got_f.shape[0]
        away = pl.multiple_of((1 - self.place.core) * rows, rows)
        return remote(
            self.total.at[pl.ds(away, rows)], self.got_f, self.misc.at[0], self.misc.at[1], self.place.partner
        )

    def close(self):
        total = self.own[self.tasks[3] * 4 + self.place.z].astype(F32)
        if not self.line_last:
            self.along_a(self.place.z).wait_recv()
            total = total + self.got_a[0].astype(F32)
        self.total[...] = total
        self.last().start()

    def finish(self):
        rows = self.got_f.shape[0]
        core = self.place.core
        self.last().wait_recv()
        self.out[:, self.cols(core)] = self.total[pl.ds(pl.multiple_of(core * rows, rows), rows), :]
        self.out[:, self.cols(1 - core)] = self.got_f[...]
        for index in range(4):
            self.pair(index).wait_send()
        for which in range(2):
            for z in range(4):
                self.along_b(which, z).wait_send()
        for which in range(1 if self.line_last else 0, 2):
            for m in range(4):

                @pl.when(self.place.inner < m)
                def _():
                    self.along_z(which, m, True).wait_send()

                @pl.when(self.place.inner > m)
                def _():
                    self.along_z(which, m, False).wait_send()

        for z in range(4 if self.line_last else 1):
            self.along_a(z if self.line_last else self.place.z).wait_send()
        self.last().wait_send()

    def events(self):
        out = [self.begin] + [partial(self.add_pair, i) for i in range(4)]
        if self.line_last:
            out += [partial(self.add_b, which, m) for which in range(2) for m in (3, 2, 1, 0)]
            for m in (3, 2, 1):
                out += [partial(self.add_a, m), partial(self.far_out, 1, m)]
            out.append(partial(self.add_a, 0))
            out += [partial(self.far_on, 1, m) for m in (3, 2, 1)]
            out += [partial(self.near_on, 1, 0), partial(self.near_on, 1, 1), partial(self.near_in, 1)]
        else:
            for which in range(2):
                for m in (3, 2, 1):
                    out += [partial(self.add_b, which, m), partial(self.far_out, which, m)]
                out.append(partial(self.add_b, which, 0))
                out += [partial(self.far_on, which, m) for m in (3, 2, 1)]
            for which in range(2):
                out += [partial(self.near_on, which, 0), partial(self.near_on, which, 1), partial(self.near_in, which)]
                if which == 0:
                    out.append(self.to_a)
        return out + [self.close, self.finish]


def dot(left, right):
    return lax.dot_general(left, right, (((1,), (0,)), ((), ())), preferred_element_type=F32)


def dot_right(left, right):
    return lax.dot_general(left, right, (((1,), (1,)), ((), ())), preferred_element_type=F32)


def at_slot(slot, plan):
    def choose(slots):
        if len(slots) == 1:

            @pl.when(slot == slots[0])
            def _():
                for event in plan[slots[0]]:
                    event()

            return
        middle_slot = slots[len(slots) // 2]

        @pl.when(slot < middle_slot)
        def _():
            choose(slots[: len(slots) // 2])

        @pl.when(slot >= middle_slot)
        def _():
            choose(slots[len(slots) // 2 :])

    if plan:
        choose(sorted(plan))


def fill_mask(seg_ref, pad_ref, row, mask_ref):
    length = mask_ref.shape[0]
    seg_row = seg_ref[pl.ds(row, 1), :].astype(F32)
    pad_row = pad_ref[pl.ds(row, 1), :].astype(F32)
    seg_col = jnp.transpose(jnp.broadcast_to(seg_row, (128, length)))
    pad_col = jnp.transpose(jnp.broadcast_to(pad_row, (128, length)))
    key_at = lax.broadcasted_iota(jnp.int32, (length, 128), 0)
    lane = lax.broadcasted_iota(jnp.int32, (length, 128), 1)
    for block in range(length // 128):
        same = seg_col == seg_row[:, 128 * block : 128 * block + 128]
        seen = (pad_col == 1.0) | (key_at == lane + 128 * block)
        mask_ref[:, 128 * block : 128 * block + 128] = jnp.where(same & seen, 0.0, -1e30)


def planned(table, jobs):
    plan = {}
    events = [job.events() for job in jobs]
    for slot, job, event in table:
        plan.setdefault(slot, []).append(events[job][event])
    return plan


def run_now(plan, slot):
    for event in plan.get(slot, []):
        event()


def forward_kernel(near, devices, x_ref, seg_ref, pad_ref, *refs):
    if near:
        vector_refs, refs = refs[: BIN + 1], refs[BIN + 1 :]
        wqkv_ref, wo_ref, win_ref, wd_ref = refs[:4]
        qkv_ref, att_ref, lse_ref, vec_ref, bin_ref = refs[4:9]
        fulls = refs[9:14]
        mask_ref, w_ref, small_ref, load_sem, shard_ref, square_ref = refs[14:20]
        sems = refs[20:]
    else:
        small, *groups = [ref.at[:, pl.ds(0, size)] for ref, size in zip(refs[:4], (128, 768, 768, 768))]
        qkv_ref, att_ref, lse_ref, vec_ref, bin_ref = refs[4:9]
        mask_ref, w_ref, small_ref, load_sem = refs[9:]
    step = pl.program_id(0)
    length, width = x_ref.shape
    part = width // GROUPS
    half = width // HEADS
    steps = GROUPS * SEQS
    per = GATHER_SLOTS
    last = per * steps
    plan = {}
    if near:
        groups = [fulls[0].at[:, pl.ds(0, width)], *fulls[1:GROUPS]]
        small = fulls[0].at[:, pl.ds(width, 128)]
        place = Place()
        windows = []
        for group in range(GROUPS):
            windows.append([wqkv_ref.at[:, pl.ds(third * width + group * part, part)] for third in range(3)])
        windows[0].append(shard_ref)
        windows += [[win_ref, wo_ref], [wd_ref]]
        jobs = [
            Gather(place, w, fulls[i], sems[5 * i : 5 * i + 5], GATHER_LINE_FIRST[i]) for i, w in enumerate(windows)
        ]
        plan = planned(GATHER_TABLE, jobs)

    @pl.when(step == 0)
    def _():
        if near:
            mine = shard_ref.shape[0]
            square_ref[...] = jnp.zeros_like(square_ref)
            for row, ref in enumerate(vector_refs):
                vector = ref[...].astype(F32).reshape(1, ref.shape[0])
                for j in range(ref.shape[0] // mine):
                    square_ref[row + j : row + j + 1, :mine] = vector[:, j * mine : (j + 1) * mine]
            shard_ref[:, :128] = jnp.transpose(square_ref[...])[:mine].astype(BF16)
            shard_ref[:, 128:] = jnp.zeros((shard_ref.shape[0], 128), BF16)
            place.meet()
            run_now(plan, 0)
        copy = pltpu.make_async_copy(small, small_ref, load_sem.at[0])
        copy.start()
        copy.wait()
        vec_ref[...] = jnp.transpose(small_ref[...].astype(F32))[:16]
        mine = small_ref.shape[0] // devices
        for d in range(devices):
            for j in range(VECTORS - BIN):
                start = (d * (VECTORS - BIN) + j) * mine
                bin_ref[:, start : start + mine] = vec_ref[BIN + j : BIN + j + 1, d * mine : (d + 1) * mine]

    if near:
        at_slot(per * step, {s: e for s, e in plan.items() if s % per == 0 and 0 < s < last})
    for group in range(GROUPS):

        @pl.when(step == group * SEQS)
        def _():
            copy = pltpu.make_async_copy(groups[group], w_ref, load_sem.at[1])
            copy.start()
            copy.wait()

    fill_mask(seg_ref, pad_ref, step % SEQS, mask_ref)
    at = pl.multiple_of(step // SEQS * part, part)
    for third, row in enumerate((BQ, None, BV)):
        cols = slice(third * part, (third + 1) * part)
        product = dot(x_ref[...], w_ref[:, cols])
        if row is not None:
            product = product + vec_ref[row : row + 1, pl.ds(at, part)]
        qkv_ref[:, cols] = product.astype(BF16)
    first_half = lax.broadcasted_iota(jnp.int32, (1, 2 * half), 1) < half
    pairs = part // (2 * half)

    def attend(pair):
        if near and 0 < pair < per:
            at_slot(per * step + pair, {s: e for s, e in plan.items() if s % per == pair and s < last})
        base = pair * 2 * half
        queries = qkv_ref[:, pl.ds(base, 2 * half)]
        keys = qkv_ref[:, pl.ds(part + base, 2 * half)] * jnp.asarray(0.125, BF16)
        values_t = jnp.transpose(qkv_ref[:, pl.ds(2 * part + base, 2 * half)])
        outs = []
        for head in range(2):
            mine = first_half if head == 0 else ~first_half
            scores = dot_right(jnp.where(mine, keys, jnp.zeros_like(keys)), queries) + mask_ref[...]
            top = jnp.max(scores, 0, keepdims=True)
            expo = jnp.exp(scores - top)
            total = jnp.sum(expo, 0, keepdims=True)
            probs = (expo * (1.0 / total)).astype(BF16)
            outs.append(dot(values_t[head * half : (head + 1) * half], probs))
            lse_ref[0, pl.ds(2 * pair + head, 1), :] = top + jnp.log(total)
        att_ref[:, pl.ds(base, 2 * half)] = jnp.transpose(jnp.concatenate(outs, 0)).astype(BF16)

    for pair in range(pairs):
        attend(pair)
    if near:

        @pl.when(step == steps - 1)
        def _():
            run_now(plan, last)


def attention_forward(near, rows, segments, pads, weights):
    seqs, length = segments.shape
    width = rows.shape[1]
    part = width // GROUPS
    anywhere = lambda count: [pl.BlockSpec(memory_space=pl.ANY)] * count
    tokens = pl.BlockSpec((seqs, length), lambda i: (0, 0))
    shape = jax.ShapeDtypeStruct
    out_specs = [
        pl.BlockSpec((length, width), lambda i: (i % seqs, i // seqs)),
        pl.BlockSpec((length, part), lambda i: (i % seqs, i // seqs)),
        pl.BlockSpec((1, 8, length), lambda i: (i, 0, 0)),
        pl.BlockSpec((16, width), lambda i: (0, 0)),
        pl.BlockSpec((1, (VECTORS - BIN) * width), lambda i: (0, 0)),
    ]
    out_shape = [
        shape((rows.shape[0], 3 * width), BF16),
        shape((rows.shape[0], width), BF16),
        shape((GROUPS * seqs, 8, length), F32),
        shape((16, width), F32),
        shape((1, (VECTORS - BIN) * width), F32),
    ]
    in_specs = [pl.BlockSpec((length, width), lambda i: (i % seqs, 0)), tokens, tokens]
    scratch = [
        pltpu.VMEM((length, length), F32),
        pltpu.VMEM((width, width), BF16),
        pltpu.VMEM((width, 128), BF16),
        pltpu.SemaphoreType.DMA((2,)),
    ]
    remotely = {}
    if near:
        *vectors, w_qkv, w_out, w_in, w_down = weights
        in_specs += [pl.BlockSpec(v.shape, lambda i: (0,)) for v in vectors]
        in_specs += [pl.BlockSpec(w.shape, lambda i: (0, 0)) for w in (w_qkv, w_out, w_in, w_down)]
        mine = w_qkv.shape[0]
        fulls = [(mine, width + 256)] + [(mine, width)] * (GROUPS - 1)
        fulls += [(mine, w_in.shape[1] + w_out.shape[1]), w_down.shape]
        out_specs += anywhere(5)
        out_shape += [shape((32 * r, c), BF16) for r, c in fulls]
        scratch += [pltpu.VMEM((mine, 256), BF16), pltpu.VMEM((128, 128), F32)] + GATHER_SEMS * 5
        remotely = dict(collective_id=0, has_side_effects=True)
    else:
        in_specs += anywhere(4)
    return pl.pallas_call(
        partial(forward_kernel, near, lax.axis_size(AXES)),
        name="attention_forward",
        grid=(GROUPS * seqs,),
        in_specs=in_specs,
        out_specs=out_specs,
        out_shape=out_shape,
        scratch_shapes=scratch,
        compiler_params=pltpu.CompilerParams(vmem_limit_bytes=VMEM_BYTES, **remotely),
    )(rows, segments, pads, *weights)


def norm_parts(arr):
    centre = arr - jnp.mean(arr, -1, keepdims=True)
    scale = lax.rsqrt(jnp.mean(centre * centre, -1, keepdims=True) + 1e-12)
    return centre * scale, scale


def norm_back(grad_normal, normal, scale):
    return scale * (
        grad_normal
        - jnp.mean(grad_normal, -1, keepdims=True)
        - normal * jnp.mean(grad_normal * normal, -1, keepdims=True)
    )


def column_sum(arr):
    return jnp.sum(arr.astype(F32), 0, keepdims=True)


def middle_kernel(
    mine, scale_ref, x_ref, att_ref, cot_ref, wo_ref, win_ref, wd_ref, vec_ref, bin_ref,
    out_ref, sum_ref, datt_ref, gboth_ref, gwd_ref, gvec_ref,
    gbin_ref, acc_wo, acc_win, acc_wd, act_ref, slope_ref,
):
    step = pl.program_id(0)
    width = x_ref.shape[1]
    hidden = win_ref.shape[1]
    chunks = hidden // width

    @pl.when(step == 0)
    def _():
        acc_wo[...] = jnp.zeros_like(acc_wo)
        acc_win[...] = jnp.zeros_like(acc_win)
        acc_wd[...] = jnp.zeros_like(acc_wd)
        gvec_ref[...] = jnp.zeros_like(gvec_ref)
        gbin_ref[...] = jnp.zeros_like(gbin_ref)

    vec = lambda row: vec_ref[row : row + 1, :]
    branch = dot(att_ref[...], wo_ref[...]) + vec(BO)
    normal_one, scale_one = norm_parts(x_ref[...].astype(F32) + branch)
    first = normal_one * vec(G1) + vec(S1)
    first_low = first.astype(BF16)
    second = first + vec(BD)
    for chunk in range(chunks):
        cols = slice(chunk * width, (chunk + 1) * width)
        pre = dot(first_low, win_ref[:, cols]) + bin_ref[:, cols]
        below = 0.5 + 0.5 * lax.erf(pre * 0.7071067811865476)
        act = (pre * below).astype(BF16)
        act_ref[:, cols] = act
        slope_ref[:, cols] = below + pre * (jnp.exp(pre * pre * -0.5) * 0.3989422804014327)
        second = second + dot(act, wd_ref[cols, :])
    normal_two, scale_two = norm_parts(second)
    out_ref[...] = (normal_two * vec(G2) + vec(S2)).astype(BF16)
    cot = cot_ref[...].astype(F32)
    gvec_ref[G2 : G2 + 1, :] += column_sum(cot * normal_two)
    gvec_ref[S2 : S2 + 1, :] += column_sum(cot)
    grad_second = norm_back(cot * vec(G2), normal_two, scale_two)
    grad_low = grad_second.astype(BF16)
    gvec_ref[BD : BD + 1, :] += column_sum(grad_low)
    first_t = jnp.transpose(first_low)
    grad_first = grad_second
    for chunk in range(chunks):
        cols = slice(chunk * width, (chunk + 1) * width)
        grad_pre = (slope_ref[:, cols] * dot_right(grad_low, wd_ref[cols, :])).astype(BF16)
        gbin_ref[:, cols] += column_sum(grad_pre)
        acc_wd[cols, :] += dot(jnp.transpose(act_ref[:, cols]), grad_low)
        acc_win[:, cols] += dot(first_t, grad_pre)
        grad_first = grad_first + dot_right(grad_pre, win_ref[:, cols])
    gvec_ref[G1 : G1 + 1, :] += column_sum(grad_first * normal_one)
    gvec_ref[S1 : S1 + 1, :] += column_sum(grad_first)
    grad_sum = norm_back(grad_first * vec(G1), normal_one, scale_one)
    sum_ref[...] = grad_sum
    grad_one = grad_sum.astype(BF16)
    gvec_ref[BO : BO + 1, :] += column_sum(grad_one)
    acc_wo[...] += dot(jnp.transpose(att_ref[...]), grad_one)
    datt_ref[...] = dot_right(grad_one, wo_ref[...]).astype(BF16)

    @pl.when(step == pl.num_programs(0) - 1)
    def _():
        weight = scale_ref[0]

        def cast(index, carry):
            here = pl.ds(0, hidden)
            for ref, acc, cols in (
                (gboth_ref, acc_win, here), (gboth_ref, acc_wo, pl.ds(hidden, width)), (gwd_ref, acc_wd, pl.ds(0, width)),
            ):
                size = acc.shape[0] // 24
                some = pl.ds(pl.multiple_of(index * size, size), size)
                ref[some, cols] = (acc[some, :] * weight).astype(BF16)
            return carry

        lax.fori_loop(0, 24, cast, 0)
        gvec_ref[...] = gvec_ref[...] * weight
        for row in range(VECTORS - BIN):
            for d in range(width // mine):
                start = (d * (VECTORS - BIN) + row) * mine
                piece = gbin_ref[:, start : start + mine] * weight
                gvec_ref[BIN + row : BIN + row + 1, d * mine : (d + 1) * mine] = piece


def middle(scale, rows, att, cot, w_out, w_in, w_down, vectors, b_in, mine):
    count, width = rows.shape
    hidden = w_down.shape[0]
    tile = 256
    last = w_out.shape[1] // width - 1
    whole = lambda shape: pl.BlockSpec(shape, lambda i: (0,) * len(shape), pipeline_mode=pl.Buffered(1))
    row = pl.BlockSpec((tile, width), lambda i: (i, 0))
    shape = jax.ShapeDtypeStruct
    return pl.pallas_call(
        partial(middle_kernel, mine),
        name="middle",
        grid=(count // tile,),
        in_specs=[pl.BlockSpec(memory_space=pltpu.SMEM), row, row, row]
        + [pl.BlockSpec((width, width), lambda i: (0, last), pipeline_mode=pl.Buffered(1)), whole((width, hidden))]
        + [whole(a.shape) for a in (w_down, vectors, b_in)],
        out_specs=[row, row, row]
        + [whole(s) for s in ((width, hidden + width), w_down.shape, (16, width))],
        out_shape=[
            shape((count, width), BF16),
            shape((count, width), F32),
            shape((count, width), BF16),
            shape((width, hidden + width), BF16),
            shape(w_down.shape, BF16),
            shape((16, width), F32),
        ],
        scratch_shapes=[
            pltpu.VMEM((1, hidden), F32),
            pltpu.VMEM((width, width), F32),
            pltpu.VMEM((width, hidden), F32),
            pltpu.VMEM(w_down.shape, F32),
            pltpu.VMEM((tile, hidden), BF16),
            pltpu.VMEM((tile, hidden), F32),
        ],
        compiler_params=pltpu.CompilerParams(vmem_limit_bytes=VMEM_BYTES),
        cost_estimate=pl.CostEstimate(flops=65_000_000_000, bytes_accessed=60_000_000, transcendentals=12_000_000),
    )(scale, rows, att, cot, w_out, w_in, w_down, vectors, b_in)


def backward_kernel(near, scale_ref, x_ref, qkv_ref, datt_ref, lse_ref, seg_ref, pad_ref, sum_ref, rest_ref, *refs):
    w_refs, refs = refs[:GROUPS], refs[GROUPS:]
    step = pl.program_id(0)
    length, width = x_ref.shape
    part = width // GROUPS
    half = width // HEADS
    steps = GROUPS * SEQS
    per = SCATTER_SLOTS
    last = per * steps + GROUPS * SEQS
    plan = {}
    if near:
        given, gx_ref, sums, refs = refs[:2], refs[2], refs[3:8], refs[8:]
        xt_ref, dqkv_ref, gvec_ref, mask_ref = refs[:4]
        terms = refs[4 : 4 + GROUPS]
        refs = refs[4 + GROUPS :]
        each = len(refs) // 5
        place = Place()
        jobs = [
            Scatter(place, t, sums[i], refs[each * i : each * (i + 1)], SCATTER_LINE_LAST[i])
            for i, t in enumerate(given + terms)
        ]
        plan = planned(SCATTER_TABLE, jobs)
    else:
        gx_ref, terms, refs = refs[0], refs[1 : 1 + GROUPS], refs[1 + GROUPS :]
        xt_ref, dqkv_ref, gvec_ref, mask_ref = refs

    @pl.when(step == 0)
    def _():
        if near:
            place.meet()
        gvec_ref[...] = jnp.zeros_like(gvec_ref)

    @pl.when(step < SEQS)
    def _():
        xt_ref[:, pl.ds(pl.multiple_of(step * length, length), length)] = jnp.transpose(x_ref[...])

    at = pl.multiple_of(step % SEQS * length, length)

    @pl.when(step < steps)
    def _():
        group = step // SEQS
        fill_mask(seg_ref, pad_ref, step % SEQS, mask_ref)
        first_half = lax.broadcasted_iota(jnp.int32, (1, 2 * half), 1) < half
        pairs = part // (2 * half)

        def back(pair):
            if near and pair < per:
                at_slot(per * step + pair, {s: e for s, e in plan.items() if s % per == pair and s < per * steps})
            base = pair * 2 * half
            pick = lambda ref, start: ref[:, pl.ds(start + base, 2 * half)]
            queries, keys, values = (pick(qkv_ref, third * part) for third in range(3))
            grads = pick(datt_ref, 0)
            keys_t = jnp.transpose(keys)
            keys = keys * jnp.asarray(0.125, BF16)
            grad_k = jnp.zeros(keys.shape, F32)
            grad_v = jnp.zeros(keys.shape, F32)
            grad_q = []
            for head in range(2):
                mine = first_half if head == 0 else ~first_half
                only = lambda arr: jnp.where(mine, arr, jnp.zeros_like(arr))
                scores = dot_right(only(keys), queries) + mask_ref[...]
                probs = jnp.exp(scores - lse_ref[0, pl.ds(2 * pair + head, 1), :])
                grad_probs = dot_right(only(values), grads)
                inner = jnp.sum(probs * grad_probs, 0, keepdims=True)
                grad_scores = (probs * (grad_probs - inner)).astype(BF16)
                grad_v = grad_v + dot(probs.astype(BF16), only(grads))
                grad_k = grad_k + dot(grad_scores, only(queries))
                grad_q.append(dot(keys_t[head * half : (head + 1) * half], grad_scores))
            grad_q = jnp.transpose(jnp.concatenate(grad_q, 0))
            for third, value in enumerate((grad_q * 0.125, grad_k * 0.125, grad_v)):
                dqkv_ref[group, pl.ds(at, length), pl.ds(third * part + base, 2 * half)] = value.astype(BF16)
                if third != 1:
                    row = BQ if third == 0 else BV
                    into = pl.ds(pl.multiple_of(group * part + base, 2 * half), 2 * half)
                    gvec_ref[row : row + 1, into] += column_sum(value.astype(BF16))

        for pair in range(pairs):
            back(pair)

    for group in range(GROUPS):

        @pl.when(step == group * SEQS + SEQS - 1)
        def _():
            for third in range(3):
                cols = slice(third * part, (third + 1) * part)
                grad = dot(xt_ref[...], dqkv_ref[group, :, cols]) * scale_ref[0]
                if near:
                    terms[group][:, :, cols] = grad.astype(BF16).reshape(*terms[group].shape[:2], part)
                else:
                    terms[group][:, cols] = grad.astype(BF16)

    @pl.when(step == steps - 1)
    def _():
        gvec_ref[:2] = gvec_ref[:2] * scale_ref[0]
        gvec_ref[2:VECTORS] = rest_ref[2:VECTORS]
        packed = jnp.transpose(gvec_ref[...]).astype(BF16)
        for start, value in ((width, packed), (width + 128, jnp.zeros_like(packed))):
            if near:
                blocks = value.reshape(*terms[-1].shape[:2], 128)
                terms[-1][:, :, start : start + 128] = blocks
            else:
                terms[-1][:, start : start + 128] = value

    @pl.when(step >= steps)
    def _():
        grad_x = sum_ref[...]
        for group in range(GROUPS):
            if near:
                here = {s - per * steps: e for s, e in plan.items() if per * steps <= s < last}
                at_slot(GROUPS * (step - steps) + group, {s: e for s, e in here.items() if s % GROUPS == group})
                grad_x = grad_x if group == 0 else gx_ref[...]
            grad_x = grad_x + dot_right(dqkv_ref[group, pl.ds(at, length), :], w_refs[group][...])
            if near or group == GROUPS - 1:
                gx_ref[...] = grad_x

    if near:

        @pl.when(step == steps + SEQS - 1)
        def _():
            run_now(plan, last)


def attention_backward(near, scale, rows, qkv, datt, lse, segments, pads, grad_sum, rest, w_groups, given):
    seqs, length = segments.shape
    count, width = rows.shape
    part = width // GROUPS
    steps = GROUPS * seqs
    whole = lambda shape: pl.BlockSpec(shape, lambda i: (0,) * len(shape), pipeline_mode=pl.Buffered(1))
    now = lambda i: jnp.minimum(i, steps - 1)
    tokens = whole((seqs, length))
    late = pl.BlockSpec((length, width), lambda i: (jnp.maximum(i - steps, 0), 0))
    shape = jax.ShapeDtypeStruct
    in_specs = [
        pl.BlockSpec(memory_space=pltpu.SMEM),
        pl.BlockSpec((length, width), lambda i: (jnp.minimum(i, seqs - 1), 0)),
        pl.BlockSpec((length, width), lambda i: (now(i) % seqs, now(i) // seqs)),
        pl.BlockSpec((length, part), lambda i: (now(i) % seqs, now(i) // seqs)),
        pl.BlockSpec((1, 8, length), lambda i: (now(i), 0, 0)),
        tokens,
        tokens,
        late,
        whole(rest.shape),
    ] + [whole((width, width))] * GROUPS
    scratch = [
        pltpu.VMEM((width, count), BF16),
        pltpu.VMEM((GROUPS, count, width), BF16),
        pltpu.VMEM((128, width), F32),
        pltpu.VMEM((length, length), F32),
    ]
    out_shape = [shape((count, width), F32)]
    remotely = {}
    if near:
        in_specs += [pl.BlockSpec(memory_space=pl.ANY)] * 2
        made = [(16, width // 16, width)] * (GROUPS - 1) + [(16, width // 16, width + 256)]
        scratch += [pltpu.VMEM(m, BF16) for m in made]
        every_shape = [g.shape for g in given] + made
        out_shape += [shape((s[1] // 2, s[2]), F32) for s in every_shape]
        for s, line_last in zip(every_shape, SCATTER_LINE_LAST):
            scratch += scatter_buffers(s[1], s[2], line_last)
        remotely = dict(collective_id=1, has_side_effects=True)
    else:
        out_shape += [shape((width, width), BF16)] * (GROUPS - 1) + [shape((width, width + 256), BF16)]
    return pl.pallas_call(
        partial(backward_kernel, near),
        name="attention_backward",
        grid=(steps + seqs,),
        in_specs=in_specs,
        out_specs=[late] + [whole(s.shape) for s in out_shape[1:]],
        out_shape=out_shape,
        scratch_shapes=scratch,
        compiler_params=pltpu.CompilerParams(vmem_limit_bytes=VMEM_BYTES, **remotely),
    )(scale, rows, qkv, datt, lse, segments, pads, grad_sum, rest, *w_groups, *given)


def join_groups(parts, width):
    part = width // GROUPS
    cut = [p[:, third * part : (third + 1) * part] for third in range(3) for p in parts]
    return jnp.concatenate(cut, 1)


def finish_kernel(wd_ref, both_ref, *refs):
    parts, outs = refs[:GROUPS], refs[GROUPS:]
    qkv_ref, o_wd, o_win, o_wo = outs[:4]
    width = parts[0].shape[1]
    part = width // GROUPS
    for third in range(3):
        for group in range(GROUPS):
            cols = slice(third * width + group * part, third * width + (group + 1) * part)
            qkv_ref[:, cols] = parts[group][:, third * part : (third + 1) * part]
    o_wd[...] = wd_ref[...]
    o_win[...] = both_ref[:, : o_win.shape[1]]
    o_wo[...] = both_ref[:, o_win.shape[1] :]
    small_ref = parts[-1].at[:, pl.ds(width, 128)]
    mine = small_ref.shape[0]
    square = jnp.concatenate([small_ref[...], jnp.zeros((128 - mine, 128), F32)], 0)
    vectors = jnp.transpose(square)
    for row in range(BIN):
        outs[4 + row][...] = vectors[row : row + 1, :mine]
    outs[4 + BIN][...] = jnp.concatenate([vectors[row : row + 1, :mine] for row in range(BIN, VECTORS)], 1)


def finish(sums):
    wd, both, *parts = sums
    mine, width = parts[0].shape
    shape = jax.ShapeDtypeStruct
    vmem = pl.BlockSpec(memory_space=pltpu.VMEM)
    outs = pl.pallas_call(
        finish_kernel,
        name="finish",
        in_specs=[vmem] * (2 + GROUPS),
        out_specs=[vmem] * (5 + BIN),
        out_shape=[shape((mine, 3 * width), F32)]
        + [shape(wd.shape, F32), shape((mine, both.shape[1] - width), F32), shape((mine, width), F32)]
        + [shape((1, mine), F32)] * BIN
        + [shape((1, (VECTORS - BIN) * mine), F32)],
    )(*sums)
    return outs[0], outs[1:4], [v.reshape(-1) for v in outs[4:]]


def body(
    hidden_in, out_grad, segment_ids, pad_mask, task_weight, w_qkv, b_query, b_value, w_out, b_out,
    gain_one, shift_one, w_in, b_in, w_down, b_down, gain_two, shift_two,
):
    seqs, length, width = hidden_in.shape
    mine = w_qkv.shape[0]
    part = width // GROUPS
    near = lax.axis_size("task") == 4 and lax.axis_size("batch") == 8 and mine % 8 == 0
    vectors = [b_query, b_value, b_out, gain_one, shift_one, b_down, gain_two, shift_two, b_in]
    rows = hidden_in.reshape(-1, width)
    if near:
        weights = [*vectors, w_qkv, w_out, w_in, w_down]
        qkv, att, lse, vectors, bin_full, *full = attention_forward(True, rows, segment_ids, pad_mask, weights)
    else:
        packed = jnp.transpose(jnp.concatenate(vectors).reshape(VECTORS, mine))
        packed = jnp.pad(packed, ((0, 0), (0, 256 - VECTORS)))
        cut = w_qkv.reshape(mine, 3, GROUPS, part)
        groups = [cut[:, :, g].reshape(mine, width) for g in range(GROUPS)]
        full = [lax.all_gather(w, AXES, axis=0, tiled=True) for w in (packed, *groups, w_in, w_down, w_out)]
        qkv, att, lse, vectors, bin_full = attention_forward(False, rows, segment_ids, pad_mask, full[:4])
        full = full[1:]
    *w_groups, win_full, wd_full = full[:5]
    wo_full = win_full if near else full[5]
    hidden_out, grad_sum, datt, g_both, g_wd, g_rest = middle(
        task_weight, rows, att, out_grad.reshape(-1, width), wo_full, win_full, wd_full, vectors, bin_full, mine
    )
    given = [g.reshape(16, -1, g.shape[1]) for g in (g_wd, g_both)] if near else []
    grad_x, *terms = attention_backward(
        near, task_weight, rows, qkv, datt, lse, segment_ids, pad_mask, grad_sum, g_rest, w_groups, given
    )
    if near:
        s_qkv, (s_wd, s_win, s_wo), s_vec = finish(terms)
    else:
        s_wd, both, *parts = [
            lax.psum_scatter(t, AXES, scatter_dimension=0, tiled=True).astype(F32) for t in (g_wd, g_both, *terms)
        ]
        s_win, s_wo = both[:, :-width], both[:, -width:]
        s_qkv = join_groups(parts, width)
        small = parts[-1][:, width:]
        s_vec = [small[:, row] for row in range(BIN)] + [jnp.transpose(small[:, BIN:VECTORS]).reshape(-1)]
    return (
        hidden_out.reshape(hidden_in.shape),
        grad_x.reshape(hidden_in.shape),
        s_qkv,
        s_vec[BQ],
        s_vec[BV],
        s_wo,
        s_vec[BO],
        s_vec[G1],
        s_vec[S1],
        s_win,
        s_vec[BIN],
        s_wd,
        s_vec[BD],
        s_vec[G2],
        s_vec[S2],
    )


def solution(mesh):
    seq, mat, vec = P(AXES, None, None), P(AXES, None), P(AXES)
    weights = (mat, vec, vec, mat, vec, vec, vec, mat, vec, mat, vec, vec, vec)
    return jax.shard_map(
        body,
        mesh=mesh,
        in_specs=(seq, seq, mat, mat, P("task")) + weights,
        out_specs=(seq, seq) + weights,
        check_vma=False,
    )
```

```python
from functools import partial

import jax
import jax.numpy as jnp
from jax import lax
from jax.experimental import pallas as pl
from jax.experimental.pallas import tpu as pltpu
from jax.sharding import PartitionSpec as P

HEADS = 12
GROUPS = 3
SEQS = 4
AXES = ("task", "batch")
F32 = jnp.float32
BF16 = jnp.bfloat16
VMEM_BYTES = 66_900_000
BQ, BV, BO, G1, S1, BD, G2, S2, BIN = range(9)
VECTORS = 12

GATHER_TABLE = [
    (0, 0, 0), (0, 1, 0), (0, 2, 0), (0, 0, 1), (0, 1, 1), (0, 2, 1), (0, 0, 2), (0, 0, 3), (0, 0, 4), (0, 0, 5),
    (0, 1, 2), (0, 1, 3), (0, 1, 4), (0, 1, 5), (0, 2, 2), (0, 2, 3), (0, 2, 4), (0, 2, 5), (0, 0, 6), (0, 0, 7),
    (0, 0, 8), (0, 0, 9), (0, 0, 10), (0, 0, 11), (0, 0, 12), (0, 1, 6), (0, 1, 9), (0, 1, 7), (0, 1, 8), (0, 1, 10),
    (0, 1, 11), (0, 1, 12), (0, 2, 6), (0, 2, 7), (0, 2, 8), (0, 2, 9), (0, 2, 10), (0, 4, 0), (0, 0, 13), (0, 0, 14),
    (0, 2, 11), (0, 2, 12), (0, 0, 15), (0, 0, 16), (0, 0, 17), (0, 0, 18), (0, 1, 13), (0, 1, 14), (0, 4, 1),
    (0, 0, 19), (0, 0, 20), (0, 1, 15), (0, 1, 16), (0, 1, 17), (0, 1, 18), (0, 2, 13), (0, 2, 14), (0, 3, 0),
    (0, 0, 21), (0, 0, 22), (0, 1, 19), (0, 1, 20), (0, 2, 17), (0, 2, 18), (0, 2, 15), (0, 2, 16), (0, 0, 23),
    (0, 2, 19), (0, 2, 20), (0, 3, 1), (0, 0, 24), (0, 0, 25), (0, 4, 2), (0, 4, 5), (0, 0, 26), (0, 0, 27),
    (0, 1, 21), (0, 1, 22), (0, 1, 23), (0, 1, 24), (0, 1, 25), (0, 1, 26), (0, 2, 21), (0, 2, 22), (0, 2, 26),
    (0, 4, 3), (0, 4, 4), (0, 0, 28), (0, 2, 23), (0, 2, 24), (0, 2, 25), (0, 3, 2), (0, 3, 3), (0, 3, 4), (0, 3, 5),
    (0, 0, 29), (1, 1, 27), (1, 1, 28), (1, 4, 6), (1, 4, 7), (1, 4, 8), (2, 1, 29), (2, 2, 27), (2, 2, 28),
    (2, 4, 9), (2, 4, 10), (2, 4, 11), (2, 4, 12), (3, 2, 29), (3, 3, 6), (3, 3, 7), (3, 3, 8), (3, 3, 10),
    (4, 4, 15), (4, 4, 16), (4, 3, 9), (4, 3, 11), (4, 3, 14), (5, 4, 13), (5, 4, 14), (5, 4, 19), (5, 4, 20),
    (6, 4, 17), (6, 4, 18), (6, 3, 12), (6, 3, 13), (7, 4, 23), (7, 4, 24), (7, 4, 25), (7, 4, 26), (7, 3, 15),
    (7, 3, 16), (7, 3, 17), (7, 3, 18), (7, 3, 21), (8, 4, 21), (8, 4, 22), (8, 3, 19), (8, 3, 20), (8, 3, 22),
    (8, 3, 23), (8, 3, 24), (9, 4, 27), (9, 4, 28), (9, 3, 25), (9, 3, 26), (10, 4, 29), (10, 3, 27), (10, 3, 28),
    (11, 3, 29),
]
SCATTER_TABLE = [
    (0, 1, 0), (1, 1, 1), (1, 0, 0), (2, 1, 2), (2, 1, 3), (2, 1, 4), (3, 1, 5), (3, 1, 6), (3, 1, 7), (3, 1, 8),
    (3, 0, 1), (3, 0, 2), (3, 0, 3), (3, 0, 4), (3, 1, 9), (3, 1, 10), (4, 2, 0), (4, 1, 11), (4, 1, 12), (4, 1, 15),
    (4, 1, 16), (4, 1, 17), (4, 1, 18), (5, 2, 1), (5, 2, 2), (5, 2, 3), (5, 2, 4), (5, 1, 13), (5, 1, 19),
    (5, 1, 20), (5, 1, 21), (5, 0, 5), (5, 0, 6), (6, 1, 14), (6, 1, 25), (6, 0, 7), (6, 0, 8), (6, 0, 9), (6, 0, 10),
    (7, 1, 22), (7, 1, 23), (7, 1, 26), (7, 0, 11), (7, 0, 15), (7, 0, 16), (7, 0, 17), (7, 0, 18), (8, 3, 0),
    (8, 2, 5), (8, 2, 6), (8, 2, 7), (8, 2, 8), (8, 2, 9), (8, 2, 10), (8, 2, 11), (8, 2, 12), (8, 1, 24), (8, 1, 27),
    (8, 1, 28), (8, 1, 29), (8, 0, 12), (8, 0, 19), (8, 0, 20), (8, 0, 21), (9, 3, 1), (9, 3, 2), (9, 3, 3),
    (9, 3, 4), (9, 2, 13), (9, 2, 14), (9, 2, 15), (9, 2, 16), (9, 2, 17), (9, 2, 18), (9, 2, 19), (9, 1, 30),
    (9, 0, 13), (9, 0, 14), (10, 3, 5), (10, 3, 6), (10, 3, 7), (10, 3, 8), (10, 3, 9), (10, 3, 10), (10, 3, 11),
    (10, 1, 31), (10, 1, 32), (10, 0, 22), (10, 0, 25), (10, 3, 12), (11, 3, 13), (11, 3, 14), (11, 3, 15),
    (11, 3, 16), (11, 3, 17), (11, 3, 18), (11, 3, 19), (11, 2, 20), (11, 1, 33), (11, 0, 23), (11, 0, 24),
    (11, 0, 26), (12, 4, 0), (12, 3, 20), (12, 3, 21), (12, 3, 22), (12, 2, 21), (12, 2, 22), (12, 2, 23),
    (12, 0, 27), (12, 0, 28), (12, 0, 29), (12, 0, 30), (14, 4, 1), (14, 4, 2), (15, 4, 3), (15, 4, 4), (15, 3, 23),
    (15, 2, 25), (16, 3, 24), (16, 2, 24), (16, 2, 26), (17, 4, 5), (18, 4, 6), (18, 4, 7), (18, 2, 27), (18, 0, 31),
    (18, 0, 32), (19, 4, 8), (19, 4, 9), (19, 3, 25), (19, 3, 26), (20, 4, 10), (20, 4, 11), (20, 0, 33), (21, 4, 12),
    (21, 4, 13), (21, 4, 14), (21, 3, 27), (22, 4, 15), (22, 4, 16), (22, 4, 17), (22, 4, 18), (23, 4, 19),
    (24, 4, 20), (24, 4, 21), (24, 4, 22), (24, 4, 23), (24, 4, 24), (24, 4, 25), (24, 4, 26), (24, 4, 27),
]
GATHER_LINE_FIRST = [False, False, False, True, False]
SCATTER_LINE_LAST = [False, False, True, True, True]
GATHER_SLOTS, SCATTER_SLOTS = 1, 1


MESH = pl.DeviceIdType.MESH


class Place:
    def __init__(self):
        self.task = lax.axis_index("task")
        self.batch = lax.axis_index("batch")
        self.core = self.batch % 2
        self.z = self.batch // 2
        x, y = self.task % 2, self.task // 2
        flip_x, flip_y = self.task + 1 - 2 * x, self.task + 2 - 4 * y
        self.task_a = (1 - self.core) * flip_x + self.core * flip_y
        self.task_b = (1 - self.core) * flip_y + self.core * flip_x
        self.task_ab = 3 - self.task
        self.partner = (self.task, self.batch + 1 - 2 * self.core)
        self.peer_a = (self.task_a, self.batch)
        self.peer_b = (self.task_b, self.batch)
        self.above = (self.task, self.batch + 2)
        self.below = (self.task, self.batch - 2)
        self.low = 1 - self.z // 2
        self.inner = self.low * self.z + (1 - self.low) * (3 - self.z)
        self.far = (self.task, self.batch + 4 * self.low - 2)
        self.near = (self.task, self.batch + 2 - 4 * self.low)

    def meet(self):
        barrier = pltpu.get_barrier_semaphore()
        for peer in (self.partner, self.peer_a, self.peer_b):
            pl.semaphore_signal(barrier, inc=1, device_id=peer, device_id_type=MESH)

        @pl.when(self.z < 3)
        def _():
            pl.semaphore_signal(barrier, inc=1, device_id=self.above, device_id_type=MESH)

        @pl.when(self.z > 0)
        def _():
            pl.semaphore_signal(barrier, inc=1, device_id=self.below, device_id_type=MESH)

        pl.semaphore_wait(barrier, 4 + self.z * (3 - self.z) // 2)


def remote(src, dst, send, recv, peer):
    return pltpu.make_async_remote_copy(src, dst, send, recv, device_id=peer, device_id_type=MESH)


GATHER_SEMS = [
    pltpu.SemaphoreType.DMA((12,)),
    pltpu.SemaphoreType.DMA((7,)),
    pltpu.SemaphoreType.DMA((14,)),
    pltpu.SemaphoreType.DMA((14,)),
    pltpu.SemaphoreType.DMA((6,)),
]


class Gather:
    def __init__(self, place, windows, full, sems, line_first=False):
        self.place, self.windows, self.full, self.line_first = place, windows, full, line_first
        self.send_z, self.send_a, self.recv, self.recv_b, self.misc = sems
        self.half = full.shape[1] // 2
        self.r = full.shape[0] // 32

    def rows(self, task, batch, count):
        return pl.ds(pl.multiple_of((task * 8 + batch) * self.r, 8), count * self.r)

    def cols(self, core):
        return pl.ds(pl.multiple_of(core * self.half, 128), self.half)

    def task(self, which):
        return self.place.task if which == 0 else self.place.task_a

    def level(self, spot):
        return self.place.z - spot if spot < 4 else self.place.z + spot - 3

    def here(self, spot):
        return self.place.z >= spot if spot < 4 else self.place.z + spot <= 6

    def chunk(self, task, spot):
        return self.full.at[self.rows(task, 2 * self.level(spot), 2), self.cols(self.place.core)]

    def begin(self):
        place, at = self.place, 0
        for window in self.windows:
            into = self.full.at[self.rows(place.task, place.batch, 1), pl.ds(at, window.shape[1])]
            pltpu.make_async_copy(window, into, self.misc.at[0]).start()
            remote(window, into, self.misc.at[1], self.misc.at[2], place.partner).start()
            at += window.shape[1]

    def along_z(self, which, spot, up):
        step = spot if up else max(spot - 3, 0)
        slot = which * 6 + step + (0 if up else 3)
        chunk = self.chunk(self.task(which), spot)
        into = which * 7 + step + (1 if up else 4)
        return remote(chunk, chunk, self.send_z.at[slot], self.recv.at[into], self.place.above if up else self.place.below)

    def along_a(self, spot):
        chunk = self.chunk(self.place.task, spot)
        return remote(chunk, chunk, self.send_a.at[spot], self.recv.at[7 + spot], self.place.peer_a)

    def along_b(self, which, spot):
        chunk = self.chunk(self.task(which), spot)
        return remote(chunk, chunk, self.misc.at[3], self.recv_b.at[which * 7 + spot], self.place.peer_b)

    def hand_over(self, task, spot):
        chunk = self.chunk(task, spot)
        remote(chunk, chunk, self.misc.at[4], self.misc.at[5], self.place.partner).start()

    def arrived(self, task, spot, sem):
        chunk = self.chunk(task, spot)
        remote(chunk, chunk, self.misc.at[1], sem, self.place.partner).wait_recv()

    def onward(self, which, spot):
        place = self.place
        if which == 0 or not self.line_first:
            for up in (True, False):
                if spot == 0 or (spot < 3 if up else 3 < spot < 6):
                    more = place.z < 3 if up else place.z > 0

                    @pl.when(more)
                    def _():
                        self.along_z(which, spot, up).start()

        if which == 0 and (spot == 0 or self.line_first):
            self.along_a(spot).start()
        self.along_b(which, spot).start()
        if which or spot:
            self.hand_over(self.task(which), spot)

    def spread(self):
        place = self.place
        mine = self.full.at[self.rows(place.task, place.batch, 1), :]
        pltpu.make_async_copy(mine, mine, self.misc.at[0]).wait()
        other = self.full.at[self.rows(place.task, place.partner[1], 1), :]
        remote(other, other, self.misc.at[1], self.misc.at[2], place.partner).wait_recv()
        self.onward(0, 0)

    def line(self, which, spot):
        @pl.when(self.here(spot))
        def _():
            self.arrived(self.task(which), spot, self.recv.at[which * 7 + spot])
            self.onward(which, spot)

    def from_b(self, which, spot):
        task = self.place.task_b if which == 0 else self.place.task_ab

        @pl.when(self.here(spot))
        def _():
            self.arrived(task, spot, self.recv_b.at[which * 7 + spot])
            self.hand_over(task, spot)

    def finish(self):
        place, full, r = self.place, self.full, self.r
        rest = full.at[pl.ds(0, 30 * r), self.cols(1 - place.core)]
        remote(rest, rest, self.misc.at[4], self.misc.at[5], place.partner).wait_recv()
        mine = full.at[pl.ds(0, 30 * r), self.cols(place.core)]
        remote(mine, mine, self.misc.at[4], self.misc.at[5], place.partner).wait_send()
        eight = full.at[pl.ds(0, 16 * r), self.cols(place.core)]
        remote(eight, eight, self.misc.at[3], self.recv_b.at[0], place.peer_b).wait_send()
        own = full.at[self.rows(place.task, place.batch, 1), :]
        remote(own, own, self.misc.at[1], self.misc.at[2], place.partner).wait_send()
        for spot in range(7 if self.line_first else 1):

            @pl.when(self.here(spot))
            def _():
                self.along_a(spot).wait_send()

        for which in range(1 if self.line_first else 2):
            for spot in (0, 1, 2):

                @pl.when(self.here(spot) & (place.z < 3))
                def _():
                    self.along_z(which, spot, True).wait_send()

            for spot in (0, 4, 5):

                @pl.when(self.here(spot) & (place.z > 0))
                def _():
                    self.along_z(which, spot, False).wait_send()

    def events(self):
        line, b = self.line, self.from_b
        out = [self.begin, self.spread]
        if self.line_first:
            out += [partial(line, 0, 1), partial(line, 0, 4), partial(line, 1, 0), partial(b, 0, 0)]
            out += [partial(line, 0, 2), partial(line, 0, 5), partial(line, 1, 1), partial(line, 1, 4)]
            out += [partial(b, 0, 1), partial(b, 0, 4), partial(line, 0, 3), partial(line, 0, 6), partial(b, 1, 0)]
            out += [partial(line, 1, 2), partial(line, 1, 5), partial(b, 0, 2), partial(b, 0, 5)]
            out += [partial(line, 1, 3), partial(line, 1, 6), partial(b, 1, 1), partial(b, 1, 4)]
            out += [partial(b, w, s) for w, s in ((0, 3), (0, 6), (1, 2), (1, 5), (1, 3), (1, 6))]
        else:
            out += [partial(line, 1, 0), partial(line, 0, 1), partial(line, 0, 4), partial(b, 0, 0), partial(b, 1, 0)]
            out += [partial(line, 1, 1), partial(line, 1, 4), partial(b, 0, 1), partial(b, 0, 4)]
            out += [partial(line, 0, 2), partial(line, 0, 5), partial(b, 1, 1), partial(b, 1, 4)]
            out += [partial(line, 1, 2), partial(line, 1, 5), partial(b, 0, 2), partial(b, 0, 5)]
            out += [partial(line, 0, 3), partial(line, 0, 6), partial(b, 1, 2), partial(b, 1, 5)]
            out += [partial(line, 1, 3), partial(line, 1, 6), partial(b, 0, 3), partial(b, 0, 6)]
            out += [partial(b, 1, 3), partial(b, 1, 6)]
        return out + [self.finish]


SCATTER_SEMS = [
    pltpu.SemaphoreType.DMA((4,)),
    pltpu.SemaphoreType.DMA((4,)),
    pltpu.SemaphoreType.DMA((4,)),
    pltpu.SemaphoreType.DMA((8,)),
    pltpu.SemaphoreType.DMA((8,)),
    pltpu.SemaphoreType.DMA((8,)),
    pltpu.SemaphoreType.DMA((10,)),
    pltpu.SemaphoreType.DMA((4,)),
    pltpu.SemaphoreType.DMA((4,)),
    pltpu.SemaphoreType.DMA((2,)),
]


def scatter_buffers(rows, cols, line_last=False):
    half = cols // 2
    return [
        pltpu.VMEM((16, rows, half), BF16),
        pltpu.VMEM((16, rows, half), BF16),
        pltpu.VMEM((8, rows, half), BF16),
        pltpu.VMEM((5 if line_last else 10, rows, half), BF16),
        pltpu.VMEM((4 if line_last else 1, rows, half), BF16),
        pltpu.VMEM((rows, half), F32),
        pltpu.VMEM((rows // 2, half), F32),
    ] + SCATTER_SEMS


class Scatter:
    def __init__(self, place, terms, out, buffers, line_last=False):
        self.place, self.terms, self.out, self.line_last = place, terms, out, line_last
        (self.own, self.other, self.got_b, self.got_z, self.got_a, self.total, self.got_f) = buffers[:7]
        (
            self.s_load, self.s_pair, self.r_pair, self.s_b, self.r_b, self.s_z, self.r_z, self.s_a, self.r_a, self.misc
        ) = buffers[7:]
        self.half = self.own.shape[2]
        self.tasks = (place.task_ab, place.task_b, place.task_a, place.task)
        self.tasks_partner = (place.task_ab, place.task_a, place.task_b, place.task)

    def cols(self, core):
        return pl.ds(pl.multiple_of(core * self.half, 128), self.half)

    def level(self, m):
        return self.place.low * m + (1 - self.place.low) * (3 - m)

    def load(self, index):
        first = self.tasks[index] * 4
        return pltpu.make_async_copy(
            self.terms.at[pl.ds(first, 4), :, self.cols(self.place.core)],
            self.own.at[pl.ds(first, 4)],
            self.s_load.at[index],
        )

    def pair(self, index, sent=True):
        first = (self.tasks_partner if sent else self.tasks)[index] * 4
        return remote(
            self.terms.at[pl.ds(first, 4), :, self.cols(1 - self.place.core)],
            self.other.at[pl.ds(first, 4)],
            self.s_pair.at[index],
            self.r_pair.at[index],
            self.place.partner,
        )

    def begin(self):
        for index in range(4):
            self.load(index).start()
            self.pair(index).start()

    def add(self, at, ref, where):
        size = 48 if self.half <= 512 else 16

        def some(index, carry):
            rows = pl.ds(pl.multiple_of(index * size, size), size)
            self.own[at, rows] = self.own[at, rows] + ref[where, rows]
            return carry

        lax.fori_loop(0, self.own.shape[1] // size, some, 0)

    def along_b(self, which, z):
        slot = which * 4 + z
        return remote(
            self.own.at[self.tasks[which] * 4 + z], self.got_b.at[slot], self.s_b.at[slot], self.r_b.at[slot],
            self.place.peer_b,
        )

    def add_pair(self, index):
        self.load(index).wait()
        self.pair(index, False).wait_recv()
        first = self.tasks[index] * 4

        def chunk(count, carry):
            z = self.level(3 - count)
            self.add(first + z, self.other, first + z)
            if index < 2:
                self.along_b(index, z).start()
            return carry

        lax.fori_loop(0, 4, chunk, 0)

    def add_b(self, which, m):
        z = self.level(m)
        self.along_b(which, z).wait_recv()
        self.add(self.tasks[2 + which] * 4 + z, self.got_b, which * 4 + z)
        if which == 0 and self.line_last:
            self.along_a(z).start()

    def along_z(self, which, m, far):
        place = self.place
        at = self.tasks[2 + which] * 4 + self.level(m)
        line = 0 if self.line_last else 5 * which
        into = line + ((1 - place.inner) * (m - 1) + place.inner * (6 - m) if far else 3 + m)
        peer = place.far if far else place.near
        return remote(self.own.at[at], self.got_z.at[into], self.s_z.at[which * 4 + m], self.r_z.at[into], peer)

    def add_z(self, which, m, slot):
        into = slot + (0 if self.line_last else 5 * which)
        got = self.got_z.at[into]
        remote(got, got, self.s_z.at[0], self.r_z.at[into], self.place.partner).wait_recv()
        self.add(self.tasks[2 + which] * 4 + self.level(m), self.got_z, into)

    def far_out(self, which, m):
        @pl.when(self.place.inner == 0)
        def _():
            self.along_z(which, m, True).start()

    def far_on(self, which, m):
        @pl.when(self.place.inner == 1)
        def _():
            self.add_z(which, m, m - 1)
            if m > 1:
                self.along_z(which, m, True).start()

    def near_on(self, which, m):
        @pl.when(self.place.inner == 1)
        def _():
            self.add_z(which, m, 3 + m)
            if m == 0:
                self.along_z(which, m, False).start()

    def near_in(self, which):
        @pl.when(self.place.inner == 0)
        def _():
            self.add_z(which, 0, 3)

    def along_a(self, z):
        slot = z if self.line_last else 0
        return remote(
            self.own.at[self.tasks[2] * 4 + z], self.got_a.at[slot], self.s_a.at[slot], self.r_a.at[slot],
            self.place.peer_a,
        )

    def to_a(self):
        self.along_a(self.place.z).start()

    def add_a(self, m):
        z = self.level(m)
        self.along_a(z).wait_recv()
        self.add(self.tasks[3] * 4 + z, self.got_a, z)

    def last(self):
        rows = self.got_f.shape[0]
        away = pl.multiple_of((1 - self.place.core) * rows, rows)
        return remote(
            self.total.at[pl.ds(away, rows)], self.got_f, self.misc.at[0], self.misc.at[1], self.place.partner
        )

    def close(self):
        total = self.own[self.tasks[3] * 4 + self.place.z].astype(F32)
        if not self.line_last:
            self.along_a(self.place.z).wait_recv()
            total = total + self.got_a[0].astype(F32)
        self.total[...] = total
        self.last().start()

    def finish(self):
        rows = self.got_f.shape[0]
        core = self.place.core
        self.last().wait_recv()
        self.out[:, self.cols(core)] = self.total[pl.ds(pl.multiple_of(core * rows, rows), rows), :]
        self.out[:, self.cols(1 - core)] = self.got_f[...]
        for index in range(4):
            self.pair(index).wait_send()
        for which in range(2):
            for z in range(4):
                self.along_b(which, z).wait_send()
        for which in range(1 if self.line_last else 0, 2):
            for m in range(4):

                @pl.when(self.place.inner < m)
                def _():
                    self.along_z(which, m, True).wait_send()

                @pl.when(self.place.inner > m)
                def _():
                    self.along_z(which, m, False).wait_send()

        for z in range(4 if self.line_last else 1):
            self.along_a(z if self.line_last else self.place.z).wait_send()
        self.last().wait_send()

    def events(self):
        out = [self.begin] + [partial(self.add_pair, i) for i in range(4)]
        if self.line_last:
            out += [partial(self.add_b, which, m) for which in range(2) for m in (3, 2, 1, 0)]
            for m in (3, 2, 1):
                out += [partial(self.add_a, m), partial(self.far_out, 1, m)]
            out.append(partial(self.add_a, 0))
            out += [partial(self.far_on, 1, m) for m in (3, 2, 1)]
            out += [partial(self.near_on, 1, 0), partial(self.near_on, 1, 1), partial(self.near_in, 1)]
        else:
            for which in range(2):
                for m in (3, 2, 1):
                    out += [partial(self.add_b, which, m), partial(self.far_out, which, m)]
                out.append(partial(self.add_b, which, 0))
                out += [partial(self.far_on, which, m) for m in (3, 2, 1)]
            for which in range(2):
                out += [partial(self.near_on, which, 0), partial(self.near_on, which, 1), partial(self.near_in, which)]
                if which == 0:
                    out.append(self.to_a)
        return out + [self.close, self.finish]


def dot(left, right):
    return lax.dot_general(left, right, (((1,), (0,)), ((), ())), preferred_element_type=F32)


def dot_right(left, right):
    return lax.dot_general(left, right, (((1,), (1,)), ((), ())), preferred_element_type=F32)


def at_slot(slot, plan):
    def choose(slots):
        if len(slots) == 1:

            @pl.when(slot == slots[0])
            def _():
                for event in plan[slots[0]]:
                    event()

            return
        middle_slot = slots[len(slots) // 2]

        @pl.when(slot < middle_slot)
        def _():
            choose(slots[: len(slots) // 2])

        @pl.when(slot >= middle_slot)
        def _():
            choose(slots[len(slots) // 2 :])

    if plan:
        choose(sorted(plan))


def fill_mask(seg_ref, pad_ref, row, mask_ref):
    length = mask_ref.shape[0]
    seg_row = seg_ref[pl.ds(row, 1), :].astype(F32)
    pad_row = pad_ref[pl.ds(row, 1), :].astype(F32)
    seg_col = jnp.transpose(jnp.broadcast_to(seg_row, (128, length)))
    pad_col = jnp.transpose(jnp.broadcast_to(pad_row, (128, length)))
    key_at = lax.broadcasted_iota(jnp.int32, (length, 128), 0)
    lane = lax.broadcasted_iota(jnp.int32, (length, 128), 1)
    for block in range(length // 128):
        same = seg_col == seg_row[:, 128 * block : 128 * block + 128]
        seen = (pad_col == 1.0) | (key_at == lane + 128 * block)
        mask_ref[:, 128 * block : 128 * block + 128] = jnp.where(same & seen, 0.0, -1e30)


def planned(table, jobs):
    plan = {}
    events = [job.events() for job in jobs]
    for slot, job, event in table:
        plan.setdefault(slot, []).append(events[job][event])
    return plan


def run_now(plan, slot):
    for event in plan.get(slot, []):
        event()


def forward_kernel(near, devices, x_ref, seg_ref, pad_ref, *refs):
    if near:
        vector_refs, refs = refs[: BIN + 1], refs[BIN + 1 :]
        wqkv_ref, wo_ref, win_ref, wd_ref = refs[:4]
        qkv_ref, att_ref, lse_ref, vec_ref, bin_ref = refs[4:9]
        fulls = refs[9:14]
        mask_ref, w_ref, small_ref, load_sem, shard_ref, square_ref = refs[14:20]
        sems = refs[20:]
    else:
        small, *groups = [ref.at[:, pl.ds(0, size)] for ref, size in zip(refs[:4], (128, 768, 768, 768))]
        qkv_ref, att_ref, lse_ref, vec_ref, bin_ref = refs[4:9]
        mask_ref, w_ref, small_ref, load_sem = refs[9:]
    step = pl.program_id(0)
    length, width = x_ref.shape
    part = width // GROUPS
    half = width // HEADS
    steps = GROUPS * SEQS
    per = GATHER_SLOTS
    last = per * steps
    plan = {}
    if near:
        groups = [fulls[0].at[:, pl.ds(0, width)], *fulls[1:GROUPS]]
        small = fulls[0].at[:, pl.ds(width, 128)]
        place = Place()
        windows = []
        for group in range(GROUPS):
            windows.append([wqkv_ref.at[:, pl.ds(third * width + group * part, part)] for third in range(3)])
        windows[0].append(shard_ref)
        windows += [[win_ref, wo_ref], [wd_ref]]
        jobs = [
            Gather(place, w, fulls[i], sems[5 * i : 5 * i + 5], GATHER_LINE_FIRST[i]) for i, w in enumerate(windows)
        ]
        plan = planned(GATHER_TABLE, jobs)

    @pl.when(step == 0)
    def _():
        if near:
            mine = shard_ref.shape[0]
            square_ref[...] = jnp.zeros_like(square_ref)
            for row, ref in enumerate(vector_refs):
                vector = ref[...].astype(F32).reshape(1, ref.shape[0])
                for j in range(ref.shape[0] // mine):
                    square_ref[row + j : row + j + 1, :mine] = vector[:, j * mine : (j + 1) * mine]
            shard_ref[:, :128] = jnp.transpose(square_ref[...])[:mine].astype(BF16)
            shard_ref[:, 128:] = jnp.zeros((shard_ref.shape[0], 128), BF16)
            place.meet()
            run_now(plan, 0)
        copy = pltpu.make_async_copy(small, small_ref, load_sem.at[0])
        copy.start()
        copy.wait()
        vec_ref[...] = jnp.transpose(small_ref[...].astype(F32))[:16]
        mine = small_ref.shape[0] // devices
        for d in range(devices):
            for j in range(VECTORS - BIN):
                start = (d * (VECTORS - BIN) + j) * mine
                bin_ref[:, start : start + mine] = vec_ref[BIN + j : BIN + j + 1, d * mine : (d + 1) * mine]

    if near:
        at_slot(per * step, {s: e for s, e in plan.items() if s % per == 0 and 0 < s < last})
    for group in range(GROUPS):

        @pl.when(step == group * SEQS)
        def _():
            copy = pltpu.make_async_copy(groups[group], w_ref, load_sem.at[1])
            copy.start()
            copy.wait()

    fill_mask(seg_ref, pad_ref, step % SEQS, mask_ref)
    at = pl.multiple_of(step // SEQS * part, part)
    for third, row in enumerate((BQ, None, BV)):
        cols = slice(third * part, (third + 1) * part)
        product = dot(x_ref[...], w_ref[:, cols])
        if row is not None:
            product = product + vec_ref[row : row + 1, pl.ds(at, part)]
        qkv_ref[:, cols] = product.astype(BF16)
    first_half = lax.broadcasted_iota(jnp.int32, (1, 2 * half), 1) < half
    pairs = part // (2 * half)

    def attend(pair):
        if near and 0 < pair < per:
            at_slot(per * step + pair, {s: e for s, e in plan.items() if s % per == pair and s < last})
        base = pair * 2 * half
        queries = qkv_ref[:, pl.ds(base, 2 * half)]
        keys = qkv_ref[:, pl.ds(part + base, 2 * half)] * jnp.asarray(0.125, BF16)
        values_t = jnp.transpose(qkv_ref[:, pl.ds(2 * part + base, 2 * half)])
        outs = []
        for head in range(2):
            mine = first_half if head == 0 else ~first_half
            scores = dot_right(jnp.where(mine, keys, jnp.zeros_like(keys)), queries) + mask_ref[...]
            top = jnp.max(scores, 0, keepdims=True)
            expo = jnp.exp(scores - top)
            total = jnp.sum(expo, 0, keepdims=True)
            probs = (expo * (1.0 / total)).astype(BF16)
            outs.append(dot(values_t[head * half : (head + 1) * half], probs))
            lse_ref[0, pl.ds(2 * pair + head, 1), :] = top + jnp.log(total)
        att_ref[:, pl.ds(base, 2 * half)] = jnp.transpose(jnp.concatenate(outs, 0)).astype(BF16)

    for pair in range(pairs):
        attend(pair)
    if near:

        @pl.when(step == steps - 1)
        def _():
            run_now(plan, last)


def attention_forward(near, rows, segments, pads, weights):
    seqs, length = segments.shape
    width = rows.shape[1]
    part = width // GROUPS
    anywhere = lambda count: [pl.BlockSpec(memory_space=pl.ANY)] * count
    tokens = pl.BlockSpec((seqs, length), lambda i: (0, 0))
    shape = jax.ShapeDtypeStruct
    out_specs = [
        pl.BlockSpec((length, width), lambda i: (i % seqs, i // seqs)),
        pl.BlockSpec((length, part), lambda i: (i % seqs, i // seqs)),
        pl.BlockSpec((1, 8, length), lambda i: (i, 0, 0)),
        pl.BlockSpec((16, width), lambda i: (0, 0)),
        pl.BlockSpec((1, (VECTORS - BIN) * width), lambda i: (0, 0)),
    ]
    out_shape = [
        shape((rows.shape[0], 3 * width), BF16),
        shape((rows.shape[0], width), BF16),
        shape((GROUPS * seqs, 8, length), F32),
        shape((16, width), F32),
        shape((1, (VECTORS - BIN) * width), F32),
    ]
    in_specs = [pl.BlockSpec((length, width), lambda i: (i % seqs, 0)), tokens, tokens]
    scratch = [
        pltpu.VMEM((length, length), F32),
        pltpu.VMEM((width, width), BF16),
        pltpu.VMEM((width, 128), BF16),
        pltpu.SemaphoreType.DMA((2,)),
    ]
    remotely = {}
    if near:
        *vectors, w_qkv, w_out, w_in, w_down = weights
        in_specs += [pl.BlockSpec(v.shape, lambda i: (0,)) for v in vectors]
        in_specs += [pl.BlockSpec(w.shape, lambda i: (0, 0)) for w in (w_qkv, w_out, w_in, w_down)]
        mine = w_qkv.shape[0]
        fulls = [(mine, width + 256)] + [(mine, width)] * (GROUPS - 1)
        fulls += [(mine, w_in.shape[1] + w_out.shape[1]), w_down.shape]
        out_specs += anywhere(5)
        out_shape += [shape((32 * r, c), BF16) for r, c in fulls]
        scratch += [pltpu.VMEM((mine, 256), BF16), pltpu.VMEM((128, 128), F32)] + GATHER_SEMS * 5
        remotely = dict(collective_id=0, has_side_effects=True)
    else:
        in_specs += anywhere(4)
    return pl.pallas_call(
        partial(forward_kernel, near, lax.axis_size(AXES)),
        name="attention_forward",
        grid=(GROUPS * seqs,),
        in_specs=in_specs,
        out_specs=out_specs,
        out_shape=out_shape,
        scratch_shapes=scratch,
        compiler_params=pltpu.CompilerParams(vmem_limit_bytes=VMEM_BYTES, **remotely),
    )(rows, segments, pads, *weights)


def norm_parts(arr):
    centre = arr - jnp.mean(arr, -1, keepdims=True)
    scale = lax.rsqrt(jnp.mean(centre * centre, -1, keepdims=True) + 1e-12)
    return centre * scale, scale


def norm_back(grad_normal, normal, scale):
    return scale * (
        grad_normal
        - jnp.mean(grad_normal, -1, keepdims=True)
        - normal * jnp.mean(grad_normal * normal, -1, keepdims=True)
    )


def column_sum(arr):
    return jnp.sum(arr.astype(F32), 0, keepdims=True)


def middle_kernel(
    mine, scale_ref, x_ref, att_ref, cot_ref, wo_ref, win_ref, wd_ref, vec_ref, bin_ref,
    out_ref, sum_ref, datt_ref, gboth_ref, gwd_ref, gvec_ref,
    gbin_ref, acc_wo, acc_win, acc_wd, act_ref, slope_ref,
):
    step = pl.program_id(0)
    width = x_ref.shape[1]
    hidden = win_ref.shape[1]
    chunks = hidden // width

    @pl.when(step == 0)
    def _():
        acc_wo[...] = jnp.zeros_like(acc_wo)
        acc_win[...] = jnp.zeros_like(acc_win)
        acc_wd[...] = jnp.zeros_like(acc_wd)
        gvec_ref[...] = jnp.zeros_like(gvec_ref)
        gbin_ref[...] = jnp.zeros_like(gbin_ref)

    vec = lambda row: vec_ref[row : row + 1, :]
    branch = dot(att_ref[...], wo_ref[...]) + vec(BO)
    normal_one, scale_one = norm_parts(x_ref[...].astype(F32) + branch)
    first = normal_one * vec(G1) + vec(S1)
    first_low = first.astype(BF16)
    second = first + vec(BD)
    for chunk in range(chunks):
        cols = slice(chunk * width, (chunk + 1) * width)
        pre = dot(first_low, win_ref[:, cols]) + bin_ref[:, cols]
        below = 0.5 + 0.5 * lax.erf(pre * 0.7071067811865476)
        act = (pre * below).astype(BF16)
        act_ref[:, cols] = act
        slope_ref[:, cols] = below + pre * (jnp.exp(pre * pre * -0.5) * 0.3989422804014327)
        second = second + dot(act, wd_ref[cols, :])
    normal_two, scale_two = norm_parts(second)
    out_ref[...] = (normal_two * vec(G2) + vec(S2)).astype(BF16)
    cot = cot_ref[...].astype(F32)
    gvec_ref[G2 : G2 + 1, :] += column_sum(cot * normal_two)
    gvec_ref[S2 : S2 + 1, :] += column_sum(cot)
    grad_second = norm_back(cot * vec(G2), normal_two, scale_two)
    grad_low = grad_second.astype(BF16)
    gvec_ref[BD : BD + 1, :] += column_sum(grad_low)
    first_t = jnp.transpose(first_low)
    grad_first = grad_second
    for chunk in range(chunks):
        cols = slice(chunk * width, (chunk + 1) * width)
        grad_pre = (slope_ref[:, cols] * dot_right(grad_low, wd_ref[cols, :])).astype(BF16)
        gbin_ref[:, cols] += column_sum(grad_pre)
        acc_wd[cols, :] += dot(jnp.transpose(act_ref[:, cols]), grad_low)
        acc_win[:, cols] += dot(first_t, grad_pre)
        grad_first = grad_first + dot_right(grad_pre, win_ref[:, cols])
    gvec_ref[G1 : G1 + 1, :] += column_sum(grad_first * normal_one)
    gvec_ref[S1 : S1 + 1, :] += column_sum(grad_first)
    grad_sum = norm_back(grad_first * vec(G1), normal_one, scale_one)
    sum_ref[...] = grad_sum
    grad_one = grad_sum.astype(BF16)
    gvec_ref[BO : BO + 1, :] += column_sum(grad_one)
    acc_wo[...] += dot(jnp.transpose(att_ref[...]), grad_one)
    datt_ref[...] = dot_right(grad_one, wo_ref[...]).astype(BF16)

    @pl.when(step == pl.num_programs(0) - 1)
    def _():
        weight = scale_ref[0]

        def cast(index, carry):
            here = pl.ds(0, hidden)
            for ref, acc, cols in (
                (gboth_ref, acc_win, here), (gboth_ref, acc_wo, pl.ds(hidden, width)), (gwd_ref, acc_wd, pl.ds(0, width)),
            ):
                size = acc.shape[0] // 24
                some = pl.ds(pl.multiple_of(index * size, size), size)
                ref[some, cols] = (acc[some, :] * weight).astype(BF16)
            return carry

        lax.fori_loop(0, 24, cast, 0)
        gvec_ref[...] = gvec_ref[...] * weight
        for row in range(VECTORS - BIN):
            for d in range(width // mine):
                start = (d * (VECTORS - BIN) + row) * mine
                piece = gbin_ref[:, start : start + mine] * weight
                gvec_ref[BIN + row : BIN + row + 1, d * mine : (d + 1) * mine] = piece


def middle(scale, rows, att, cot, w_out, w_in, w_down, vectors, b_in, mine):
    count, width = rows.shape
    hidden = w_down.shape[0]
    tile = 256
    last = w_out.shape[1] // width - 1
    whole = lambda shape: pl.BlockSpec(shape, lambda i: (0,) * len(shape), pipeline_mode=pl.Buffered(1))
    row = pl.BlockSpec((tile, width), lambda i: (i, 0))
    shape = jax.ShapeDtypeStruct
    return pl.pallas_call(
        partial(middle_kernel, mine),
        name="middle",
        grid=(count // tile,),
        in_specs=[pl.BlockSpec(memory_space=pltpu.SMEM), row, row, row]
        + [pl.BlockSpec((width, width), lambda i: (0, last), pipeline_mode=pl.Buffered(1)), whole((width, hidden))]
        + [whole(a.shape) for a in (w_down, vectors, b_in)],
        out_specs=[row, row, row]
        + [whole(s) for s in ((width, hidden + width), w_down.shape, (16, width))],
        out_shape=[
            shape((count, width), BF16),
            shape((count, width), F32),
            shape((count, width), BF16),
            shape((width, hidden + width), BF16),
            shape(w_down.shape, BF16),
            shape((16, width), F32),
        ],
        scratch_shapes=[
            pltpu.VMEM((1, hidden), F32),
            pltpu.VMEM((width, width), F32),
            pltpu.VMEM((width, hidden), F32),
            pltpu.VMEM(w_down.shape, F32),
            pltpu.VMEM((tile, hidden), BF16),
            pltpu.VMEM((tile, hidden), F32),
        ],
        compiler_params=pltpu.CompilerParams(vmem_limit_bytes=VMEM_BYTES),
        cost_estimate=pl.CostEstimate(flops=65_000_000_000, bytes_accessed=60_000_000, transcendentals=12_000_000),
    )(scale, rows, att, cot, w_out, w_in, w_down, vectors, b_in)


def backward_kernel(near, scale_ref, x_ref, qkv_ref, datt_ref, lse_ref, seg_ref, pad_ref, sum_ref, rest_ref, *refs):
    w_refs, refs = refs[:GROUPS], refs[GROUPS:]
    step = pl.program_id(0)
    length, width = x_ref.shape
    part = width // GROUPS
    half = width // HEADS
    steps = GROUPS * SEQS
    per = SCATTER_SLOTS
    last = per * steps + GROUPS * SEQS
    plan = {}
    if near:
        given, gx_ref, sums, refs = refs[:2], refs[2], refs[3:8], refs[8:]
        xt_ref, dqkv_ref, gvec_ref, mask_ref = refs[:4]
        terms = refs[4 : 4 + GROUPS]
        refs = refs[4 + GROUPS :]
        each = len(refs) // 5
        place = Place()
        jobs = [
            Scatter(place, t, sums[i], refs[each * i : each * (i + 1)], SCATTER_LINE_LAST[i])
            for i, t in enumerate(given + terms)
        ]
        plan = planned(SCATTER_TABLE, jobs)
    else:
        gx_ref, terms, refs = refs[0], refs[1 : 1 + GROUPS], refs[1 + GROUPS :]
        xt_ref, dqkv_ref, gvec_ref, mask_ref = refs

    @pl.when(step == 0)
    def _():
        if near:
            place.meet()
        gvec_ref[...] = jnp.zeros_like(gvec_ref)

    @pl.when(step < SEQS)
    def _():
        xt_ref[:, pl.ds(pl.multiple_of(step * length, length), length)] = jnp.transpose(x_ref[...])

    at = pl.multiple_of(step % SEQS * length, length)

    @pl.when(step < steps)
    def _():
        group = step // SEQS
        fill_mask(seg_ref, pad_ref, step % SEQS, mask_ref)
        first_half = lax.broadcasted_iota(jnp.int32, (1, 2 * half), 1) < half
        pairs = part // (2 * half)

        def back(pair):
            if near and pair < per:
                at_slot(per * step + pair, {s: e for s, e in plan.items() if s % per == pair and s < per * steps})
            base = pair * 2 * half
            pick = lambda ref, start: ref[:, pl.ds(start + base, 2 * half)]
            queries, keys, values = (pick(qkv_ref, third * part) for third in range(3))
            grads = pick(datt_ref, 0)
            keys_t = jnp.transpose(keys)
            keys = keys * jnp.asarray(0.125, BF16)
            grad_k = jnp.zeros(keys.shape, F32)
            grad_v = jnp.zeros(keys.shape, F32)
            grad_q = []
            for head in range(2):
                mine = first_half if head == 0 else ~first_half
                only = lambda arr: jnp.where(mine, arr, jnp.zeros_like(arr))
                scores = dot_right(only(keys), queries) + mask_ref[...]
                probs = jnp.exp(scores - lse_ref[0, pl.ds(2 * pair + head, 1), :])
                grad_probs = dot_right(only(values), grads)
                inner = jnp.sum(probs * grad_probs, 0, keepdims=True)
                grad_scores = (probs * (grad_probs - inner)).astype(BF16)
                grad_v = grad_v + dot(probs.astype(BF16), only(grads))
                grad_k = grad_k + dot(grad_scores, only(queries))
                grad_q.append(dot(keys_t[head * half : (head + 1) * half], grad_scores))
            grad_q = jnp.transpose(jnp.concatenate(grad_q, 0))
            for third, value in enumerate((grad_q * 0.125, grad_k * 0.125, grad_v)):
                dqkv_ref[group, pl.ds(at, length), pl.ds(third * part + base, 2 * half)] = value.astype(BF16)
                if third != 1:
                    row = BQ if third == 0 else BV
                    into = pl.ds(pl.multiple_of(group * part + base, 2 * half), 2 * half)
                    gvec_ref[row : row + 1, into] += column_sum(value.astype(BF16))

        for pair in range(pairs):
            back(pair)

    for group in range(GROUPS):

        @pl.when(step == group * SEQS + SEQS - 1)
        def _():
            for third in range(3):
                cols = slice(third * part, (third + 1) * part)
                grad = dot(xt_ref[...], dqkv_ref[group, :, cols]) * scale_ref[0]
                if near:
                    terms[group][:, :, cols] = grad.astype(BF16).reshape(*terms[group].shape[:2], part)
                else:
                    terms[group][:, cols] = grad.astype(BF16)

    @pl.when(step == steps - 1)
    def _():
        gvec_ref[:2] = gvec_ref[:2] * scale_ref[0]
        gvec_ref[2:VECTORS] = rest_ref[2:VECTORS]
        packed = jnp.transpose(gvec_ref[...]).astype(BF16)
        for start, value in ((width, packed), (width + 128, jnp.zeros_like(packed))):
            if near:
                blocks = value.reshape(*terms[-1].shape[:2], 128)
                terms[-1][:, :, start : start + 128] = blocks
            else:
                terms[-1][:, start : start + 128] = value

    @pl.when(step >= steps)
    def _():
        grad_x = sum_ref[...]
        for group in range(GROUPS):
            if near:
                here = {s - per * steps: e for s, e in plan.items() if per * steps <= s < last}
                at_slot(GROUPS * (step - steps) + group, {s: e for s, e in here.items() if s % GROUPS == group})
                grad_x = grad_x if group == 0 else gx_ref[...]
            grad_x = grad_x + dot_right(dqkv_ref[group, pl.ds(at, length), :], w_refs[group][...])
            if near or group == GROUPS - 1:
                gx_ref[...] = grad_x

    if near:

        @pl.when(step == steps + SEQS - 1)
        def _():
            run_now(plan, last)


def attention_backward(near, scale, rows, qkv, datt, lse, segments, pads, grad_sum, rest, w_groups, given):
    seqs, length = segments.shape
    count, width = rows.shape
    part = width // GROUPS
    steps = GROUPS * seqs
    whole = lambda shape: pl.BlockSpec(shape, lambda i: (0,) * len(shape), pipeline_mode=pl.Buffered(1))
    now = lambda i: jnp.minimum(i, steps - 1)
    tokens = whole((seqs, length))
    late = pl.BlockSpec((length, width), lambda i: (jnp.maximum(i - steps, 0), 0))
    shape = jax.ShapeDtypeStruct
    in_specs = [
        pl.BlockSpec(memory_space=pltpu.SMEM),
        pl.BlockSpec((length, width), lambda i: (jnp.minimum(i, seqs - 1), 0)),
        pl.BlockSpec((length, width), lambda i: (now(i) % seqs, now(i) // seqs)),
        pl.BlockSpec((length, part), lambda i: (now(i) % seqs, now(i) // seqs)),
        pl.BlockSpec((1, 8, length), lambda i: (now(i), 0, 0)),
        tokens,
        tokens,
        late,
        whole(rest.shape),
    ] + [whole((width, width))] * GROUPS
    scratch = [
        pltpu.VMEM((width, count), BF16),
        pltpu.VMEM((GROUPS, count, width), BF16),
        pltpu.VMEM((128, width), F32),
        pltpu.VMEM((length, length), F32),
    ]
    out_shape = [shape((count, width), F32)]
    remotely = {}
    if near:
        in_specs += [pl.BlockSpec(memory_space=pl.ANY)] * 2
        made = [(16, width // 16, width)] * (GROUPS - 1) + [(16, width // 16, width + 256)]
        scratch += [pltpu.VMEM(m, BF16) for m in made]
        every_shape = [g.shape for g in given] + made
        out_shape += [shape((s[1] // 2, s[2]), F32) for s in every_shape]
        for s, line_last in zip(every_shape, SCATTER_LINE_LAST):
            scratch += scatter_buffers(s[1], s[2], line_last)
        remotely = dict(collective_id=1, has_side_effects=True)
    else:
        out_shape += [shape((width, width), BF16)] * (GROUPS - 1) + [shape((width, width + 256), BF16)]
    return pl.pallas_call(
        partial(backward_kernel, near),
        name="attention_backward",
        grid=(steps + seqs,),
        in_specs=in_specs,
        out_specs=[late] + [whole(s.shape) for s in out_shape[1:]],
        out_shape=out_shape,
        scratch_shapes=scratch,
        compiler_params=pltpu.CompilerParams(vmem_limit_bytes=VMEM_BYTES, **remotely),
    )(scale, rows, qkv, datt, lse, segments, pads, grad_sum, rest, *w_groups, *given)


def join_groups(parts, width):
    part = width // GROUPS
    cut = [p[:, third * part : (third + 1) * part] for third in range(3) for p in parts]
    return jnp.concatenate(cut, 1)


def finish_kernel(wd_ref, both_ref, *refs):
    parts, outs = refs[:GROUPS], refs[GROUPS:]
    qkv_ref, o_wd, o_win, o_wo = outs[:4]
    width = parts[0].shape[1]
    part = width // GROUPS
    for third in range(3):
        for group in range(GROUPS):
            cols = slice(third * width + group * part, third * width + (group + 1) * part)
            qkv_ref[:, cols] = parts[group][:, third * part : (third + 1) * part]
    o_wd[...] = wd_ref[...]
    o_win[...] = both_ref[:, : o_win.shape[1]]
    o_wo[...] = both_ref[:, o_win.shape[1] :]
    small_ref = parts[-1].at[:, pl.ds(width, 128)]
    mine = small_ref.shape[0]
    square = jnp.concatenate([small_ref[...], jnp.zeros((128 - mine, 128), F32)], 0)
    vectors = jnp.transpose(square)
    for row in range(BIN):
        outs[4 + row][...] = vectors[row : row + 1, :mine]
    outs[4 + BIN][...] = jnp.concatenate([vectors[row : row + 1, :mine] for row in range(BIN, VECTORS)], 1)


def finish(sums):
    wd, both, *parts = sums
    mine, width = parts[0].shape
    shape = jax.ShapeDtypeStruct
    vmem = pl.BlockSpec(memory_space=pltpu.VMEM)
    outs = pl.pallas_call(
        finish_kernel,
        name="finish",
        in_specs=[vmem] * (2 + GROUPS),
        out_specs=[vmem] * (5 + BIN),
        out_shape=[shape((mine, 3 * width), F32)]
        + [shape(wd.shape, F32), shape((mine, both.shape[1] - width), F32), shape((mine, width), F32)]
        + [shape((1, mine), F32)] * BIN
        + [shape((1, (VECTORS - BIN) * mine), F32)],
    )(*sums)
    return outs[0], outs[1:4], [v.reshape(-1) for v in outs[4:]]


def body(
    hidden_in, out_grad, segment_ids, pad_mask, task_weight, w_qkv, b_query, b_value, w_out, b_out,
    gain_one, shift_one, w_in, b_in, w_down, b_down, gain_two, shift_two,
):
    seqs, length, width = hidden_in.shape
    mine = w_qkv.shape[0]
    part = width // GROUPS
    near = lax.axis_size("task") == 4 and lax.axis_size("batch") == 8 and mine % 8 == 0
    vectors = [b_query, b_value, b_out, gain_one, shift_one, b_down, gain_two, shift_two, b_in]
    rows = hidden_in.reshape(-1, width)
    if near:
        weights = [*vectors, w_qkv, w_out, w_in, w_down]
        qkv, att, lse, vectors, bin_full, *full = attention_forward(True, rows, segment_ids, pad_mask, weights)
    else:
        packed = jnp.transpose(jnp.concatenate(vectors).reshape(VECTORS, mine))
        packed = jnp.pad(packed, ((0, 0), (0, 256 - VECTORS)))
        cut = w_qkv.reshape(mine, 3, GROUPS, part)
        groups = [cut[:, :, g].reshape(mine, width) for g in range(GROUPS)]
        full = [lax.all_gather(w, AXES, axis=0, tiled=True) for w in (packed, *groups, w_in, w_down, w_out)]
        qkv, att, lse, vectors, bin_full = attention_forward(False, rows, segment_ids, pad_mask, full[:4])
        full = full[1:]
    *w_groups, win_full, wd_full = full[:5]
    wo_full = win_full if near else full[5]
    hidden_out, grad_sum, datt, g_both, g_wd, g_rest = middle(
        task_weight, rows, att, out_grad.reshape(-1, width), wo_full, win_full, wd_full, vectors, bin_full, mine
    )
    given = [g.reshape(16, -1, g.shape[1]) for g in (g_wd, g_both)] if near else []
    grad_x, *terms = attention_backward(
        near, task_weight, rows, qkv, datt, lse, segment_ids, pad_mask, grad_sum, g_rest, w_groups, given
    )
    if near:
        s_qkv, (s_wd, s_win, s_wo), s_vec = finish(terms)
    else:
        s_wd, both, *parts = [
            lax.psum_scatter(t, AXES, scatter_dimension=0, tiled=True).astype(F32) for t in (g_wd, g_both, *terms)
        ]
        s_win, s_wo = both[:, :-width], both[:, -width:]
        s_qkv = join_groups(parts, width)
        small = parts[-1][:, width:]
        s_vec = [small[:, row] for row in range(BIN)] + [jnp.transpose(small[:, BIN:VECTORS]).reshape(-1)]
    return (
        hidden_out.reshape(hidden_in.shape),
        grad_x.reshape(hidden_in.shape),
        s_qkv,
        s_vec[BQ],
        s_vec[BV],
        s_wo,
        s_vec[BO],
        s_vec[G1],
        s_vec[S1],
        s_win,
        s_vec[BIN],
        s_wd,
        s_vec[BD],
        s_vec[G2],
        s_vec[S2],
    )


def solution(mesh):
    seq, mat, vec = P(AXES, None, None), P(AXES, None), P(AXES)
    weights = (mat, vec, vec, mat, vec, vec, vec, mat, vec, mat, vec, vec, vec)
    return jax.shard_map(
        body,
        mesh=mesh,
        in_specs=(seq, seq, mat, mat, P("task")) + weights,
        out_specs=(seq, seq) + weights,
        check_vma=False,
    )
```
